32 devices in a mesh: tm: 8 (over y, x, core), space: 4 (over z).
Axes of the slice: x: 2, y: 2, z: 4, core: 2. Of those that a mesh axis runs over, the one named last changes fastest.
Arguments:
- initial_state: float32 [192, 512], P('space'), may hold values from -6 to 6
- velocity: bfloat16 [192, 512], P('space'), may hold values from -0.5 to 0.5
- diffusion: bfloat16 [192, 512], P('space'), may hold values from 0.25 to 0.5
- forcing: bfloat16 [64, 192, 512], P('tm', 'space'), may hold values from -6 to 6
- implicit: float32 [512, 512], replicated, may hold values from 0 to 1
- coarse_implicit: float32 [512, 512], replicated, may hold values from 0 to 1
Outputs:
- solution: float32 [64, 192, 512], P('tm', 'space')
The draws below stay inside these ranges and needn't reach their ends.
All inputs are finite; a program needn't handle non-finite values.
Results may differ from the reference program's by a relative error of at most 0.0003.
Values may be sent and summed in bfloat16 or wider, within the bound.
No kernel may reach another device: no remote copies, remote signals or barrier semaphores. Data moves between devices by JAX's collectives and lax.ppermute only.
A program may use at most 64 MiB of HBM per device.

```python
import math
import jax
import jax.numpy as jnp
from jax import lax

NY = 512
BLK = 8
CYCLES = 2
NX = 192
NT = 64
N_TM = 8


def implicit_matrix(key, lowest, highest):
    strengths = jnp.exp(jax.random.uniform(key, (NY,), jnp.float32, math.log(lowest), math.log(highest)))
    places = jnp.arange(NY)
    offsets = jnp.abs(places[:, None] - places[None, :])
    distance = jnp.minimum(offsets, NY - offsets).astype(jnp.float32)
    kernel = jnp.where(offsets == 0, 0.0, -1.0 / jnp.maximum(distance, 1.0) ** 1.5)
    identity = jnp.eye(NY, dtype=jnp.float32)
    kernel = kernel - identity * jnp.sum(kernel, axis=1)[:, None]
    system = identity + kernel * strengths[None, :]
    return jnp.clip(jnp.linalg.inv(system), 0.0, 1.0)


def draw_implicit(key, part):
    return implicit_matrix(jax.random.fold_in(key, 11), 0.05, 0.8)


def draw_coarse_implicit(key, part):
    return implicit_matrix(jax.random.fold_in(key, 23), 0.4, 6.4)


def draw_forcing(key, part):
    noise_part = jnp.clip(jax.random.normal(jax.random.fold_in(key, 5), (NT, NX, NY), jnp.float32), -6.0, 6.0)
    return noise_part.astype(jnp.bfloat16)


def level_of(stream_key, shape, split, least, largest):
    def one(axis_at, shards_of):
        heights = jax.random.uniform(jax.random.fold_in(jax.random.fold_in(stream_key, 6), axis_at), (shards_of,), jnp.float32, least / len(split), largest / len(split))
        return jnp.repeat(jnp.exp(heights), shape[axis_at] // shards_of).reshape((-1,) + (1,) * (len(shape) - axis_at - 1))

    gain = one(*split[0])
    for cut in split[1:]:
        gain = gain * one(*cut)
    return gain


def scatter_about(key, shape, scale, bound, cuts=(), held_as=jnp.bfloat16):
    gain = level_of(key, shape, cuts, -0.22, 0.18) if cuts else 1.0
    values = jax.random.normal(key, shape, jnp.float32) * scale * gain
    return jnp.minimum(jnp.maximum(values, -bound), bound).astype(held_as)


def setup_inputs(seed: int = 0) -> dict:
    streams_of = jax.random.split(jax.random.key(seed), 7)
    initial_state = scatter_about(streams_of[0], (NX, NY), 1.0, 6.0, ((0, 4),), jnp.float32)
    velocity = jnp.clip(jax.random.uniform(streams_of[1], (NX, NY), jnp.float32, -0.5, 0.5) * level_of(streams_of[1], (NX, NY), ((0, 4),), -0.4, 0.0), -0.5, 0.5).astype(jnp.bfloat16)
    diffusion = jnp.clip(0.25 + 0.25 * jax.random.uniform(streams_of[2], (NX, NY), jnp.float32) ** level_of(streams_of[2], (NX, NY), ((0, 4),), -0.2, 0.2), 0.25, 0.5).astype(jnp.bfloat16)
    forcing = draw_forcing(jax.random.fold_in(streams_of[6], 71), 0)
    implicit = draw_implicit(jax.random.fold_in(streams_of[6], 71), 0)
    coarse_implicit = draw_coarse_implicit(jax.random.fold_in(streams_of[6], 71), 0)
    return {"initial_state": initial_state, "velocity": velocity, "diffusion": diffusion, "forcing": forcing, "implicit": implicit, "coarse_implicit": coarse_implicit}


HIGHEST = lax.Precision.HIGHEST

def stencil_weights(velocity, diffusion):
    moving = velocity.astype(jnp.float32)
    spread = diffusion.astype(jnp.float32)
    return (spread + 0.5 * moving, 1.0 - 2.0 * spread, spread - 0.5 * moving)

def advance(current, forcing_now, weights, implicit):
    west_weight, centre_weight, east_weight = weights
    summed = centre_weight * current + east_weight * jnp.roll(current, -1, -2) + west_weight * jnp.roll(current, 1, -2) + forcing_now.astype(jnp.float32)
    return jnp.matmul(summed, implicit, precision=HIGHEST)

def sweep_blocks(starts, blocks, step_count, weights, implicit):
    current = starts
    values = []
    for offset in range(step_count):
        current = advance(current, blocks[:, offset], weights, implicit)
        values.append(current)
    return values

def reference(initial_state, velocity, diffusion, forcing, implicit, coarse_implicit):
    weights = stencil_weights(velocity, diffusion)
    blocks = forcing.reshape(N_TM, BLK, NX, NY)
    end_values = jnp.zeros((N_TM, NX, NY), jnp.float32)

    def coarse_chain(carried, residual):
        updated = jnp.matmul(carried, coarse_implicit, precision=HIGHEST) + residual
        return (updated, updated)
    for repeat in range(CYCLES):
        starts = jnp.concatenate([initial_state[None], end_values[:-1]], axis=0)
        end_values = sweep_blocks(starts, blocks, BLK, weights, implicit)[-1]
        starts = jnp.concatenate([initial_state[None], end_values[:-1]], axis=0)
        residual = sweep_blocks(starts, blocks, BLK, weights, implicit)[-1] - end_values
        _, errors = lax.scan(coarse_chain, jnp.zeros((NX, NY), jnp.float32), residual)
        end_values = end_values + errors
    starts = jnp.concatenate([initial_state[None], end_values[:-1]], axis=0)
    values = sweep_blocks(starts, blocks, BLK - 1, weights, implicit)
    return jnp.stack(values + [end_values], axis=1).reshape(NT, NX, NY)
```

```python
import functools

import jax
import jax.numpy as jnp
from jax import lax
from jax.experimental import pallas as pl
from jax.experimental.pallas import tpu as pltpu
from jax.sharding import PartitionSpec as P

F32 = jnp.float32
BF16 = jnp.bfloat16


def ring(count, distance):
    return [(i, (i + distance) % count) for i in range(count)]


def split(value):
    high = value.astype(BF16)
    return high, (value - high.astype(F32)).astype(BF16)


def product(left, right):
    return jnp.dot(left, right, preferred_element_type=F32)


def product3(value, high_matrix, low_matrix):
    rows = value.shape[0]
    high, low = split(value)
    both = product(jnp.concatenate([high, low], axis=0), high_matrix)
    return both[:rows] + (both[rows:] + product(high, low_matrix))


def stencil(value, weights):
    west, centre, east = weights
    return centre * value + east * jnp.roll(value, -1, 0) + west * jnp.roll(value, 1, 0)


def make_weights(low, own, high, rows):
    wide = low.shape[1]

    def extended(at):
        return jnp.concatenate(
            [low[at, wide - rows :].astype(F32), own[at].astype(F32), high[at, :rows].astype(F32)], axis=0
        )

    moving, spread = extended(0), extended(1)
    return (spread + 0.5 * moving, 1.0 - 2.0 * spread, spread - 0.5 * moving)


def call(kernel, out_shape, *operands, smem=()):
    in_specs = [
        pl.BlockSpec(memory_space=pltpu.SMEM if i in smem else pltpu.VMEM) for i in range(len(operands))
    ]
    single = not isinstance(out_shape, (list, tuple))
    out_specs = jax.tree.map(lambda _: pl.BlockSpec(memory_space=pltpu.VMEM), out_shape)
    return pl.pallas_call(
        kernel,
        out_shape=out_shape,
        in_specs=in_specs,
        out_specs=out_specs if not single else pl.BlockSpec(memory_space=pltpu.VMEM),
        name=getattr(kernel, "__name__", None) or kernel.func.__name__,
    )(*operands)


def extended_forcing(low, own, high, at):
    return jnp.concatenate([low[at].astype(F32), own[at].astype(F32), high[at].astype(F32)], axis=0)


def pack(steps, wide, velocity, diffusion, forcing, start, head, tail):
    own = start.shape[0]
    f_rows = steps * steps
    for out, lead in ((head, 0), (tail, own)):
        near = slice(0, steps) if lead == 0 else slice(own - steps, own)
        far = slice(0, wide) if lead == 0 else slice(own - wide, own)
        for step in range(steps):
            out[step * steps : (step + 1) * steps] = forcing[step, near]
        out[f_rows : f_rows + wide] = velocity[far]
        out[f_rows + wide : f_rows + 2 * wide] = diffusion[far]
        parts = split(start[near])
        for i in range(2):
            at = f_rows + 2 * wide + i * steps
            out[at : at + steps] = parts[i]


def split_matrices(implicit, coarse_implicit, high_m, low_m, coarse):
    high_m[...], low_m[...] = split(implicit[...])
    coarse[...] = coarse_implicit[...].astype(BF16)


def first_sweep(steps, place, flow, fhigh, chigh, uhigh, clow_, ulow, forcing, coef, start, high_m, low_m, out):
    lead = fhigh.shape[1]
    own = start.shape[0]
    weights = make_weights(clow_, coef, chigh, lead)
    current = jnp.concatenate(
        [
            ulow[0].astype(F32) + ulow[1].astype(F32),
            start[...],
            uhigh[0].astype(F32) + uhigh[1].astype(F32),
        ],
        axis=0,
    )
    current = jnp.where(place[0] == 0, current, 0.0)
    for step in range(steps):
        summed = stencil(current, weights) + extended_forcing(flow, forcing, fhigh, step)
        current = product3(summed, high_m[...], low_m[...])
    out[...] = current[lead : lead + own]


def second_sweep(steps, keep, alow, ahigh, clow, chigh, a, coef, high_m, low_m, rho_high, rho_low, a_near):
    wide = alow.shape[0]
    own = a.shape[0]
    weights = make_weights(clow, coef, chigh, wide)
    current = jnp.concatenate([alow[...], a[...], ahigh[...]], axis=0)
    a_near[...] = current[wide - steps : wide + own + steps]
    for _ in range(steps):
        current = product3(stencil(current, weights), high_m[...], low_m[...])
    current = current[wide - keep : wide + own + keep]
    high = current.astype(BF16)
    rho_high[...] = high
    near = slice(keep - steps, keep + own + steps)
    rho_low[...] = (current[near] - high[near].astype(F32)).astype(BF16)


def coarse_and_third(steps, place, rho, clow, chigh, coef, high_m, low_m, coarse, le_out, psi_out, err_scratch):
    own = coef.shape[1]
    keep = (rho.shape[1] - own) // 2
    at = place[0]
    weights = make_weights(clow, coef, chigh, keep)
    first = jnp.where(at >= 2, rho[0].astype(F32), 0.0)

    def turn(source, carried):
        return product(carried.astype(BF16), coarse[...]) + rho[source].astype(F32)

    error = lax.fori_loop(1, at - 1, turn, first)
    err_scratch[...] = error
    current = error
    for _ in range(steps):
        current = product3(stencil(current, weights), high_m[...], low_m[...])
    mid = slice(keep - steps, keep + own + steps)
    le_out[...] = current[mid]
    current = current - product(err_scratch[...].astype(BF16), coarse[...])
    for _ in range(steps):
        current = product(stencil(current, weights).astype(BF16), high_m[...])
    psi_out[...] = current[mid].astype(BF16)


def last_sweep(
    steps, place, psi, b_before, b, flow, fhigh, clow, chigh, uhigh, ulow, forcing, coef, start, high_m, low_m, coarse, out
):
    own = coef.shape[1]
    lead = (b_before.shape[0] - own) // 2
    at = place[0]
    weights = make_weights(clow, coef, chigh, lead)

    def turn(source, carried):
        return product(carried.astype(BF16), coarse[...]) + psi[source].astype(F32)

    error = lax.fori_loop(2, at - 1, turn, jnp.zeros(b_before.shape, F32))
    initial = jnp.concatenate(
        [
            ulow[0].astype(F32) + ulow[1].astype(F32),
            start[...],
            uhigh[0].astype(F32) + uhigh[1].astype(F32),
        ],
        axis=0,
    )
    current = jnp.where(at == 0, initial, b_before[...] + error)
    mid = slice(lead, lead + own)
    before = psi[jnp.maximum(at - 1, 0)].astype(F32)
    last = jnp.where(at >= 1, product(error.astype(BF16), coarse[...]) + before, 0.0)
    out[steps - 1] = b[mid] + last[mid]
    for step in range(steps - 1):
        summed = stencil(current, weights) + extended_forcing(flow, forcing, fhigh, step)
        current = product3(summed, high_m[...], low_m[...])
        out[step] = current[mid]


def per_device(initial_state, velocity, diffusion, forcing, implicit, coarse_implicit):
    own, columns = initial_state.shape
    steps = forcing.shape[0]
    blocks = lax.axis_size("tm")
    slabs = lax.axis_size("space")
    at = lax.axis_index("tm")
    place = at.astype(jnp.int32).reshape(1)
    keep = 3 * steps
    wide = 4 * steps

    coef = jnp.stack([velocity, diffusion])
    f_rows, c_rows = steps * steps, 2 * wide

    def unpack(packed):
        return (
            packed[:f_rows].reshape(steps, steps, columns),
            packed[f_rows : f_rows + c_rows].reshape(2, wide, columns),
            packed[f_rows + c_rows :].reshape(2, steps, columns),
        )

    packed_shape = jax.ShapeDtypeStruct((f_rows + c_rows + 2 * steps, columns), BF16)
    head, tail = call(
        functools.partial(pack, steps, wide), [packed_shape, packed_shape], velocity, diffusion, forcing, initial_state
    )
    flow, clow, ulow = unpack(lax.ppermute(tail, "space", ring(slabs, 1)))
    fhigh, chigh, uhigh = unpack(lax.ppermute(head, "space", ring(slabs, -1)))
    matrix_shape = jax.ShapeDtypeStruct(implicit.shape, BF16)
    high_m, low_m, coarse = call(split_matrices, [matrix_shape] * 3, implicit, coarse_implicit)

    def field(rows, dtype=F32):
        return jax.ShapeDtypeStruct((rows, columns), dtype)

    a = call(
        functools.partial(first_sweep, steps),
        field(own),
        place, flow, fhigh, chigh, uhigh, clow, ulow, forcing, coef, initial_state, high_m, low_m,
        smem=(0,),
    )
    alow = lax.ppermute(a[own - wide :], "space", ring(slabs, 1))
    ahigh = lax.ppermute(a[:wide], "space", ring(slabs, -1))
    near = own + 2 * steps
    rho, rho_low, a_near = call(
        functools.partial(second_sweep, steps, keep),
        [field(own + 2 * keep, BF16), field(near, BF16), field(near)],
        alow, ahigh, clow, chigh, a, coef, high_m, low_m,
    )
    rho_all = lax.all_gather(rho, "tm", axis=0)
    low_before = lax.ppermute(rho_low, "tm", ring(blocks, 1))
    le, psi = third(steps, own, keep, columns, place, rho_all, clow, chigh, coef, high_m, low_m, coarse)
    rho_before = rho_all[jnp.maximum(at - 1, 0)][keep - steps : keep + own + steps].astype(F32) + low_before.astype(F32)
    b = a_near + jnp.where(at == 0, 0.0, rho_before) + le
    b_before = lax.ppermute(b, "tm", ring(blocks, 1))
    psi_all = lax.all_gather(psi, "tm", axis=0)
    return call(
        functools.partial(last_sweep, steps),
        jax.ShapeDtypeStruct((steps, own, columns), F32),
        place, psi_all, b_before, b, flow, fhigh, clow, chigh, uhigh, ulow, forcing, coef, initial_state,
        high_m, low_m, coarse,
        smem=(0,),
    )


def third(steps, own, keep, columns, place, *operands):
    near = own + 2 * steps
    vmem = pl.BlockSpec(memory_space=pltpu.VMEM)
    return pl.pallas_call(
        functools.partial(coarse_and_third, steps),
        out_shape=[jax.ShapeDtypeStruct((near, columns), F32), jax.ShapeDtypeStruct((near, columns), BF16)],
        in_specs=[pl.BlockSpec(memory_space=pltpu.SMEM)] + [vmem] * len(operands),
        out_specs=[vmem, vmem],
        scratch_shapes=[pltpu.VMEM((own + 2 * keep, columns), F32)],
        name="coarse_and_third",
    )(place, *operands)


def solution(mesh):
    in_specs = (
        P("space", None),
        P("space", None),
        P("space", None),
        P("tm", "space", None),
        P(),
        P(),
    )
    out_specs = P("tm", "space", None)
    return jax.shard_map(per_device, mesh=mesh, in_specs=in_specs, out_specs=out_specs, check_vma=False)
```

```python
import functools

import jax
import jax.numpy as jnp
from jax import lax
from jax.experimental import pallas as pl
from jax.experimental.pallas import tpu as pltpu
from jax.sharding import PartitionSpec as P

F32 = jnp.float32
BF16 = jnp.bfloat16


def ring(count, distance):
    return [(i, (i + distance) % count) for i in range(count)]


def split(value):
    high = value.astype(BF16)
    return high, (value - high.astype(F32)).astype(BF16)


def product(left, right):
    return jnp.dot(left, right, preferred_element_type=F32)


def product3(value, high_matrix, low_matrix):
    rows = value.shape[0]
    high, low = split(value)
    both = product(jnp.concatenate([high, low], axis=0), high_matrix)
    return both[:rows] + (both[rows:] + product(high, low_matrix))


def stencil(value, weights):
    west, centre, east = weights
    return centre * value + east * jnp.roll(value, -1, 0) + west * jnp.roll(value, 1, 0)


class Layout:
    def __init__(self, steps, own):
        self.steps = steps
        self.own = own
        self.wide = 5 * steps
        self.keep = 3 * steps
        self.fine = 2 * steps
        self.velocity = steps * self.wide
        self.diffusion = self.velocity + self.wide
        self.start = self.diffusion + self.wide
        self.start_low = self.start + self.wide
        self.rows = self.start_low + self.fine

    def centred(self, width, inside):
        return slice(width - inside, width + self.own + inside)


def pack(lay, velocity, diffusion, forcing, start, head, tail):
    for out, first in ((head, 0), (tail, lay.own - lay.wide)):
        near = slice(first, first + lay.wide)
        for step in range(lay.steps):
            out[step * lay.wide : (step + 1) * lay.wide] = forcing[step, near]
        out[lay.velocity : lay.diffusion] = velocity[near]
        out[lay.diffusion : lay.start] = diffusion[near]
        high, low = split(start[near])
        out[lay.start : lay.start_low] = high
        out[lay.start_low : lay.rows] = low[: lay.fine] if first == 0 else low[lay.wide - lay.fine :]


def split_matrices(implicit, coarse_implicit, high_m, low_m, coarse):
    high_m[...], low_m[...] = split(implicit[...])
    coarse[...] = coarse_implicit[...].astype(BF16)


def from_packs(lay, low, own, high, at, width):
    return jnp.concatenate(
        [
            low[at + lay.wide - width : at + lay.wide].astype(F32),
            own.astype(F32),
            high[at : at + width].astype(F32),
        ],
        axis=0,
    )


def start_from_packs(lay, low, own, high, width):
    value = from_packs(lay, low, own, high, lay.start, width)
    fine = min(width, lay.fine)
    low_tail = low[lay.start_low + lay.fine - fine : lay.rows].astype(F32)
    high_tail = high[lay.start_low : lay.start_low + fine].astype(F32)
    pieces = [
        value[: width - fine] if width > fine else None,
        value[width - fine : width] + low_tail,
        value[width : width + lay.own],
        value[width + lay.own : width + lay.own + fine] + high_tail,
        value[width + lay.own + fine :] if width > fine else None,
    ]
    return jnp.concatenate([piece for piece in pieces if piece is not None], axis=0)


def two_sweeps(lay, place, low, high, forcing, velocity, diffusion, start, high_m, low_m, rho, rho_low, a_near, weights):
    wide, steps = lay.wide, lay.steps
    moving = from_packs(lay, low, velocity[...], high, lay.velocity, wide)
    spread = from_packs(lay, low, diffusion[...], high, lay.diffusion, wide)
    weights[0] = spread + 0.5 * moving
    weights[1] = 1.0 - 2.0 * spread
    weights[2] = spread - 0.5 * moving
    current = start_from_packs(lay, low, start[...], high, wide)
    current = jnp.where(place[0] == 0, current, 0.0)
    for step in range(steps):
        summed = stencil(current, weights[...]) + from_packs(lay, low, forcing[step], high, step * wide, wide)
        current = product3(summed, high_m[...], low_m[...])
    a_near[...] = current[lay.centred(wide, steps)]
    width = wide - steps
    current = current[lay.centred(wide, width)]
    narrow = weights[:, lay.centred(wide, width)]
    for _ in range(steps):
        current = product3(stencil(current, narrow), high_m[...], low_m[...])
    high_part, low_part = split(current)
    rho[...] = high_part[lay.centred(width, lay.keep)]
    rho_low[...] = low_part[lay.centred(width, 0)]


def coarse_and_third(lay, place, rho, rho_low, a_near, weights, high_m, low_m, coarse, psi, passed, b_own, error_kept):
    keep, steps, own = lay.keep, lay.steps, lay.own
    at = place[0]
    narrow = weights[:, lay.centred(lay.wide, keep)]
    first = jnp.where(at >= 2, rho[0].astype(F32), 0.0)

    def turn(source, carried):
        return product(carried.astype(BF16), coarse[...]) + rho[source].astype(F32)

    current = lax.fori_loop(1, at - 1, turn, first)
    error_kept[...] = current
    for _ in range(steps):
        current = product3(stencil(current, narrow), high_m[...], low_m[...])
    near = lay.centred(keep, steps)
    before = rho[jnp.maximum(at - 1, 0)].astype(F32)[near]
    b = a_near[...] + jnp.where(at == 0, 0.0, before) + current[near]
    b_own[...] = b[lay.centred(steps, 0)]
    rows = own + 2 * steps
    passed[:rows], passed[rows : 2 * rows] = split(b)
    passed[2 * rows :] = rho_low[...]
    current = current - product(error_kept[...].astype(BF16), coarse[...])
    for _ in range(steps):
        current = product(stencil(current, narrow).astype(BF16), high_m[...])
    psi[...] = current[near].astype(BF16)


def last_sweep(lay, place, psi, passed, b_own, low, high, forcing, weights, start, high_m, low_m, coarse, out):
    steps, own = lay.steps, lay.own
    at = place[0]
    rows = own + 2 * steps
    narrow = weights[:, lay.centred(lay.wide, steps)]

    def turn(source, carried):
        return product(carried.astype(BF16), coarse[...]) + psi[source].astype(F32)

    error = lax.fori_loop(2, at - 1, turn, jnp.zeros((rows, start.shape[1]), F32))
    b_before = passed[:rows].astype(F32) + passed[rows : 2 * rows].astype(F32)
    initial = start_from_packs(lay, low, start[...], high, steps)
    current = jnp.where(at == 0, initial, b_before + error)
    mid = lay.centred(steps, 0)
    last = product(error[mid].astype(BF16), coarse[...]) + psi[jnp.maximum(at - 1, 0)].astype(F32)[mid]
    last = last + passed[2 * rows :].astype(F32)
    out[steps - 1] = b_own[...] + jnp.where(at == 0, 0.0, last)
    for step in range(steps - 1):
        summed = stencil(current, narrow) + from_packs(lay, low, forcing[step], high, step * lay.wide, steps)
        current = product3(summed, high_m[...], low_m[...])
        out[step] = current[mid]


def in_vmem(value):
    return pltpu.with_memory_space_constraint(value, pltpu.VMEM)


def call(kernel, lay, outs, *operands, scratch=()):
    spaces = [pltpu.SMEM if o.dtype == jnp.int32 else pltpu.VMEM for o in operands]
    return pl.pallas_call(
        kernel if lay is None else functools.partial(kernel, lay),
        out_shape=outs,
        in_specs=[pl.BlockSpec(memory_space=space) for space in spaces],
        out_specs=jax.tree.map(lambda _: pl.BlockSpec(memory_space=pltpu.VMEM), outs),
        scratch_shapes=scratch,
        compiler_params=pltpu.CompilerParams(vmem_limit_bytes=16 << 20),
        name=kernel.__name__,
    )(*operands)


def per_device(initial_state, velocity, diffusion, forcing, implicit, coarse_implicit):
    own, columns = initial_state.shape
    steps = forcing.shape[0]
    blocks = lax.axis_size("tm")
    slabs = lax.axis_size("space")
    place = lax.axis_index("tm").astype(jnp.int32).reshape(1)
    lay = Layout(steps, own)
    near = own + 2 * steps

    def kept(*shape, dtype=F32):
        return pltpu.VMEM(shape, dtype)

    head, tail = call(pack, lay, [kept(lay.rows, columns, dtype=BF16)] * 2, velocity, diffusion, forcing, initial_state)
    low = in_vmem(lax.ppermute(tail, "space", ring(slabs, 1)))
    high = in_vmem(lax.ppermute(head, "space", ring(slabs, -1)))
    high_m, low_m, coarse = call(
        split_matrices, None, [kept(*implicit.shape, dtype=BF16)] * 3, implicit, coarse_implicit
    )
    high_m, low_m, coarse = in_vmem(high_m), in_vmem(low_m), in_vmem(coarse)
    rho, rho_low, a_near, weights = call(
        two_sweeps,
        lay,
        [
            kept(own + 2 * lay.keep, columns, dtype=BF16),
            kept(own, columns, dtype=BF16),
            kept(near, columns),
            kept(3, own + 2 * lay.wide, columns),
        ],
        place, low, high, forcing, velocity, diffusion, initial_state, high_m, low_m,
    )
    weights = in_vmem(weights)
    rho_all = lax.all_gather(rho, "tm", axis=0)
    psi, passed, b_own = call(
        coarse_and_third,
        lay,
        [
            kept(near, columns, dtype=BF16),
            kept(2 * near + own, columns, dtype=BF16),
            kept(own, columns),
        ],
        place, rho_all, in_vmem(rho_low), in_vmem(a_near), weights, high_m, low_m, coarse,
        scratch=[pltpu.VMEM((own + 2 * lay.keep, columns), F32)],
    )
    passed = lax.ppermute(passed, "tm", ring(blocks, 1))
    psi_all = lax.all_gather(psi, "tm", axis=0)
    return call(
        last_sweep,
        lay,
        jax.ShapeDtypeStruct((steps, own, columns), F32),
        place, psi_all, in_vmem(passed), in_vmem(b_own), low, high, forcing, weights, initial_state, high_m, low_m, coarse,
    )


def solution(mesh):
    in_specs = (
        P("space", None),
        P("space", None),
        P("space", None),
        P("tm", "space", None),
        P(),
        P(),
    )
    out_specs = P("tm", "space", None)
    return jax.shard_map(per_device, mesh=mesh, in_specs=in_specs, out_specs=out_specs, check_vma=False)
```

```python
import functools

import jax
import jax.numpy as jnp
from jax import lax
from jax.experimental import pallas as pl
from jax.experimental.pallas import tpu as pltpu
from jax.sharding import PartitionSpec as P

F32 = jnp.float32
BF16 = jnp.bfloat16
LIMIT = 16 << 20


def ring(count, distance):
    return [(i, (i + distance) % count) for i in range(count)]


def split(value):
    high = value.astype(BF16)
    return high, (value - high.astype(F32)).astype(BF16)


def product(left, right):
    return jnp.dot(left, right, preferred_element_type=F32)


def product3(value, high_matrix, low_matrix):
    rows = value.shape[0]
    high, low = split(value)
    both = product(jnp.concatenate([high, low], axis=0), high_matrix)
    return both[:rows] + (both[rows:] + product(high, low_matrix))


def stencil(value, weights):
    west, centre, east = weights
    return centre * value + east * jnp.roll(value, -1, 0) + west * jnp.roll(value, 1, 0)


class Layout:
    def __init__(self, steps, own):
        self.steps = steps
        self.own = own
        self.wide = 4 * steps
        self.keep = 3 * steps
        self.fine = 2 * steps
        self.velocity = steps * steps
        self.diffusion = self.velocity + steps
        self.start = self.diffusion + steps
        self.start_low = self.start + steps
        self.first_rows = self.start_low + steps
        self.tail = self.wide
        self.far_velocity = self.tail + self.fine
        self.far_diffusion = self.far_velocity + self.wide
        self.second_rows = self.far_diffusion + self.wide

    def centred(self, width, inside):
        return slice(width - inside, width + self.own + inside)


def pack(lay, velocity, diffusion, forcing, start, head, tail, start_kept, semaphores):
    steps, own = lay.steps, lay.own
    copies = [(start, start_kept)]
    for out, first in ((head, 0), (tail, own - steps)):
        near = pl.ds(first, steps)
        for step in range(steps):
            copies.append((forcing.at[step, near], out.at[pl.ds(step * steps, steps)]))
        copies.append((velocity.at[near], out.at[pl.ds(lay.velocity, steps)]))
        copies.append((diffusion.at[near], out.at[pl.ds(lay.diffusion, steps)]))
    copies = [pltpu.make_async_copy(*pair, semaphores.at[i]) for i, pair in enumerate(copies)]
    for copy in copies:
        copy.start()
    for copy in copies:
        copy.wait()
    for out, first in ((head, 0), (tail, own - steps)):
        high, low = split(start_kept[first : first + steps])
        out[lay.start : lay.start_low] = high
        out[lay.start_low : lay.first_rows] = low


def split_matrices(implicit, coarse_implicit, high_m, low_m, coarse):
    high_m[...], low_m[...] = split(implicit[...])
    coarse[...] = coarse_implicit[...].astype(BF16)


def joined(low, own, high):
    return jnp.concatenate([low.astype(F32), own.astype(F32), high.astype(F32)], axis=0)


def from_first(lay, low, own, high, at):
    rows = slice(at, at + lay.steps)
    return joined(low[rows], own, high[rows])


def start_from_first(lay, low, own, high):
    value = from_first(lay, low, own, high, lay.start)
    return value + from_first(lay, low, jnp.zeros(own.shape, F32), high, lay.start_low)


def make_weights(moving, spread):
    return spread + 0.5 * moving, 1.0 - 2.0 * spread, spread - 0.5 * moving


def first_sweep(lay, place, low, high, forcing, velocity, diffusion, start, high_m, low_m, a, head, tail):
    steps, own = lay.steps, lay.own
    weights = make_weights(
        from_first(lay, low, velocity[...], high, lay.velocity),
        from_first(lay, low, diffusion[...], high, lay.diffusion),
    )
    current = jnp.where(place[0] == 0, start_from_first(lay, low, start[...], high), 0.0)
    for step in range(steps):
        summed = stencil(current, weights) + from_first(lay, low, forcing[step], high, step * steps)
        current = product3(summed, high_m[...], low_m[...])
    current = current[lay.centred(steps, 0)]
    a[...] = current
    high_part, low_part = split(current)
    for out, far, near in (
        (head, slice(0, lay.wide), slice(0, lay.fine)),
        (tail, slice(own - lay.wide, own), slice(own - lay.fine, own)),
    ):
        out[: lay.tail] = high_part[far]
        out[lay.tail : lay.far_velocity] = low_part[near]
        out[lay.far_velocity : lay.far_diffusion] = velocity[far]
        out[lay.far_diffusion :] = diffusion[far]


def second_sweep(lay, low, high, a, velocity, diffusion, high_m, low_m, rho, rho_low, a_near, weights):
    wide, steps, fine = lay.wide, lay.steps, lay.fine

    def extended(own, at):
        return joined(low[at : at + wide], own, high[at : at + wide])

    weights[0], weights[1], weights[2] = make_weights(
        extended(velocity[...], lay.far_velocity), extended(diffusion[...], lay.far_diffusion)
    )
    tails = slice(lay.tail, lay.far_velocity)
    current = joined(
        jnp.concatenate([low[: wide - fine].astype(F32), low[wide - fine : wide].astype(F32) + low[tails].astype(F32)], axis=0),
        a[...],
        jnp.concatenate([high[:fine].astype(F32) + high[tails].astype(F32), high[fine:wide].astype(F32)], axis=0),
    )
    a_near[...] = current[lay.centred(wide, steps)]
    for _ in range(steps):
        current = product3(stencil(current, weights[...]), high_m[...], low_m[...])
    high_part, low_part = split(current)
    rho[...] = high_part[lay.centred(wide, lay.keep)]
    rho_low[...] = low_part[lay.centred(wide, 0)]


def coarse_and_third(lay, place, rho, rho_low, a_near, weights, high_m, low_m, coarse, psi, passed, b_own, error_kept):
    keep, steps, own = lay.keep, lay.steps, lay.own
    at = place[0]
    narrow = weights[:, lay.centred(lay.wide, keep)]
    first = jnp.where(at >= 2, rho[0].astype(F32), 0.0)

    def turn(source, carried):
        return product(carried.astype(BF16), coarse[...]) + rho[source].astype(F32)

    current = lax.fori_loop(1, at - 1, turn, first)
    error_kept[...] = current
    for _ in range(steps):
        current = product3(stencil(current, narrow), high_m[...], low_m[...])
    near = lay.centred(keep, steps)
    before = rho[jnp.maximum(at - 1, 0)].astype(F32)[near]
    b = a_near[...] + jnp.where(at == 0, 0.0, before) + current[near]
    b_own[...] = b[lay.centred(steps, 0)]
    rows = own + 2 * steps
    passed[:rows], passed[rows : 2 * rows] = split(b)
    passed[2 * rows :] = rho_low[...]
    current = current - product(error_kept[...].astype(BF16), coarse[...])
    for _ in range(steps):
        current = product(stencil(current, narrow).astype(BF16), high_m[...])
    psi[...] = current[near].astype(BF16)


def last_sweep(lay, place, psi, passed, b_own, low, high, forcing, weights, start, high_m, low_m, coarse, out):
    steps, own = lay.steps, lay.own
    at = place[0]
    rows = own + 2 * steps
    narrow = weights[:, lay.centred(lay.wide, steps)]

    def turn(source, carried):
        return product(carried.astype(BF16), coarse[...]) + psi[source].astype(F32)

    error = lax.fori_loop(2, at - 1, turn, jnp.zeros((rows, start.shape[1]), F32))
    b_before = passed[:rows].astype(F32) + passed[rows : 2 * rows].astype(F32)
    initial = start_from_first(lay, low, start[...], high)
    current = jnp.where(at == 0, initial, b_before + error)
    mid = lay.centred(steps, 0)
    last = product(error[mid].astype(BF16), coarse[...]) + psi[jnp.maximum(at - 1, 0)].astype(F32)[mid]
    last = last + passed[2 * rows :].astype(F32)
    out[steps - 1] = b_own[...] + jnp.where(at == 0, 0.0, last)
    for step in range(steps - 1):
        summed = stencil(current, narrow) + from_first(lay, low, forcing[step], high, step * steps)
        current = product3(summed, high_m[...], low_m[...])
        out[step] = current[mid]


def in_vmem(value):
    return pltpu.with_memory_space_constraint(value, pltpu.VMEM)


def call(kernel, lay, outs, *operands, scratch=()):
    spaces = [pltpu.SMEM if o.dtype == jnp.int32 else pltpu.VMEM for o in operands]
    return pl.pallas_call(
        kernel if lay is None else functools.partial(kernel, lay),
        out_shape=outs,
        in_specs=[pl.BlockSpec(memory_space=space) for space in spaces],
        out_specs=jax.tree.map(lambda _: pl.BlockSpec(memory_space=pltpu.VMEM), outs),
        scratch_shapes=scratch,
        compiler_params=pltpu.CompilerParams(vmem_limit_bytes=LIMIT),
        name=kernel.__name__,
    )(*operands)


def per_device(initial_state, velocity, diffusion, forcing, implicit, coarse_implicit):
    own, columns = initial_state.shape
    steps = forcing.shape[0]
    blocks = lax.axis_size("tm")
    slabs = lax.axis_size("space")
    place = lax.axis_index("tm").astype(jnp.int32).reshape(1)
    lay = Layout(steps, own)
    near = own + 2 * steps

    def kept(*shape, dtype=F32):
        return pltpu.VMEM(shape, dtype)

    first_pack = kept(lay.first_rows, columns, dtype=BF16)
    hbm = pl.BlockSpec(memory_space=pltpu.HBM)
    head, tail = pl.pallas_call(
        functools.partial(pack, lay),
        out_shape=[first_pack] * 2,
        in_specs=[hbm] * 4,
        out_specs=[pl.BlockSpec(memory_space=pltpu.VMEM)] * 2,
        scratch_shapes=[pltpu.VMEM((own, columns), F32), pltpu.SemaphoreType.DMA((1 + 2 * (steps + 2),))],
        compiler_params=pltpu.CompilerParams(vmem_limit_bytes=LIMIT),
        name="pack",
    )(*(pltpu.with_memory_space_constraint(x, pltpu.HBM) for x in (velocity, diffusion, forcing, initial_state)))
    low = in_vmem(lax.ppermute(tail, "space", ring(slabs, 1)))
    high = in_vmem(lax.ppermute(head, "space", ring(slabs, -1)))
    high_m, low_m, coarse = call(
        split_matrices, None, [kept(*implicit.shape, dtype=BF16)] * 3, implicit, coarse_implicit
    )
    high_m, low_m, coarse = in_vmem(high_m), in_vmem(low_m), in_vmem(coarse)
    second_pack = kept(lay.second_rows, columns, dtype=BF16)
    a, head, tail = call(
        first_sweep,
        lay,
        [kept(own, columns), second_pack, second_pack],
        place, low, high, forcing, velocity, diffusion, initial_state, high_m, low_m,
    )
    far_low = in_vmem(lax.ppermute(tail, "space", ring(slabs, 1)))
    far_high = in_vmem(lax.ppermute(head, "space", ring(slabs, -1)))
    rho, rho_low, a_near, weights = call(
        second_sweep,
        lay,
        [
            kept(own + 2 * lay.keep, columns, dtype=BF16),
            kept(own, columns, dtype=BF16),
            kept(near, columns),
            kept(3, own + 2 * lay.wide, columns),
        ],
        far_low, far_high, in_vmem(a), velocity, diffusion, high_m, low_m,
    )
    weights = in_vmem(weights)
    rho_all = lax.all_gather(rho, "tm", axis=0)
    psi, passed, b_own = call(
        coarse_and_third,
        lay,
        [
            kept(near, columns, dtype=BF16),
            kept(2 * near + own, columns, dtype=BF16),
            kept(own, columns),
        ],
        place, rho_all, in_vmem(rho_low), in_vmem(a_near), weights, high_m, low_m, coarse,
        scratch=[pltpu.VMEM((own + 2 * lay.keep, columns), F32)],
    )
    passed = lax.ppermute(passed, "tm", ring(blocks, 1))
    psi_all = lax.all_gather(psi, "tm", axis=0)
    return call(
        last_sweep,
        lay,
        jax.ShapeDtypeStruct((steps, own, columns), F32),
        place, psi_all, in_vmem(passed), in_vmem(b_own), low, high, forcing, weights, initial_state, high_m, low_m, coarse,
    )


def solution(mesh):
    in_specs = (
        P("space", None),
        P("space", None),
        P("space", None),
        P("tm", "space", None),
        P(),
        P(),
    )
    out_specs = P("tm", "space", None)
    return jax.shard_map(per_device, mesh=mesh, in_specs=in_specs, out_specs=out_specs, check_vma=False)
```

```python
import functools

import jax
import jax.numpy as jnp
from jax import lax
from jax.experimental import pallas as pl
from jax.experimental.pallas import tpu as pltpu
from jax.sharding import PartitionSpec as P

F32 = jnp.float32
BF16 = jnp.bfloat16
LIMIT = 16 << 20


def ring(count, distance):
    return [(i, (i + distance) % count) for i in range(count)]


def split(value):
    high = value.astype(BF16)
    return high, (value - high.astype(F32)).astype(BF16)


def product(left, right):
    return jnp.dot(left, right, preferred_element_type=F32)


def product3(value, high_matrix, low_matrix):
    rows = value.shape[0]
    high, low = split(value)
    both = product(jnp.concatenate([high, low], axis=0), high_matrix)
    return both[:rows] + (both[rows:] + product(high, low_matrix))


def stencil(value, weights):
    west, centre, east = weights
    return centre * value + east * jnp.roll(value, -1, 0) + west * jnp.roll(value, 1, 0)


class Layout:
    def __init__(self, steps, own):
        self.steps = steps
        self.own = own
        self.wide = 4 * steps
        self.keep = 3 * steps
        self.fine = 2 * steps
        self.velocity = steps * steps
        self.diffusion = self.velocity + steps
        self.start = self.diffusion + steps
        self.start_low = self.start + steps
        self.first_rows = self.start_low + steps
        self.tail = self.wide
        self.far_velocity = self.tail + self.fine
        self.far_diffusion = self.far_velocity + self.wide
        self.second_rows = self.far_diffusion + self.wide

    def centred(self, width, inside):
        return slice(width - inside, width + self.own + inside)


def pack(lay, velocity, diffusion, forcing, start, head, tail, start_kept, semaphores):
    steps, own = lay.steps, lay.own
    copies = [(start, start_kept)]
    for out, first in ((head, 0), (tail, own - steps)):
        near = pl.ds(first, steps)
        for step in range(steps):
            copies.append((forcing.at[step, near], out.at[pl.ds(step * steps, steps)]))
        copies.append((velocity.at[near], out.at[pl.ds(lay.velocity, steps)]))
        copies.append((diffusion.at[near], out.at[pl.ds(lay.diffusion, steps)]))
    copies = [pltpu.make_async_copy(*pair, semaphores.at[i]) for i, pair in enumerate(copies)]
    for copy in copies:
        copy.start()
    for copy in copies:
        copy.wait()
    for out, first in ((head, 0), (tail, own - steps)):
        high, low = split(start_kept[first : first + steps])
        out[lay.start : lay.start_low] = high
        out[lay.start_low : lay.first_rows] = low


def split_matrices(implicit, coarse_implicit, high_m, low_m, coarse):
    high_m[...], low_m[...] = split(implicit[...])
    coarse[...] = coarse_implicit[...].astype(BF16)


def joined(low, own, high):
    return jnp.concatenate([low.astype(F32), own.astype(F32), high.astype(F32)], axis=0)


def from_first(lay, low, own, high, at):
    rows = slice(at, at + lay.steps)
    return joined(low[rows], own, high[rows])


def start_from_first(lay, low, own, high):
    value = from_first(lay, low, own, high, lay.start)
    return value + from_first(lay, low, jnp.zeros(own.shape, F32), high, lay.start_low)


def make_weights(moving, spread):
    return spread + 0.5 * moving, 1.0 - 2.0 * spread, spread - 0.5 * moving


def first_sweep(lay, place, low, high, forcing, velocity, diffusion, start, high_m, low_m, a, head, tail):
    steps, own = lay.steps, lay.own
    weights = make_weights(
        from_first(lay, low, velocity[...], high, lay.velocity),
        from_first(lay, low, diffusion[...], high, lay.diffusion),
    )
    current = jnp.where(place[0] == 0, start_from_first(lay, low, start[...], high), 0.0)
    for step in range(steps):
        summed = stencil(current, weights) + from_first(lay, low, forcing[step], high, step * steps)
        current = product3(summed, high_m[...], low_m[...])
    current = current[lay.centred(steps, 0)]
    a[...] = current
    high_part, low_part = split(current)
    for out, far, near in (
        (head, slice(0, lay.wide), slice(0, lay.fine)),
        (tail, slice(own - lay.wide, own), slice(own - lay.fine, own)),
    ):
        out[: lay.tail] = high_part[far]
        out[lay.tail : lay.far_velocity] = low_part[near]
        out[lay.far_velocity : lay.far_diffusion] = velocity[far]
        out[lay.far_diffusion :] = diffusion[far]


def second_sweep(lay, low, high, a, velocity, diffusion, high_m, low_m, rho, rho_low, a_near, weights):
    wide, steps, fine = lay.wide, lay.steps, lay.fine

    def extended(own, at):
        return joined(low[at : at + wide], own, high[at : at + wide])

    weights[0], weights[1], weights[2] = make_weights(
        extended(velocity[...], lay.far_velocity), extended(diffusion[...], lay.far_diffusion)
    )
    tails = slice(lay.tail, lay.far_velocity)
    current = joined(
        jnp.concatenate([low[: wide - fine].astype(F32), low[wide - fine : wide].astype(F32) + low[tails].astype(F32)], axis=0),
        a[...],
        jnp.concatenate([high[:fine].astype(F32) + high[tails].astype(F32), high[fine:wide].astype(F32)], axis=0),
    )
    a_near[...] = current[lay.centred(wide, steps)]
    for _ in range(steps):
        current = product3(stencil(current, weights[...]), high_m[...], low_m[...])
    high_part, low_part = split(current)
    rho[...] = high_part[lay.centred(wide, lay.keep)]
    rho_low[...] = low_part[lay.centred(wide, 0)]


def coarse_and_third(lay, place, rho, rho_low, a_near, weights, high_m, low_m, coarse, change, passed, b_own):
    keep, steps, own = lay.keep, lay.steps, lay.own
    rows = own + 2 * keep
    count = change.shape[0]
    at = place[0]
    narrow = weights[:, lay.centred(lay.wide, keep)]
    near = lay.centred(keep, steps)
    shared = count > 1

    def turn(source, carried):
        return product(carried.astype(BF16), coarse[...]) + rho[source].astype(F32)

    if shared:
        odd = at % 2 == 1
        error = rho[0].astype(F32)
        errors = []
        for item in range(count):
            following = turn(2 * item + 1, error)
            errors.append(jnp.where(odd, following, error))
            if item < count - 1:
                error = turn(2 * item + 2, following)
    else:
        first = jnp.where(at >= 2, rho[0].astype(F32), 0.0)
        errors = [lax.fori_loop(1, at - 1, turn, first)]
    kept = jnp.concatenate([error.astype(BF16) for error in errors], axis=0)
    current = jnp.concatenate(errors, axis=0)
    for _ in range(steps):
        moved = [stencil(current[i * rows : (i + 1) * rows], narrow) for i in range(count)]
        current = product3(jnp.concatenate(moved, axis=0), high_m[...], low_m[...])
    coarse_part = product(kept, coarse[...])
    mine = jnp.zeros((own + 2 * steps, current.shape[1]), F32)
    inner = lay.centred(keep, lay.fine)
    for i in range(count):
        swept = current[i * rows : (i + 1) * rows]
        here = (at - 2) // 2 == i if shared else True
        mine = mine + jnp.where(jnp.logical_and(here, at >= 2), swept[near], 0.0)
        change[i] = swept[inner] - coarse_part[i * rows : (i + 1) * rows][inner]
    before = rho[jnp.maximum(at - 1, 0)].astype(F32)[near]
    b = a_near[...] + jnp.where(at == 0, 0.0, before) + mine
    b_own[...] = b[lay.centred(steps, 0)]
    rows = own + 2 * steps
    passed[:rows], passed[rows : 2 * rows] = split(b)
    passed[2 * rows :] = rho_low[...]


def fourth_sweep(lay, change, weights, high_m, psi):
    steps = lay.steps
    count, rows, _ = change.shape
    narrow = weights[:, lay.centred(lay.wide, lay.fine)]
    current = jnp.concatenate([change[i] for i in range(count)], axis=0)
    for _ in range(steps):
        moved = [stencil(current[i * rows : (i + 1) * rows], narrow).astype(BF16) for i in range(count)]
        current = product(jnp.concatenate(moved, axis=0), high_m[...])
    for i in range(count):
        psi[i] = current[i * rows : (i + 1) * rows][lay.centred(lay.fine, steps)].astype(BF16)


def last_sweep(lay, place, psi, psi_other, passed, b_own, low, high, forcing, weights, start, high_m, low_m, coarse, out):
    steps, own = lay.steps, lay.own
    at = place[0]
    rows = own + 2 * steps
    narrow = weights[:, lay.centred(lay.wide, steps)]
    shared = psi_other is not None

    def source(block):
        if not shared:
            return psi[block].astype(F32)
        item = block // 2 - 1
        return jnp.where((block - at) % 2 == 0, psi[item].astype(F32), psi_other[item].astype(F32))

    def turn(block, carried):
        return product(carried.astype(BF16), coarse[...]) + source(block)

    error = lax.fori_loop(2, at - 1, turn, jnp.zeros((rows, start.shape[1]), F32))
    b_before = passed[:rows].astype(F32) + passed[rows : 2 * rows].astype(F32)
    initial = start_from_first(lay, low, start[...], high)
    current = jnp.where(at == 0, initial, b_before + error)
    mid = lay.centred(steps, 0)
    last = product(error[mid].astype(BF16), coarse[...])
    last = last + jnp.where(at >= 3, source(jnp.maximum(at - 1, 2))[mid], 0.0)
    last = last + passed[2 * rows :].astype(F32)
    out[steps - 1] = b_own[...] + jnp.where(at == 0, 0.0, last)
    for step in range(steps - 1):
        summed = stencil(current, narrow) + from_first(lay, low, forcing[step], high, step * steps)
        current = product3(summed, high_m[...], low_m[...])
        out[step] = current[mid]


def last_sweep_gathered(lay, place, psi, *rest):
    last_sweep(lay, place, psi, None, *rest)


def in_vmem(value):
    return pltpu.with_memory_space_constraint(value, pltpu.VMEM)


def call(kernel, lay, outs, *operands, cost=None):
    spaces = [pltpu.SMEM if o.dtype == jnp.int32 else pltpu.VMEM for o in operands]
    return pl.pallas_call(
        kernel if lay is None else functools.partial(kernel, lay),
        out_shape=outs,
        in_specs=[pl.BlockSpec(memory_space=space) for space in spaces],
        out_specs=jax.tree.map(lambda _: pl.BlockSpec(memory_space=pltpu.VMEM), outs),
        cost_estimate=cost,
        compiler_params=pltpu.CompilerParams(vmem_limit_bytes=LIMIT),
        name=kernel.__name__,
    )(*operands)


def per_device(initial_state, velocity, diffusion, forcing, implicit, coarse_implicit):
    own, columns = initial_state.shape
    steps = forcing.shape[0]
    blocks = lax.axis_size("tm")
    slabs = lax.axis_size("space")
    place = lax.axis_index("tm").astype(jnp.int32).reshape(1)
    lay = Layout(steps, own)
    near = own + 2 * steps

    def kept(*shape, dtype=F32):
        return pltpu.VMEM(shape, dtype)

    first_pack = kept(lay.first_rows, columns, dtype=BF16)
    hbm = pl.BlockSpec(memory_space=pltpu.HBM)
    head, tail = pl.pallas_call(
        functools.partial(pack, lay),
        out_shape=[first_pack] * 2,
        in_specs=[hbm] * 4,
        out_specs=[pl.BlockSpec(memory_space=pltpu.VMEM)] * 2,
        scratch_shapes=[pltpu.VMEM((own, columns), F32), pltpu.SemaphoreType.DMA((1 + 2 * (steps + 2),))],
        compiler_params=pltpu.CompilerParams(vmem_limit_bytes=LIMIT),
        name="pack",
    )(*(pltpu.with_memory_space_constraint(x, pltpu.HBM) for x in (velocity, diffusion, forcing, initial_state)))
    low = in_vmem(lax.ppermute(tail, "space", ring(slabs, 1)))
    high = in_vmem(lax.ppermute(head, "space", ring(slabs, -1)))
    high_m, low_m, coarse = call(
        split_matrices, None, [kept(*implicit.shape, dtype=BF16)] * 3, implicit, coarse_implicit
    )
    high_m, low_m, coarse = in_vmem(high_m), in_vmem(low_m), in_vmem(coarse)
    second_pack = kept(lay.second_rows, columns, dtype=BF16)
    a, head, tail = call(
        first_sweep,
        lay,
        [kept(own, columns), second_pack, second_pack],
        place, low, high, forcing, velocity, diffusion, initial_state, high_m, low_m,
    )
    far_low = in_vmem(lax.ppermute(tail, "space", ring(slabs, 1)))
    far_high = in_vmem(lax.ppermute(head, "space", ring(slabs, -1)))
    rho, rho_low, a_near, weights = call(
        second_sweep,
        lay,
        [
            kept(own + 2 * lay.keep, columns, dtype=BF16),
            kept(own, columns, dtype=BF16),
            kept(near, columns),
            kept(3, own + 2 * lay.wide, columns),
        ],
        far_low, far_high, in_vmem(a), velocity, diffusion, high_m, low_m,
    )
    weights = in_vmem(weights)
    rho_all = lax.all_gather(rho, "tm", axis=0)
    shared = blocks % 2 == 0 and 4 <= blocks <= 8
    count = (blocks - 2) // 2 if shared else 1
    change, passed, b_own = call(
        coarse_and_third,
        lay,
        [
            kept(count, own + 2 * lay.fine, columns),
            kept(2 * near + own, columns, dtype=BF16),
            kept(own, columns),
        ],
        place, rho_all, in_vmem(rho_low), in_vmem(a_near), weights, high_m, low_m, coarse,
    )
    passed = lax.ppermute(passed, "tm", ring(blocks, 1))
    psi = call(
        fourth_sweep,
        lay,
        kept(count, near, columns, dtype=BF16),
        in_vmem(change), weights, high_m,
        cost=pl.CostEstimate(
            flops=2 * steps * count * (own + 2 * lay.fine) * columns * columns,
            bytes_accessed=4 * count * (own + 2 * lay.fine) * columns,
            transcendentals=0,
        ),
    )
    if shared:
        psi_other = lax.ppermute(psi, "tm", [(i, i ^ 1) for i in range(blocks)])
        sources, kernel = (in_vmem(psi), in_vmem(psi_other)), last_sweep
    else:
        sources, kernel = (lax.all_gather(psi[0], "tm", axis=0),), last_sweep_gathered
    return call(
        kernel,
        lay,
        jax.ShapeDtypeStruct((steps, own, columns), F32),
        place, *sources, in_vmem(passed), in_vmem(b_own), low, high, forcing, weights, initial_state,
        high_m, low_m, coarse,
    )


def solution(mesh):
    in_specs = (
        P("space", None),
        P("space", None),
        P("space", None),
        P("tm", "space", None),
        P(),
        P(),
    )
    out_specs = P("tm", "space", None)
    return jax.shard_map(per_device, mesh=mesh, in_specs=in_specs, out_specs=out_specs, check_vma=False)
```

```python
import functools

import jax
import jax.numpy as jnp
from jax import lax
from jax.experimental import pallas as pl
from jax.experimental.pallas import tpu as pltpu
from jax.sharding import PartitionSpec as P


F32 = jnp.float32
BF16 = jnp.bfloat16
LIMIT = 16 << 20


def ring(count, distance):
    return [(i, (i + distance) % count) for i in range(count)]


def split(value):
    high = value.astype(BF16)
    return high, (value - high.astype(F32)).astype(BF16)


def product(left, right):
    return jnp.dot(left, right, preferred_element_type=F32)


def product3(value, high_matrix, low_matrix):
    rows = value.shape[0]
    high, low = split(value)
    both = product(jnp.concatenate([high, low], axis=0), high_matrix)
    return both[:rows] + (both[rows:] + product(high, low_matrix))


def stencil(value, weights):
    west, centre, east = weights
    return centre * value + east * jnp.roll(value, -1, 0) + west * jnp.roll(value, 1, 0)


class Layout:
    def __init__(self, steps, own):
        self.steps = steps
        self.own = own
        self.wide = 4 * steps
        self.keep = 3 * steps
        self.fine = 2 * steps
        self.velocity = steps * steps
        self.diffusion = self.velocity + steps
        self.start = self.diffusion + steps
        self.start_low = self.start + steps
        self.first_rows = self.start_low + steps
        self.tail = self.wide
        self.far_velocity = self.tail + self.fine
        self.far_diffusion = self.far_velocity + self.wide
        self.second_rows = self.far_diffusion + self.wide

    def centred(self, width, inside):
        return slice(width - inside, width + self.own + inside)


def pack(lay, velocity, diffusion, forcing, start, head, tail, start_kept, semaphores):
    steps, own = lay.steps, lay.own
    copies = [(start, start_kept)]
    for out, first in ((head, 0), (tail, own - steps)):
        near = pl.ds(first, steps)
        for step in range(steps):
            copies.append((forcing.at[step, near], out.at[pl.ds(step * steps, steps)]))
        copies.append((velocity.at[near], out.at[pl.ds(lay.velocity, steps)]))
        copies.append((diffusion.at[near], out.at[pl.ds(lay.diffusion, steps)]))
    copies = [pltpu.make_async_copy(*pair, semaphores.at[i]) for i, pair in enumerate(copies)]
    for copy in copies:
        copy.start()
    for copy in copies:
        copy.wait()
    for out, first in ((head, 0), (tail, own - steps)):
        high, low = split(start_kept[first : first + steps])
        out[lay.start : lay.start_low] = high
        out[lay.start_low : lay.first_rows] = low


def split_matrices(implicit, coarse_implicit, high_m, low_m, coarse, fine_kept, coarse_kept, semaphores):
    fine_copy = pltpu.make_async_copy(implicit, fine_kept, semaphores.at[0])
    coarse_copy = pltpu.make_async_copy(coarse_implicit, coarse_kept, semaphores.at[1])
    fine_copy.start()
    coarse_copy.start()
    fine_copy.wait()
    high_m[...], low_m[...] = split(fine_kept[...])
    coarse_copy.wait()
    coarse[...] = coarse_kept[...].astype(BF16)


def joined(low, own, high):
    return jnp.concatenate([low.astype(F32), own.astype(F32), high.astype(F32)], axis=0)


def from_first(lay, low, own, high, at):
    rows = slice(at, at + lay.steps)
    return joined(low[rows], own, high[rows])


def start_from_first(lay, low, own, high):
    value = from_first(lay, low, own, high, lay.start)
    return value + from_first(lay, low, jnp.zeros(own.shape, F32), high, lay.start_low)


def make_weights(moving, spread):
    return spread + 0.5 * moving, 1.0 - 2.0 * spread, spread - 0.5 * moving


def first_sweep(lay, place, low, high, forcing, velocity, diffusion, start, high_m, low_m, a, head, tail):
    steps, own = lay.steps, lay.own
    weights = make_weights(
        from_first(lay, low, velocity[...], high, lay.velocity),
        from_first(lay, low, diffusion[...], high, lay.diffusion),
    )
    current = jnp.where(place[0] == 0, start_from_first(lay, low, start[...], high), 0.0)
    for step in range(steps):
        summed = stencil(current, weights) + from_first(lay, low, forcing[step], high, step * steps)
        current = product3(summed, high_m[...], low_m[...])
    current = current[lay.centred(steps, 0)]
    a[...] = current
    high_part, low_part = split(current)
    for out, far, near in (
        (head, slice(0, lay.wide), slice(0, lay.fine)),
        (tail, slice(own - lay.wide, own), slice(own - lay.fine, own)),
    ):
        out[: lay.tail] = high_part[far]
        out[lay.tail : lay.far_velocity] = low_part[near]
        out[lay.far_velocity : lay.far_diffusion] = velocity[far]
        out[lay.far_diffusion :] = diffusion[far]


def second_sweep(lay, low, high, a, velocity, diffusion, high_m, low_m, rho, rho_low, a_near, weights):
    wide, steps, fine = lay.wide, lay.steps, lay.fine

    def extended(own, at):
        return joined(low[at : at + wide], own, high[at : at + wide])

    weights[0], weights[1], weights[2] = make_weights(
        extended(velocity[...], lay.far_velocity), extended(diffusion[...], lay.far_diffusion)
    )
    tails = slice(lay.tail, lay.far_velocity)
    current = joined(
        jnp.concatenate([low[: wide - fine].astype(F32), low[wide - fine : wide].astype(F32) + low[tails].astype(F32)], axis=0),
        a[...],
        jnp.concatenate([high[:fine].astype(F32) + high[tails].astype(F32), high[fine:wide].astype(F32)], axis=0),
    )
    a_near[...] = current[lay.centred(wide, steps)]
    for _ in range(steps):
        current = product3(stencil(current, weights[...]), high_m[...], low_m[...])
    high_part, low_part = split(current)
    rho[...] = high_part[lay.centred(wide, lay.keep)]
    rho_low[...] = low_part[lay.centred(wide, 0)]


def coarse_and_third(lay, place, rho, rho_low, a_near, weights, high_m, low_m, coarse, change, passed, b_own):
    keep, steps, own = lay.keep, lay.steps, lay.own
    rows = own + 2 * keep
    count = change.shape[0]
    at = place[0]
    narrow = weights[:, lay.centred(lay.wide, keep)]
    near = lay.centred(keep, steps)
    shared = count > 1

    def turn(source, carried):
        return product(carried.astype(BF16), coarse[...]) + rho[source].astype(F32)

    if shared:
        odd = at % 2 == 1
        error = rho[0].astype(F32)
        errors = []
        for item in range(count):
            following = turn(2 * item + 1, error)
            errors.append(jnp.where(odd, following, error))
            if item < count - 1:
                error = turn(2 * item + 2, following)
    else:
        first = jnp.where(at >= 2, rho[0].astype(F32), 0.0)
        errors = [lax.fori_loop(1, at - 1, turn, first)]
    kept = jnp.concatenate([error.astype(BF16) for error in errors], axis=0)
    current = jnp.concatenate(errors, axis=0)
    for _ in range(steps):
        moved = [stencil(current[i * rows : (i + 1) * rows], narrow) for i in range(count)]
        current = product3(jnp.concatenate(moved, axis=0), high_m[...], low_m[...])
    coarse_part = product(kept, coarse[...])
    mine = jnp.zeros((own + 2 * steps, current.shape[1]), F32)
    inner = lay.centred(keep, lay.fine)
    for i in range(count):
        swept = current[i * rows : (i + 1) * rows]
        here = (at - 2) // 2 == i if shared else True
        mine = mine + jnp.where(jnp.logical_and(here, at >= 2), swept[near], 0.0)
        change[i] = swept[inner] - coarse_part[i * rows : (i + 1) * rows][inner]
    before = rho[jnp.maximum(at - 1, 0)].astype(F32)[near]
    b = a_near[...] + jnp.where(at == 0, 0.0, before) + mine
    b_own[...] = b[lay.centred(steps, 0)]
    rows = own + 2 * steps
    passed[:rows], passed[rows : 2 * rows] = split(b)
    passed[2 * rows :] = rho_low[...]


def fourth_sweep(lay, change, weights, high_m, psi):
    steps = lay.steps
    count, rows, _ = change.shape
    narrow = weights[:, lay.centred(lay.wide, lay.fine)]
    current = jnp.concatenate([change[i] for i in range(count)], axis=0)
    for _ in range(steps):
        moved = [stencil(current[i * rows : (i + 1) * rows], narrow).astype(BF16) for i in range(count)]
        current = product(jnp.concatenate(moved, axis=0), high_m[...])
    for i in range(count):
        psi[i] = current[i * rows : (i + 1) * rows][lay.centred(lay.fine, steps)].astype(BF16)


def last_sweep(lay, place, psi, psi_other, passed, b_own, low, high, forcing, weights, start, high_m, low_m, coarse, out):
    steps, own = lay.steps, lay.own
    at = place[0]
    rows = own + 2 * steps
    narrow = weights[:, lay.centred(lay.wide, steps)]
    shared = psi_other is not None

    def source(block):
        if not shared:
            return psi[block].astype(F32)
        item = block // 2 - 1
        return jnp.where((block - at) % 2 == 0, psi[item].astype(F32), psi_other[item].astype(F32))

    def turn(block, carried):
        return product(carried.astype(BF16), coarse[...]) + source(block)

    error = lax.fori_loop(2, at - 1, turn, jnp.zeros((rows, start.shape[1]), F32))
    b_before = passed[:rows].astype(F32) + passed[rows : 2 * rows].astype(F32)
    initial = start_from_first(lay, low, start[...], high)
    current = jnp.where(at == 0, initial, b_before + error)
    mid = lay.centred(steps, 0)
    last = product(error[mid].astype(BF16), coarse[...])
    last = last + jnp.where(at >= 3, source(jnp.maximum(at - 1, 2))[mid], 0.0)
    last = last + passed[2 * rows :].astype(F32)
    out[steps - 1] = b_own[...] + jnp.where(at == 0, 0.0, last)
    for step in range(steps - 1):
        summed = stencil(current, narrow) + from_first(lay, low, forcing[step], high, step * steps)
        current = product3(summed, high_m[...], low_m[...])
        out[step] = current[mid]


def last_sweep_gathered(lay, place, psi, *rest):
    last_sweep(lay, place, psi, None, *rest)


def in_vmem(value):
    return pltpu.with_memory_space_constraint(value, pltpu.VMEM)


def call(kernel, lay, outs, *operands):
    spaces = [pltpu.SMEM if o.dtype == jnp.int32 else pltpu.VMEM for o in operands]
    return pl.pallas_call(
        kernel if lay is None else functools.partial(kernel, lay),
        out_shape=outs,
        in_specs=[pl.BlockSpec(memory_space=space) for space in spaces],
        out_specs=jax.tree.map(lambda _: pl.BlockSpec(memory_space=pltpu.VMEM), outs),
        compiler_params=pltpu.CompilerParams(vmem_limit_bytes=LIMIT),
    )(*operands)


def call_from_hbm(kernel, outs, scratch, *operands):
    return pl.pallas_call(
        kernel,
        out_shape=outs,
        in_specs=[pl.BlockSpec(memory_space=pltpu.HBM)] * len(operands),
        out_specs=[pl.BlockSpec(memory_space=pltpu.VMEM)] * len(outs),
        scratch_shapes=scratch,
        compiler_params=pltpu.CompilerParams(vmem_limit_bytes=LIMIT),
    )(*(pltpu.with_memory_space_constraint(value, pltpu.HBM) for value in operands))


def per_device(initial_state, velocity, diffusion, forcing, implicit, coarse_implicit):
    own, columns = initial_state.shape
    steps = forcing.shape[0]
    blocks = lax.axis_size("tm")
    slabs = lax.axis_size("space")
    place = lax.axis_index("tm").astype(jnp.int32).reshape(1)
    lay = Layout(steps, own)
    near = own + 2 * steps

    def kept(*shape, dtype=F32):
        return pltpu.VMEM(shape, dtype)

    first_pack = kept(lay.first_rows, columns, dtype=BF16)
    head, tail = call_from_hbm(
        functools.partial(pack, lay),
        [first_pack] * 2,
        [pltpu.VMEM((own, columns), F32), pltpu.SemaphoreType.DMA((1 + 2 * (steps + 2),))],
        velocity, diffusion, forcing, initial_state,
    )
    low = in_vmem(lax.ppermute(tail, "space", ring(slabs, 1)))
    high = in_vmem(lax.ppermute(head, "space", ring(slabs, -1)))
    high_m, low_m, coarse = call_from_hbm(
        split_matrices,
        [kept(*implicit.shape, dtype=BF16)] * 3,
        [pltpu.VMEM(implicit.shape, F32), pltpu.VMEM(implicit.shape, F32), pltpu.SemaphoreType.DMA((2,))],
        implicit, coarse_implicit,
    )
    high_m, low_m, coarse = in_vmem(high_m), in_vmem(low_m), in_vmem(coarse)
    second_pack = kept(lay.second_rows, columns, dtype=BF16)
    a, head, tail = call(
        first_sweep,
        lay,
        [kept(own, columns), second_pack, second_pack],
        place, low, high, forcing, velocity, diffusion, initial_state, high_m, low_m,
    )
    far_low = in_vmem(lax.ppermute(tail, "space", ring(slabs, 1)))
    far_high = in_vmem(lax.ppermute(head, "space", ring(slabs, -1)))
    rho, rho_low, a_near, weights = call(
        second_sweep,
        lay,
        [
            kept(own + 2 * lay.keep, columns, dtype=BF16),
            kept(own, columns, dtype=BF16),
            kept(near, columns),
            kept(3, own + 2 * lay.wide, columns),
        ],
        far_low, far_high, in_vmem(a), velocity, diffusion, high_m, low_m,
    )
    weights = in_vmem(weights)
    rho_all = lax.all_gather(rho, "tm", axis=0)
    shared = blocks % 2 == 0 and 4 <= blocks <= 8
    count = (blocks - 2) // 2 if shared else 1
    change, passed, b_own = call(
        coarse_and_third,
        lay,
        [
            kept(count, own + 2 * lay.fine, columns),
            kept(2 * near + own, columns, dtype=BF16),
            kept(own, columns),
        ],
        place, rho_all, in_vmem(rho_low), in_vmem(a_near), weights, high_m, low_m, coarse,
    )
    passed = lax.ppermute(passed, "tm", ring(blocks, 1))
    psi = call(fourth_sweep, lay, kept(count, near, columns, dtype=BF16), in_vmem(change), weights, high_m)
    if shared:
        psi_other = lax.ppermute(psi, "tm", [(i, i ^ 1) for i in range(blocks)])
        sources, kernel = (in_vmem(psi), in_vmem(psi_other)), last_sweep
    else:
        sources, kernel = (lax.all_gather(psi[0], "tm", axis=0),), last_sweep_gathered
    return call(
        kernel,
        lay,
        jax.ShapeDtypeStruct((steps, own, columns), F32),
        place, *sources, in_vmem(passed), in_vmem(b_own), low, high, forcing, weights, initial_state,
        high_m, low_m, coarse,
    )


def solution(mesh):
    in_specs = (
        P("space", None),
        P("space", None),
        P("space", None),
        P("tm", "space", None),
        P(),
        P(),
    )
    out_specs = P("tm", "space", None)
    return jax.shard_map(per_device, mesh=mesh, in_specs=in_specs, out_specs=out_specs, check_vma=False)
```

```python
import functools

import jax
import jax.numpy as jnp
from jax import lax
from jax.experimental import pallas as pl
from jax.experimental.pallas import tpu as pltpu
from jax.sharding import PartitionSpec as P


F32 = jnp.float32
BF16 = jnp.bfloat16
LIMIT = 16 << 20


def ring(count, distance):
    return [(i, (i + distance) % count) for i in range(count)]


def split(value):
    high = value.astype(BF16)
    return high, (value - high.astype(F32)).astype(BF16)


def product(left, right):
    return jnp.dot(left, right, preferred_element_type=F32)


def product3(value, high_matrix, low_matrix):
    rows = value.shape[0]
    high, low = split(value)
    both = product(jnp.concatenate([high, low], axis=0), high_matrix)
    return both[:rows] + (both[rows:] + product(high, low_matrix))


def stencil(value, weights):
    west, centre, east = weights
    return centre * value + east * jnp.roll(value, -1, 0) + west * jnp.roll(value, 1, 0)


def turned(value, shift):
    return value if shift % value.shape[0] == 0 else jnp.roll(value, shift, 0)


class Layout:
    def __init__(self, steps, own):
        self.steps = steps
        self.own = own
        self.fine = 2 * steps
        self.keep = 3 * steps
        self.wide = 4 * steps
        self.groups = steps // 2
        self.outer = steps * steps
        self.velocity = self.outer + self.groups * steps
        self.diffusion = self.velocity + self.fine
        self.start = self.diffusion + self.fine
        self.start_low = self.start + self.fine
        self.first_rows = self.start_low + self.fine
        self.sent = self.wide - steps
        self.far_velocity = self.sent
        self.far_diffusion = self.far_velocity + self.wide - self.fine
        self.second_rows = self.far_diffusion + self.wide - self.fine

    def centred(self, width, inside):
        return slice(width - inside, width + self.own + inside)


def pack(lay, velocity, diffusion, forcing, start, head, tail, start_kept, outer_kept, semaphores):
    steps, own, fine = lay.steps, lay.own, lay.fine
    sides = ((head, 0, 0, steps), (tail, own - fine, own - steps, own - fine))
    copies = [(start, start_kept)]
    for side, (out, first, inner, outer) in enumerate(sides):
        near = pl.ds(first, fine)
        copies.append((forcing.at[:, pl.ds(outer, steps)], outer_kept.at[side]))
        for step in range(steps):
            copies.append((forcing.at[step, pl.ds(inner, steps)], out.at[pl.ds(step * steps, steps)]))
        copies.append((velocity.at[near], out.at[pl.ds(lay.velocity, fine)]))
        copies.append((diffusion.at[near], out.at[pl.ds(lay.diffusion, fine)]))
    copies = [pltpu.make_async_copy(*pair, semaphores.at[i]) for i, pair in enumerate(copies)]
    for copy in copies:
        copy.start()
    for copy in copies:
        copy.wait()
    for side, (out, first, _, _) in enumerate(sides):
        high, low = split(start_kept[first : first + fine])
        out[lay.start : lay.start_low] = high
        out[lay.start_low : lay.first_rows] = low
        for group in range(lay.groups):
            one = outer_kept[side, group].astype(F32)
            other = outer_kept[side, steps - 1 - group].astype(F32)
            row = lax.broadcasted_iota(jnp.int32, one.shape, 0)
            if side == 0:
                both = jnp.where(row < steps - 1 - group, one, turned(other, -group))
            else:
                both = jnp.where(row > group, one, turned(other, group))
            at = lay.outer + group * steps
            out[at : at + steps] = both.astype(BF16)


def split_matrices(implicit, coarse_implicit, high_m, low_m, coarse, fine_kept, coarse_kept, semaphores):
    fine_copy = pltpu.make_async_copy(implicit, fine_kept, semaphores.at[0])
    coarse_copy = pltpu.make_async_copy(coarse_implicit, coarse_kept, semaphores.at[1])
    fine_copy.start()
    coarse_copy.start()
    fine_copy.wait()
    high_m[...], low_m[...] = split(fine_kept[...])
    coarse_copy.wait()
    coarse[...] = coarse_kept[...].astype(BF16)


def joined(low, own, high):
    return jnp.concatenate([low.astype(F32), own.astype(F32), high.astype(F32)], axis=0)


def near_forcing(lay, low, own, high, step):
    rows = slice(step * lay.steps, (step + 1) * lay.steps)
    return joined(low[rows], own, high[rows])


def near_start(lay, low, own, high):
    def side(packed, at):
        rows = slice(at, at + lay.steps)
        shift = lay.start_low - lay.start
        return packed[rows].astype(F32) + packed[rows.start + shift : rows.stop + shift].astype(F32)

    return joined(side(low, lay.start + lay.fine - lay.steps), own, side(high, lay.start))


def make_weights(moving, spread):
    return spread + 0.5 * moving, 1.0 - 2.0 * spread, spread - 0.5 * moving


def inner_sweep(lay, place, forcing, velocity, diffusion, start, high_m, low_m, a, head, tail):
    steps, own = lay.steps, lay.own
    weights = make_weights(velocity[...].astype(F32), diffusion[...].astype(F32))
    current = jnp.where(place[0] == 0, start[...], 0.0)
    for step in range(steps):
        current = product3(stencil(current, weights) + forcing[step].astype(F32), high_m[...], low_m[...])
    a[...] = current
    for out, first, far in (
        (head, steps, slice(lay.fine, lay.wide)),
        (tail, own - steps - lay.sent, slice(own - lay.wide, own - lay.fine)),
    ):
        out[: lay.sent] = current[first : first + lay.sent].astype(BF16)
        out[lay.far_velocity : lay.far_diffusion] = velocity[far]
        out[lay.far_diffusion :] = diffusion[far]


def edge_sweep(lay, place, low, high, forcing, velocity, diffusion, start, high_m, low_m, edges):
    steps, own, fine = lay.steps, lay.own, lay.fine

    def windows(before, ours, after):
        return jnp.concatenate(
            [part.astype(F32) for part in (before, ours[:fine], ours[own - fine :], after)], axis=0
        )

    def packed(ours, at):
        return windows(low[at : at + fine], ours, high[at : at + fine])

    weights = make_weights(packed(velocity[...], lay.velocity), packed(diffusion[...], lay.diffusion))
    current = packed(start[...], lay.start)
    current = current + packed(jnp.zeros((own, start.shape[1]), F32), lay.start_low)
    current = jnp.where(place[0] == 0, current, 0.0)
    for step in range(steps):
        rows = slice(step * steps, (step + 1) * steps)
        group = min(step, steps - 1 - step)
        at = lay.outer + group * steps
        before, after = low[at : at + steps].astype(F32), high[at : at + steps].astype(F32)
        if step > group:
            before, after = turned(before, -group), turned(after, group)
        source = windows(
            jnp.concatenate([before, low[rows].astype(F32)], axis=0),
            forcing[step],
            jnp.concatenate([high[rows].astype(F32), after], axis=0),
        )
        current = product3(stencil(current, weights) + source, high_m[...], low_m[...])
    edges[:fine] = current[steps : steps + fine]
    edges[fine:] = current[3 * steps + fine : 3 * steps + 2 * fine]


def second_sweep(
    lay, low, high, far_low, far_high, a, edges, velocity, diffusion, high_m, low_m, rho, rho_low, a_near, weights
):
    steps, fine, wide, own = lay.steps, lay.fine, lay.wide, lay.own

    def extended(ours, at, far):
        rows, far_rows = slice(at, at + fine), slice(far, far + wide - fine)
        return joined(
            jnp.concatenate([far_low[far_rows].astype(F32), low[rows].astype(F32)], axis=0),
            ours,
            jnp.concatenate([high[rows].astype(F32), far_high[far_rows].astype(F32)], axis=0),
        )

    weights[0], weights[1], weights[2] = make_weights(
        extended(velocity[...], lay.velocity, lay.far_velocity),
        extended(diffusion[...], lay.diffusion, lay.far_diffusion),
    )
    near = jnp.concatenate([edges[:fine], a[steps : own - steps], edges[fine:]], axis=0)
    a_near[...] = near
    current = joined(far_low[: lay.sent], near, far_high[: lay.sent])
    for _ in range(steps):
        current = product3(stencil(current, weights[...]), high_m[...], low_m[...])
    high_part, low_part = split(current)
    rho[...] = high_part[lay.centred(wide, lay.keep)]
    rho_low[...] = low_part[lay.centred(wide, 0)]


def coarse_and_third(lay, place, rho, rho_low, a_near, weights, high_m, low_m, coarse, change, passed, b_own):
    keep, steps, own = lay.keep, lay.steps, lay.own
    rows = own + 2 * keep
    count = change.shape[0]
    at = place[0]
    narrow = weights[:, lay.centred(lay.wide, keep)]
    near = lay.centred(keep, steps)
    shared = count > 1

    def turn(source, carried):
        return product(carried.astype(BF16), coarse[...]) + rho[source].astype(F32)

    if shared:
        odd = at % 2 == 1
        error = rho[0].astype(F32)
        errors = []
        for item in range(count):
            following = turn(2 * item + 1, error)
            errors.append(jnp.where(odd, following, error))
            if item < count - 1:
                error = turn(2 * item + 2, following)
    else:
        first = jnp.where(at >= 2, rho[0].astype(F32), 0.0)
        errors = [lax.fori_loop(1, at - 1, turn, first)]
    kept = jnp.concatenate([error.astype(BF16) for error in errors], axis=0)
    current = jnp.concatenate(errors, axis=0)
    for _ in range(steps):
        moved = [stencil(current[i * rows : (i + 1) * rows], narrow) for i in range(count)]
        current = product3(jnp.concatenate(moved, axis=0), high_m[...], low_m[...])
    coarse_part = product(kept, coarse[...])
    mine = jnp.zeros((own + 2 * steps, current.shape[1]), F32)
    inner = lay.centred(keep, lay.fine)
    for i in range(count):
        swept = current[i * rows : (i + 1) * rows]
        here = (at - 2) // 2 == i if shared else True
        mine = mine + jnp.where(jnp.logical_and(here, at >= 2), swept[near], 0.0)
        change[i] = swept[inner] - coarse_part[i * rows : (i + 1) * rows][inner]
    before = rho[jnp.maximum(at - 1, 0)].astype(F32)[near]
    b = a_near[...] + jnp.where(at == 0, 0.0, before) + mine
    b_own[...] = b[lay.centred(steps, 0)]
    rows = own + 2 * steps
    passed[:rows], passed[rows : 2 * rows] = split(b)
    passed[2 * rows :] = rho_low[...]


def fourth_sweep(lay, change, weights, high_m, psi):
    steps = lay.steps
    count, rows, _ = change.shape
    narrow = weights[:, lay.centred(lay.wide, lay.fine)]
    current = jnp.concatenate([change[i] for i in range(count)], axis=0)
    for _ in range(steps):
        moved = [stencil(current[i * rows : (i + 1) * rows], narrow).astype(BF16) for i in range(count)]
        current = product(jnp.concatenate(moved, axis=0), high_m[...])
    for i in range(count):
        psi[i] = current[i * rows : (i + 1) * rows][lay.centred(lay.fine, steps)].astype(BF16)


def last_sweep(lay, place, psi, psi_other, passed, b_own, low, high, forcing, weights, start, high_m, low_m, coarse, out):
    steps, own = lay.steps, lay.own
    at = place[0]
    rows = own + 2 * steps
    narrow = weights[:, lay.centred(lay.wide, steps)]
    shared = psi_other is not None

    def source(block):
        if not shared:
            return psi[block].astype(F32)
        item = block // 2 - 1
        return jnp.where((block - at) % 2 == 0, psi[item].astype(F32), psi_other[item].astype(F32))

    def turn(block, carried):
        return product(carried.astype(BF16), coarse[...]) + source(block)

    error = lax.fori_loop(2, at - 1, turn, jnp.zeros((rows, start.shape[1]), F32))
    b_before = passed[:rows].astype(F32) + passed[rows : 2 * rows].astype(F32)
    initial = near_start(lay, low, start[...], high)
    current = jnp.where(at == 0, initial, b_before + error)
    mid = lay.centred(steps, 0)
    last = product(error[mid].astype(BF16), coarse[...])
    last = last + jnp.where(at >= 3, source(jnp.maximum(at - 1, 2))[mid], 0.0)
    last = last + passed[2 * rows :].astype(F32)
    out[steps - 1] = b_own[...] + jnp.where(at == 0, 0.0, last)
    for step in range(steps - 1):
        summed = stencil(current, narrow) + near_forcing(lay, low, forcing[step], high, step)
        current = product3(summed, high_m[...], low_m[...])
        out[step] = current[mid]


def last_sweep_gathered(lay, place, psi, *rest):
    last_sweep(lay, place, psi, None, *rest)


def in_vmem(value):
    return pltpu.with_memory_space_constraint(value, pltpu.VMEM)


def call(kernel, lay, outs, *operands):
    spaces = [pltpu.SMEM if o.dtype == jnp.int32 else pltpu.VMEM for o in operands]
    return pl.pallas_call(
        kernel if lay is None else functools.partial(kernel, lay),
        out_shape=outs,
        in_specs=[pl.BlockSpec(memory_space=space) for space in spaces],
        out_specs=jax.tree.map(lambda _: pl.BlockSpec(memory_space=pltpu.VMEM), outs),
        compiler_params=pltpu.CompilerParams(vmem_limit_bytes=LIMIT),
    )(*operands)


def call_from_hbm(kernel, outs, scratch, *operands):
    return pl.pallas_call(
        kernel,
        out_shape=outs,
        in_specs=[pl.BlockSpec(memory_space=pltpu.HBM)] * len(operands),
        out_specs=[pl.BlockSpec(memory_space=pltpu.VMEM)] * len(outs),
        scratch_shapes=scratch,
        compiler_params=pltpu.CompilerParams(vmem_limit_bytes=LIMIT),
    )(*(pltpu.with_memory_space_constraint(value, pltpu.HBM) for value in operands))


def per_device(initial_state, velocity, diffusion, forcing, implicit, coarse_implicit):
    own, columns = initial_state.shape
    steps = forcing.shape[0]
    blocks = lax.axis_size("tm")
    slabs = lax.axis_size("space")
    place = lax.axis_index("tm").astype(jnp.int32).reshape(1)
    lay = Layout(steps, own)
    near = own + 2 * steps

    def kept(*shape, dtype=F32):
        return pltpu.VMEM(shape, dtype)

    first_pack = kept(lay.first_rows, columns, dtype=BF16)
    head, tail = call_from_hbm(
        functools.partial(pack, lay),
        [first_pack] * 2,
        [
            pltpu.VMEM((own, columns), F32),
            pltpu.VMEM((2, steps, steps, columns), BF16),
            pltpu.SemaphoreType.DMA((1 + 2 * (steps + 3),)),
        ],
        velocity, diffusion, forcing, initial_state,
    )
    low = in_vmem(lax.ppermute(tail, "space", ring(slabs, 1)))
    high = in_vmem(lax.ppermute(head, "space", ring(slabs, -1)))
    high_m, low_m, coarse = call_from_hbm(
        split_matrices,
        [kept(*implicit.shape, dtype=BF16)] * 3,
        [pltpu.VMEM(implicit.shape, F32), pltpu.VMEM(implicit.shape, F32), pltpu.SemaphoreType.DMA((2,))],
        implicit, coarse_implicit,
    )
    high_m, low_m, coarse = in_vmem(high_m), in_vmem(low_m), in_vmem(coarse)
    second_pack = kept(lay.second_rows, columns, dtype=BF16)
    a, head, tail = call(
        inner_sweep,
        lay,
        [kept(own, columns), second_pack, second_pack],
        place, forcing, velocity, diffusion, initial_state, high_m, low_m,
    )
    far_low = in_vmem(lax.ppermute(tail, "space", ring(slabs, 1)))
    far_high = in_vmem(lax.ppermute(head, "space", ring(slabs, -1)))
    edges = call(
        edge_sweep,
        lay,
        kept(2 * lay.fine, columns),
        place, low, high, forcing, velocity, diffusion, initial_state, high_m, low_m,
    )
    rho, rho_low, a_near, weights = call(
        second_sweep,
        lay,
        [
            kept(own + 2 * lay.keep, columns, dtype=BF16),
            kept(own, columns, dtype=BF16),
            kept(near, columns),
            kept(3, own + 2 * lay.wide, columns),
        ],
        low, high, far_low, far_high, in_vmem(a), in_vmem(edges), velocity, diffusion, high_m, low_m,
    )
    weights = in_vmem(weights)
    rho_all = lax.all_gather(rho, "tm", axis=0)
    shared = blocks % 2 == 0 and 4 <= blocks <= 8
    count = (blocks - 2) // 2 if shared else 1
    change, passed, b_own = call(
        coarse_and_third,
        lay,
        [
            kept(count, own + 2 * lay.fine, columns),
            kept(2 * near + own, columns, dtype=BF16),
            kept(own, columns),
        ],
        place, rho_all, in_vmem(rho_low), in_vmem(a_near), weights, high_m, low_m, coarse,
    )
    passed = lax.ppermute(passed, "tm", ring(blocks, 1))
    psi = call(fourth_sweep, lay, kept(count, near, columns, dtype=BF16), in_vmem(change), weights, high_m)
    if shared:
        psi_other = lax.ppermute(psi, "tm", [(i, i ^ 1) for i in range(blocks)])
        sources, kernel = (in_vmem(psi), in_vmem(psi_other)), last_sweep
    else:
        sources, kernel = (lax.all_gather(psi[0], "tm", axis=0),), last_sweep_gathered
    return call(
        kernel,
        lay,
        jax.ShapeDtypeStruct((steps, own, columns), F32),
        place, *sources, in_vmem(passed), in_vmem(b_own), low, high, forcing, weights, initial_state,
        high_m, low_m, coarse,
    )


def solution(mesh):
    in_specs = (
        P("space", None),
        P("space", None),
        P("space", None),
        P("tm", "space", None),
        P(),
        P(),
    )
    out_specs = P("tm", "space", None)
    return jax.shard_map(per_device, mesh=mesh, in_specs=in_specs, out_specs=out_specs, check_vma=False)
```

```python
import functools

import jax
import jax.numpy as jnp
from jax import lax
from jax.experimental import pallas as pl
from jax.experimental.pallas import tpu as pltpu
from jax.sharding import PartitionSpec as P


F32 = jnp.float32
BF16 = jnp.bfloat16
LIMIT = 16 << 20
MARGIN = 8


def ring(count, distance):
    return [(i, (i + distance) % count) for i in range(count)]


def split(value):
    high = value.astype(BF16)
    return high, (value - high.astype(F32)).astype(BF16)


def product(left, right):
    return jnp.dot(left, right, preferred_element_type=F32)


def product3(value, high_matrix, low_matrix):
    rows = value.shape[0]
    high, low = split(value)
    both = product(jnp.concatenate([high, low], axis=0), high_matrix)
    return both[:rows] + (both[rows:] + product(high, low_matrix))


def stencil(value, weights):
    west, centre, east = weights
    return centre * value + east * jnp.roll(value, -1, 0) + west * jnp.roll(value, 1, 0)


def stored_stencil(kept, value, weights):
    west, centre, east = weights
    rows = value.shape[0]
    kept[MARGIN : MARGIN + rows] = value
    return centre * value + east * kept[MARGIN + 1 : MARGIN + 1 + rows] + west * kept[MARGIN - 1 : MARGIN - 1 + rows]


def clear_margins(kept):
    rows = kept.shape[0]
    kept[:MARGIN] = jnp.zeros((MARGIN, kept.shape[1]), F32)
    kept[rows - MARGIN :] = jnp.zeros((MARGIN, kept.shape[1]), F32)


def turned(value, shift):
    return value if shift % value.shape[0] == 0 else jnp.roll(value, shift, 0)


class Layout:
    def __init__(self, steps, own):
        self.steps = steps
        self.own = own
        self.fine = 2 * steps
        self.keep = 3 * steps
        self.wide = 4 * steps
        self.groups = steps // 2
        self.outer = steps * steps
        self.velocity = self.outer + self.groups * steps
        self.diffusion = self.velocity + self.fine
        self.start = self.diffusion + self.fine
        self.start_low = self.start + self.fine
        self.first_rows = self.start_low + self.fine
        self.sent = self.wide - steps
        self.far_velocity = self.sent
        self.far_diffusion = self.far_velocity + self.wide - self.fine
        self.second_rows = self.far_diffusion + self.wide - self.fine

    def centred(self, width, inside):
        return slice(width - inside, width + self.own + inside)


def pack(lay, velocity, diffusion, forcing, start, head, tail, start_kept, outer_kept, semaphores):
    steps, own, fine = lay.steps, lay.own, lay.fine
    sides = ((head, 0, 0, steps), (tail, own - fine, own - steps, own - fine))
    copies = [(start, start_kept)]
    for side, (out, first, inner, outer) in enumerate(sides):
        near = pl.ds(first, fine)
        copies.append((forcing.at[:, pl.ds(outer, steps)], outer_kept.at[side]))
        for step in range(steps):
            copies.append((forcing.at[step, pl.ds(inner, steps)], out.at[pl.ds(step * steps, steps)]))
        copies.append((velocity.at[near], out.at[pl.ds(lay.velocity, fine)]))
        copies.append((diffusion.at[near], out.at[pl.ds(lay.diffusion, fine)]))
    copies = [pltpu.make_async_copy(*pair, semaphores.at[i]) for i, pair in enumerate(copies)]
    for copy in copies:
        copy.start()
    for copy in copies:
        copy.wait()
    for side, (out, first, _, _) in enumerate(sides):
        high, low = split(start_kept[first : first + fine])
        out[lay.start : lay.start_low] = high
        out[lay.start_low : lay.first_rows] = low
        for group in range(lay.groups):
            one = outer_kept[side, group].astype(F32)
            other = outer_kept[side, steps - 1 - group].astype(F32)
            row = lax.broadcasted_iota(jnp.int32, one.shape, 0)
            if side == 0:
                both = jnp.where(row < steps - 1 - group, one, turned(other, -group))
            else:
                both = jnp.where(row > group, one, turned(other, group))
            at = lay.outer + group * steps
            out[at : at + steps] = both.astype(BF16)


def split_matrices(implicit, coarse_implicit, high_m, low_m, coarse, fine_kept, coarse_kept, semaphores):
    fine_copy = pltpu.make_async_copy(implicit, fine_kept, semaphores.at[0])
    coarse_copy = pltpu.make_async_copy(coarse_implicit, coarse_kept, semaphores.at[1])
    fine_copy.start()
    coarse_copy.start()
    fine_copy.wait()
    high_m[...], low_m[...] = split(fine_kept[...])
    coarse_copy.wait()
    coarse[...] = coarse_kept[...].astype(BF16)


def joined(low, own, high):
    return jnp.concatenate([low.astype(F32), own.astype(F32), high.astype(F32)], axis=0)


def near_forcing(lay, low, own, high, step):
    rows = slice(step * lay.steps, (step + 1) * lay.steps)
    return joined(low[rows], own, high[rows])


def near_start(lay, low, own, high):
    def side(packed, at):
        rows = slice(at, at + lay.steps)
        shift = lay.start_low - lay.start
        return packed[rows].astype(F32) + packed[rows.start + shift : rows.stop + shift].astype(F32)

    return joined(side(low, lay.start + lay.fine - lay.steps), own, side(high, lay.start))


def make_weights(moving, spread):
    return spread + 0.5 * moving, 1.0 - 2.0 * spread, spread - 0.5 * moving


def inner_sweep(lay, place, forcing, velocity, diffusion, start, high_m, low_m, a, head, tail):
    steps, own = lay.steps, lay.own
    weights = make_weights(velocity[...].astype(F32), diffusion[...].astype(F32))
    current = jnp.where(place[0] == 0, start[...], 0.0)
    for step in range(steps):
        current = product3(stencil(current, weights) + forcing[step].astype(F32), high_m[...], low_m[...])
    a[...] = current
    for out, first, far in (
        (head, steps, slice(lay.fine, lay.wide)),
        (tail, own - steps - lay.sent, slice(own - lay.wide, own - lay.fine)),
    ):
        out[: lay.sent] = current[first : first + lay.sent].astype(BF16)
        out[lay.far_velocity : lay.far_diffusion] = velocity[far]
        out[lay.far_diffusion :] = diffusion[far]


def edge_sweep(lay, place, low, high, forcing, velocity, diffusion, start, high_m, low_m, edges):
    steps, own, fine = lay.steps, lay.own, lay.fine

    def windows(before, ours, after):
        return jnp.concatenate(
            [part.astype(F32) for part in (before, ours[:fine], ours[own - fine :], after)], axis=0
        )

    def packed(ours, at):
        return windows(low[at : at + fine], ours, high[at : at + fine])

    weights = make_weights(packed(velocity[...], lay.velocity), packed(diffusion[...], lay.diffusion))
    current = packed(start[...], lay.start)
    current = current + packed(jnp.zeros((own, start.shape[1]), F32), lay.start_low)
    current = jnp.where(place[0] == 0, current, 0.0)
    for step in range(steps):
        rows = slice(step * steps, (step + 1) * steps)
        group = min(step, steps - 1 - step)
        at = lay.outer + group * steps
        before, after = low[at : at + steps].astype(F32), high[at : at + steps].astype(F32)
        if step > group:
            before, after = turned(before, -group), turned(after, group)
        source = windows(
            jnp.concatenate([before, low[rows].astype(F32)], axis=0),
            forcing[step],
            jnp.concatenate([high[rows].astype(F32), after], axis=0),
        )
        current = product3(stencil(current, weights) + source, high_m[...], low_m[...])
    edges[:fine] = current[steps : steps + fine]
    edges[fine:] = current[3 * steps + fine : 3 * steps + 2 * fine]


def second_sweep(
    lay, low, high, far_low, far_high, a, edges, velocity, diffusion, high_m, low_m, rho, rho_low, a_near, weights, kept
):
    steps, fine, wide, own = lay.steps, lay.fine, lay.wide, lay.own

    def extended(ours, at, far):
        rows, far_rows = slice(at, at + fine), slice(far, far + wide - fine)
        return joined(
            jnp.concatenate([far_low[far_rows].astype(F32), low[rows].astype(F32)], axis=0),
            ours,
            jnp.concatenate([high[rows].astype(F32), far_high[far_rows].astype(F32)], axis=0),
        )

    weights[0], weights[1], weights[2] = make_weights(
        extended(velocity[...], lay.velocity, lay.far_velocity),
        extended(diffusion[...], lay.diffusion, lay.far_diffusion),
    )
    near = jnp.concatenate([edges[:fine], a[steps : own - steps], edges[fine:]], axis=0)
    a_near[...] = near
    current = joined(far_low[: lay.sent], near, far_high[: lay.sent])
    clear_margins(kept)
    for _ in range(steps):
        current = product3(stored_stencil(kept, current, weights[...]), high_m[...], low_m[...])
    high_part, low_part = split(current)
    rho[...] = high_part[lay.centred(wide, lay.keep)]
    rho_low[...] = low_part[lay.centred(wide, 0)]


def coarse_and_third(lay, place, rho, rho_low, a_near, weights, high_m, low_m, coarse, change, passed, b_own, field):
    keep, steps, own = lay.keep, lay.steps, lay.own
    rows = own + 2 * keep
    count = change.shape[0]
    at = place[0]
    narrow = weights[:, lay.centred(lay.wide, keep)]
    near = lay.centred(keep, steps)
    shared = count > 1

    def turn(source, carried):
        return product(carried.astype(BF16), coarse[...]) + rho[source].astype(F32)

    if shared:
        odd = at % 2 == 1
        error = rho[0].astype(F32)
        errors = []
        for item in range(count):
            following = turn(2 * item + 1, error)
            errors.append(jnp.where(odd, following, error))
            if item < count - 1:
                error = turn(2 * item + 2, following)
    else:
        first = jnp.where(at >= 2, rho[0].astype(F32), 0.0)
        errors = [lax.fori_loop(1, at - 1, turn, first)]
    kept = jnp.concatenate([error.astype(BF16) for error in errors], axis=0)
    current = jnp.concatenate(errors, axis=0)
    narrow = jnp.concatenate([narrow] * count, axis=1)
    clear_margins(field)
    for _ in range(steps):
        current = product3(stored_stencil(field, current, narrow), high_m[...], low_m[...])
    coarse_part = product(kept, coarse[...])
    mine = jnp.zeros((own + 2 * steps, current.shape[1]), F32)
    inner = lay.centred(keep, lay.fine)
    for i in range(count):
        swept = current[i * rows : (i + 1) * rows]
        here = (at - 2) // 2 == i if shared else True
        mine = mine + jnp.where(jnp.logical_and(here, at >= 2), swept[near], 0.0)
        change[i] = swept[inner] - coarse_part[i * rows : (i + 1) * rows][inner]
    before = rho[jnp.maximum(at - 1, 0)].astype(F32)[near]
    b = a_near[...] + jnp.where(at == 0, 0.0, before) + mine
    b_own[...] = b[lay.centred(steps, 0)]
    rows = own + 2 * steps
    passed[:rows], passed[rows : 2 * rows] = split(b)
    passed[2 * rows :] = rho_low[...]


def fourth_sweep(lay, change, weights, high_m, psi, field):
    steps = lay.steps
    count, rows, _ = change.shape
    narrow = weights[:, lay.centred(lay.wide, lay.fine)]
    narrow = jnp.concatenate([narrow] * count, axis=1)
    current = jnp.concatenate([change[i] for i in range(count)], axis=0)
    clear_margins(field)
    for _ in range(steps):
        current = product(stored_stencil(field, current, narrow).astype(BF16), high_m[...])
    for i in range(count):
        psi[i] = current[i * rows : (i + 1) * rows][lay.centred(lay.fine, steps)].astype(BF16)


def last_sweep(lay, place, psi, psi_other, passed, b_own, low, high, forcing, weights, start, high_m, low_m, coarse, out):
    steps, own = lay.steps, lay.own
    at = place[0]
    rows = own + 2 * steps
    narrow = weights[:, lay.centred(lay.wide, steps)]
    shared = psi_other is not None

    def source(block):
        if not shared:
            return psi[block].astype(F32)
        item = block // 2 - 1
        return jnp.where((block - at) % 2 == 0, psi[item].astype(F32), psi_other[item].astype(F32))

    def turn(block, carried):
        return product(carried.astype(BF16), coarse[...]) + source(block)

    error = lax.fori_loop(2, at - 1, turn, jnp.zeros((rows, start.shape[1]), F32))
    b_before = passed[:rows].astype(F32) + passed[rows : 2 * rows].astype(F32)
    initial = near_start(lay, low, start[...], high)
    current = jnp.where(at == 0, initial, b_before + error)
    mid = lay.centred(steps, 0)
    last = product(error[mid].astype(BF16), coarse[...])
    last = last + jnp.where(at >= 3, source(jnp.maximum(at - 1, 2))[mid], 0.0)
    last = last + passed[2 * rows :].astype(F32)
    out[steps - 1] = b_own[...] + jnp.where(at == 0, 0.0, last)
    for step in range(steps - 1):
        summed = stencil(current, narrow) + near_forcing(lay, low, forcing[step], high, step)
        current = product3(summed, high_m[...], low_m[...])
        out[step] = current[mid]


def last_sweep_gathered(lay, place, psi, *rest):
    last_sweep(lay, place, psi, None, *rest)


def in_vmem(value):
    return pltpu.with_memory_space_constraint(value, pltpu.VMEM)


def call(kernel, lay, outs, *operands, field=0):
    spaces = [pltpu.SMEM if o.dtype == jnp.int32 else pltpu.VMEM for o in operands]
    return pl.pallas_call(
        kernel if lay is None else functools.partial(kernel, lay),
        out_shape=outs,
        in_specs=[pl.BlockSpec(memory_space=space) for space in spaces],
        out_specs=jax.tree.map(lambda _: pl.BlockSpec(memory_space=pltpu.VMEM), outs),
        scratch_shapes=[pltpu.VMEM((field + 2 * MARGIN, operands[-1].shape[1]), F32)] if field else [],
        compiler_params=pltpu.CompilerParams(vmem_limit_bytes=LIMIT),
    )(*operands)


def call_from_hbm(kernel, outs, scratch, *operands):
    return pl.pallas_call(
        kernel,
        out_shape=outs,
        in_specs=[pl.BlockSpec(memory_space=pltpu.HBM)] * len(operands),
        out_specs=[pl.BlockSpec(memory_space=pltpu.VMEM)] * len(outs),
        scratch_shapes=scratch,
        compiler_params=pltpu.CompilerParams(vmem_limit_bytes=LIMIT),
    )(*(pltpu.with_memory_space_constraint(value, pltpu.HBM) for value in operands))


def per_device(initial_state, velocity, diffusion, forcing, implicit, coarse_implicit):
    own, columns = initial_state.shape
    steps = forcing.shape[0]
    blocks = lax.axis_size("tm")
    slabs = lax.axis_size("space")
    place = lax.axis_index("tm").astype(jnp.int32).reshape(1)
    lay = Layout(steps, own)
    near = own + 2 * steps

    def kept(*shape, dtype=F32):
        return pltpu.VMEM(shape, dtype)

    first_pack = kept(lay.first_rows, columns, dtype=BF16)
    head, tail = call_from_hbm(
        functools.partial(pack, lay),
        [first_pack] * 2,
        [
            pltpu.VMEM((own, columns), F32),
            pltpu.VMEM((2, steps, steps, columns), BF16),
            pltpu.SemaphoreType.DMA((1 + 2 * (steps + 3),)),
        ],
        velocity, diffusion, forcing, initial_state,
    )
    low = in_vmem(lax.ppermute(tail, "space", ring(slabs, 1)))
    high = in_vmem(lax.ppermute(head, "space", ring(slabs, -1)))
    high_m, low_m, coarse = call_from_hbm(
        split_matrices,
        [kept(*implicit.shape, dtype=BF16)] * 3,
        [pltpu.VMEM(implicit.shape, F32), pltpu.VMEM(implicit.shape, F32), pltpu.SemaphoreType.DMA((2,))],
        implicit, coarse_implicit,
    )
    high_m, low_m, coarse = in_vmem(high_m), in_vmem(low_m), in_vmem(coarse)
    second_pack = kept(lay.second_rows, columns, dtype=BF16)
    a, head, tail = call(
        inner_sweep,
        lay,
        [kept(own, columns), second_pack, second_pack],
        place, forcing, velocity, diffusion, initial_state, high_m, low_m,
    )
    far_low = in_vmem(lax.ppermute(tail, "space", ring(slabs, 1)))
    far_high = in_vmem(lax.ppermute(head, "space", ring(slabs, -1)))
    edges = call(
        edge_sweep,
        lay,
        kept(2 * lay.fine, columns),
        place, low, high, forcing, velocity, diffusion, initial_state, high_m, low_m,
    )
    rho, rho_low, a_near, weights = call(
        second_sweep,
        lay,
        [
            kept(own + 2 * lay.keep, columns, dtype=BF16),
            kept(own, columns, dtype=BF16),
            kept(near, columns),
            kept(3, own + 2 * lay.wide, columns),
        ],
        low, high, far_low, far_high, in_vmem(a), in_vmem(edges), velocity, diffusion, high_m, low_m,
        field=own + 2 * lay.wide,
    )
    weights = in_vmem(weights)
    rho_all = lax.all_gather(rho, "tm", axis=0)
    shared = blocks % 2 == 0 and 4 <= blocks <= 8
    count = (blocks - 2) // 2 if shared else 1
    change, passed, b_own = call(
        coarse_and_third,
        lay,
        [
            kept(count, own + 2 * lay.fine, columns),
            kept(2 * near + own, columns, dtype=BF16),
            kept(own, columns),
        ],
        place, rho_all, in_vmem(rho_low), in_vmem(a_near), weights, high_m, low_m, coarse,
        field=count * (own + 2 * lay.keep),
    )
    passed = lax.ppermute(passed, "tm", ring(blocks, 1))
    psi = call(
        fourth_sweep,
        lay,
        kept(count, near, columns, dtype=BF16),
        in_vmem(change), weights, high_m,
        field=count * (own + 2 * lay.fine),
    )
    if shared:
        psi_other = lax.ppermute(psi, "tm", [(i, i ^ 1) for i in range(blocks)])
        sources, kernel = (in_vmem(psi), in_vmem(psi_other)), last_sweep
    else:
        sources, kernel = (lax.all_gather(psi[0], "tm", axis=0),), last_sweep_gathered
    return call(
        kernel,
        lay,
        jax.ShapeDtypeStruct((steps, own, columns), F32),
        place, *sources, in_vmem(passed), in_vmem(b_own), low, high, forcing, weights, initial_state,
        high_m, low_m, coarse,
    )


def solution(mesh):
    in_specs = (
        P("space", None),
        P("space", None),
        P("space", None),
        P("tm", "space", None),
        P(),
        P(),
    )
    out_specs = P("tm", "space", None)
    return jax.shard_map(per_device, mesh=mesh, in_specs=in_specs, out_specs=out_specs, check_vma=False)
```

```python
import functools

import jax
import jax.numpy as jnp
from jax import lax
from jax.experimental import pallas as pl
from jax.experimental.pallas import tpu as pltpu
from jax.sharding import PartitionSpec as P


F32 = jnp.float32
BF16 = jnp.bfloat16
LIMIT = 16 << 20
MARGIN = 8


def ring(count, distance):
    return [(i, (i + distance) % count) for i in range(count)]


def split(value):
    high = value.astype(BF16)
    return high, (value - high.astype(F32)).astype(BF16)


def product(left, right):
    return jnp.dot(left, right, preferred_element_type=F32)


def product3(value, high_matrix, low_matrix):
    rows = value.shape[0]
    high, low = split(value)
    both = product(jnp.concatenate([high, low], axis=0), high_matrix)
    return both[:rows] + (both[rows:] + product(high, low_matrix))


def stencil(value, weights):
    west, centre, east = weights
    return centre * value + east * jnp.roll(value, -1, 0) + west * jnp.roll(value, 1, 0)


def stored_stencil(kept, value, weights):
    west, centre, east = weights
    rows = value.shape[0]
    kept[MARGIN : MARGIN + rows] = value
    return centre * value + east * kept[MARGIN + 1 : MARGIN + 1 + rows] + west * kept[MARGIN - 1 : MARGIN - 1 + rows]


def clear_margins(kept):
    rows = kept.shape[0]
    kept[:MARGIN] = jnp.zeros((MARGIN, kept.shape[1]), F32)
    kept[rows - MARGIN :] = jnp.zeros((MARGIN, kept.shape[1]), F32)


def turned(value, shift):
    return value if shift % value.shape[0] == 0 else jnp.roll(value, shift, 0)


class Layout:
    def __init__(self, steps, own):
        self.steps = steps
        self.own = own
        self.fine = 2 * steps
        self.keep = 3 * steps
        self.wide = 4 * steps
        self.groups = steps // 2
        self.half = steps - self.groups
        self.late_rows = self.groups * steps
        self.outer = self.half * steps
        self.velocity = self.outer + self.groups * steps
        self.diffusion = self.velocity + self.fine
        self.start = self.diffusion + self.fine
        self.start_low = self.start + self.fine
        self.first_rows = self.start_low + steps
        self.sent = self.wide - steps
        self.far_velocity = self.sent
        self.far_diffusion = self.far_velocity + self.wide - self.fine
        self.second_rows = self.far_diffusion + self.wide - self.fine

    def centred(self, width, inside):
        return slice(width - inside, width + self.own + inside)


def pack(
    lay, velocity, diffusion, forcing, start, head, tail, late_head, late_tail, start_kept, outer_kept, semaphores
):
    steps, own, fine = lay.steps, lay.own, lay.fine
    sides = ((head, late_head, 0, 0, steps), (tail, late_tail, own - fine, own - steps, own - fine))
    copies = [(start, start_kept)]
    for side, (out, late, first, inner, outer) in enumerate(sides):
        near = pl.ds(first, fine)
        copies.append((forcing.at[:, pl.ds(outer, steps)], outer_kept.at[side]))
        for step in range(steps):
            target, at = (out, step) if step < lay.half else (late, step - lay.half)
            copies.append((forcing.at[step, pl.ds(inner, steps)], target.at[pl.ds(at * steps, steps)]))
        copies.append((velocity.at[near], out.at[pl.ds(lay.velocity, fine)]))
        copies.append((diffusion.at[near], out.at[pl.ds(lay.diffusion, fine)]))
    copies = [pltpu.make_async_copy(*pair, semaphores.at[i]) for i, pair in enumerate(copies)]
    for copy in copies:
        copy.start()
    for copy in copies:
        copy.wait()
    for side, (out, _, first, _, _) in enumerate(sides):
        high, low = split(start_kept[first : first + fine])
        out[lay.start : lay.start_low] = high
        out[lay.start_low : lay.first_rows] = low[:steps] if side == 0 else low[fine - steps :]
        for group in range(lay.groups):
            one = outer_kept[side, group].astype(F32)
            other = outer_kept[side, steps - 1 - group].astype(F32)
            row = lax.broadcasted_iota(jnp.int32, one.shape, 0)
            if side == 0:
                both = jnp.where(row < steps - 1 - group, one, turned(other, -group))
            else:
                both = jnp.where(row > group, one, turned(other, group))
            at = lay.outer + group * steps
            out[at : at + steps] = both.astype(BF16)


def split_matrices(implicit, coarse_implicit, high_m, low_m, coarse, fine_kept, coarse_kept, semaphores):
    fine_copy = pltpu.make_async_copy(implicit, fine_kept, semaphores.at[0])
    coarse_copy = pltpu.make_async_copy(coarse_implicit, coarse_kept, semaphores.at[1])
    fine_copy.start()
    coarse_copy.start()
    fine_copy.wait()
    high_m[...], low_m[...] = split(fine_kept[...])
    coarse_copy.wait()
    coarse[...] = coarse_kept[...].astype(BF16)


def joined(low, own, high):
    return jnp.concatenate([low.astype(F32), own.astype(F32), high.astype(F32)], axis=0)


def inner_rows(lay, packed, late, step):
    source, at = (packed, step) if step < lay.half else (late, step - lay.half)
    return source[at * lay.steps : (at + 1) * lay.steps].astype(F32)


def start_rows(lay, packed, first):
    at = lay.start + first
    return packed[at : at + lay.steps].astype(F32) + packed[lay.start_low : lay.first_rows].astype(F32)


def make_weights(moving, spread):
    return spread + 0.5 * moving, 1.0 - 2.0 * spread, spread - 0.5 * moving


def inner_sweep(lay, place, forcing, velocity, diffusion, start, high_m, low_m, a, head, tail):
    steps, own = lay.steps, lay.own
    weights = make_weights(velocity[...].astype(F32), diffusion[...].astype(F32))
    current = jnp.where(place[0] == 0, start[...], 0.0)
    for step in range(steps):
        current = product3(stencil(current, weights) + forcing[step].astype(F32), high_m[...], low_m[...])
    a[...] = current
    for out, first, far in (
        (head, steps, slice(lay.fine, lay.wide)),
        (tail, own - steps - lay.sent, slice(own - lay.wide, own - lay.fine)),
    ):
        out[: lay.sent] = current[first : first + lay.sent].astype(BF16)
        out[lay.far_velocity : lay.far_diffusion] = velocity[far]
        out[lay.far_diffusion :] = diffusion[far]


def edge_windows(lay, before, ours, after):
    parts = (before, ours[: lay.fine], ours[lay.own - lay.fine :], after)
    return jnp.concatenate([part.astype(F32) for part in parts], axis=0)


def edge_steps(lay, current, steps_at, low, high, late_low, late_high, forcing, velocity, diffusion, high_m, low_m):
    steps, fine = lay.steps, lay.fine

    def packed(ours, at):
        return edge_windows(lay, low[at : at + fine], ours, high[at : at + fine])

    weights = make_weights(packed(velocity[...], lay.velocity), packed(diffusion[...], lay.diffusion))
    for step in steps_at:
        group = min(step, steps - 1 - step)
        at = lay.outer + group * steps
        before, after = low[at : at + steps].astype(F32), high[at : at + steps].astype(F32)
        if step > group:
            before, after = turned(before, -group), turned(after, group)
        source = edge_windows(
            lay,
            jnp.concatenate([before, inner_rows(lay, low, late_low, step)], axis=0),
            forcing[step],
            jnp.concatenate([inner_rows(lay, high, late_high, step), after], axis=0),
        )
        current = product3(stencil(current, weights) + source, high_m[...], low_m[...])
    return current


def early_edge_sweep(lay, place, low, high, forcing, velocity, diffusion, start, high_m, low_m, windows):
    steps, fine = lay.steps, lay.fine
    far = slice(lay.start, lay.start + steps)
    before = jnp.concatenate([low[far].astype(F32), start_rows(lay, low, fine - steps)], axis=0)
    far = slice(lay.start + fine - steps, lay.start + fine)
    after = jnp.concatenate([start_rows(lay, high, 0), high[far].astype(F32)], axis=0)
    current = edge_windows(lay, before, start[...], after)
    current = jnp.where(place[0] == 0, current, 0.0)
    operands = (low, high, None, None, forcing, velocity, diffusion, high_m, low_m)
    windows[...] = edge_steps(lay, current, range(lay.half), *operands)


def late_edge_sweep(
    lay, windows, low, high, late_low, late_high, forcing, velocity, diffusion, high_m, low_m, edges
):
    steps, fine = lay.steps, lay.fine
    operands = (low, high, late_low, late_high, forcing, velocity, diffusion, high_m, low_m)
    current = edge_steps(lay, windows[...], range(lay.half, steps), *operands)
    edges[:fine] = current[steps : steps + fine]
    edges[fine:] = current[3 * steps + fine : 3 * steps + 2 * fine]


def second_sweep(
    lay, low, high, far_low, far_high, a, edges, velocity, diffusion, high_m, low_m, rho, rho_low, a_near, weights, kept
):
    steps, fine, wide, own = lay.steps, lay.fine, lay.wide, lay.own

    def extended(ours, at, far):
        rows, far_rows = slice(at, at + fine), slice(far, far + wide - fine)
        return joined(
            jnp.concatenate([far_low[far_rows].astype(F32), low[rows].astype(F32)], axis=0),
            ours,
            jnp.concatenate([high[rows].astype(F32), far_high[far_rows].astype(F32)], axis=0),
        )

    weights[0], weights[1], weights[2] = make_weights(
        extended(velocity[...], lay.velocity, lay.far_velocity),
        extended(diffusion[...], lay.diffusion, lay.far_diffusion),
    )
    near = jnp.concatenate([edges[:fine], a[steps : own - steps], edges[fine:]], axis=0)
    a_near[...] = near
    current = joined(far_low[: lay.sent], near, far_high[: lay.sent])
    clear_margins(kept)
    for _ in range(steps):
        current = product3(stored_stencil(kept, current, weights[...]), high_m[...], low_m[...])
    high_part, low_part = split(current)
    rho[...] = high_part[lay.centred(wide, lay.keep)]
    rho_low[...] = low_part[lay.centred(wide, 0)]


def coarse_and_third(lay, place, rho, rho_low, a_near, weights, high_m, low_m, coarse, change, passed, b_own, field):
    keep, steps, own = lay.keep, lay.steps, lay.own
    rows = own + 2 * keep
    count = change.shape[0]
    at = place[0]
    narrow = weights[:, lay.centred(lay.wide, keep)]
    near = lay.centred(keep, steps)
    shared = count > 1

    def turn(source, carried):
        return product(carried.astype(BF16), coarse[...]) + rho[source].astype(F32)

    if shared:
        odd = at % 2 == 1
        error = rho[0].astype(F32)
        errors = []
        for item in range(count):
            following = turn(2 * item + 1, error)
            errors.append(jnp.where(odd, following, error))
            if item < count - 1:
                error = turn(2 * item + 2, following)
    else:
        first = jnp.where(at >= 2, rho[0].astype(F32), 0.0)
        errors = [lax.fori_loop(1, at - 1, turn, first)]
    kept = jnp.concatenate([error.astype(BF16) for error in errors], axis=0)
    current = jnp.concatenate(errors, axis=0)
    narrow = jnp.concatenate([narrow] * count, axis=1)
    clear_margins(field)
    for _ in range(steps):
        current = product3(stored_stencil(field, current, narrow), high_m[...], low_m[...])
    coarse_part = product(kept, coarse[...])
    mine = jnp.zeros((own + 2 * steps, current.shape[1]), F32)
    inner = lay.centred(keep, lay.fine)
    for i in range(count):
        swept = current[i * rows : (i + 1) * rows]
        here = (at - 2) // 2 == i if shared else True
        mine = mine + jnp.where(jnp.logical_and(here, at >= 2), swept[near], 0.0)
        change[i] = swept[inner] - coarse_part[i * rows : (i + 1) * rows][inner]
    before = rho[jnp.maximum(at - 1, 0)].astype(F32)[near]
    b = a_near[...] + jnp.where(at == 0, 0.0, before) + mine
    b_own[...] = b[lay.centred(steps, 0)]
    rows = own + 2 * steps
    passed[:rows], passed[rows : 2 * rows] = split(b)
    passed[2 * rows :] = rho_low[...]


def fourth_sweep(lay, change, weights, high_m, psi, field):
    steps = lay.steps
    count, rows, _ = change.shape
    narrow = weights[:, lay.centred(lay.wide, lay.fine)]
    narrow = jnp.concatenate([narrow] * count, axis=1)
    current = jnp.concatenate([change[i] for i in range(count)], axis=0)
    clear_margins(field)
    for _ in range(steps):
        current = product(stored_stencil(field, current, narrow).astype(BF16), high_m[...])
    for i in range(count):
        psi[i] = current[i * rows : (i + 1) * rows][lay.centred(lay.fine, steps)].astype(BF16)


def last_sweep(lay, place, psi, psi_other, passed, b_own, low, high, late_low, late_high, forcing, weights, start, high_m, low_m, coarse, out):
    steps, own = lay.steps, lay.own
    at = place[0]
    rows = own + 2 * steps
    narrow = weights[:, lay.centred(lay.wide, steps)]
    shared = psi_other is not None

    def source(block):
        if not shared:
            return psi[block].astype(F32)
        item = block // 2 - 1
        return jnp.where((block - at) % 2 == 0, psi[item].astype(F32), psi_other[item].astype(F32))

    def turn(block, carried):
        return product(carried.astype(BF16), coarse[...]) + source(block)

    error = lax.fori_loop(2, at - 1, turn, jnp.zeros((rows, start.shape[1]), F32))
    b_before = passed[:rows].astype(F32) + passed[rows : 2 * rows].astype(F32)
    initial = joined(start_rows(lay, low, lay.fine - steps), start[...], start_rows(lay, high, 0))
    current = jnp.where(at == 0, initial, b_before + error)
    mid = lay.centred(steps, 0)
    last = product(error[mid].astype(BF16), coarse[...])
    last = last + jnp.where(at >= 3, source(jnp.maximum(at - 1, 2))[mid], 0.0)
    last = last + passed[2 * rows :].astype(F32)
    out[steps - 1] = b_own[...] + jnp.where(at == 0, 0.0, last)
    for step in range(steps - 1):
        source = joined(inner_rows(lay, low, late_low, step), forcing[step], inner_rows(lay, high, late_high, step))
        summed = stencil(current, narrow) + source
        current = product3(summed, high_m[...], low_m[...])
        out[step] = current[mid]


def last_sweep_gathered(lay, place, psi, *rest):
    last_sweep(lay, place, psi, None, *rest)


def in_vmem(value):
    return pltpu.with_memory_space_constraint(value, pltpu.VMEM)


def call(kernel, lay, outs, *operands, field=0):
    spaces = [pltpu.SMEM if o.dtype == jnp.int32 else pltpu.VMEM for o in operands]
    return pl.pallas_call(
        kernel if lay is None else functools.partial(kernel, lay),
        out_shape=outs,
        in_specs=[pl.BlockSpec(memory_space=space) for space in spaces],
        out_specs=jax.tree.map(lambda _: pl.BlockSpec(memory_space=pltpu.VMEM), outs),
        scratch_shapes=[pltpu.VMEM((field + 2 * MARGIN, operands[-1].shape[1]), F32)] if field else [],
        compiler_params=pltpu.CompilerParams(vmem_limit_bytes=LIMIT),
    )(*operands)


def call_from_hbm(kernel, outs, scratch, *operands):
    return pl.pallas_call(
        kernel,
        out_shape=outs,
        in_specs=[pl.BlockSpec(memory_space=pltpu.HBM)] * len(operands),
        out_specs=[pl.BlockSpec(memory_space=pltpu.VMEM)] * len(outs),
        scratch_shapes=scratch,
        compiler_params=pltpu.CompilerParams(vmem_limit_bytes=LIMIT),
    )(*(pltpu.with_memory_space_constraint(value, pltpu.HBM) for value in operands))


def per_device(initial_state, velocity, diffusion, forcing, implicit, coarse_implicit):
    own, columns = initial_state.shape
    steps = forcing.shape[0]
    blocks = lax.axis_size("tm")
    slabs = lax.axis_size("space")
    place = lax.axis_index("tm").astype(jnp.int32).reshape(1)
    lay = Layout(steps, own)
    near = own + 2 * steps

    def kept(*shape, dtype=F32):
        return pltpu.VMEM(shape, dtype)

    first_pack = kept(lay.first_rows, columns, dtype=BF16)
    late_pack = kept(lay.late_rows, columns, dtype=BF16)
    head, tail, late_head, late_tail = call_from_hbm(
        functools.partial(pack, lay),
        [first_pack, first_pack, late_pack, late_pack],
        [
            pltpu.VMEM((own, columns), F32),
            pltpu.VMEM((2, steps, steps, columns), BF16),
            pltpu.SemaphoreType.DMA((1 + 2 * (steps + 3),)),
        ],
        velocity, diffusion, forcing, initial_state,
    )
    low = lax.ppermute(tail, "space", ring(slabs, 1))
    high = lax.ppermute(head, "space", ring(slabs, -1))
    late_low = lax.ppermute(late_tail, "space", ring(slabs, 1))
    late_high = lax.ppermute(late_head, "space", ring(slabs, -1))
    low, high, late_low, late_high = in_vmem(low), in_vmem(high), in_vmem(late_low), in_vmem(late_high)
    high_m, low_m, coarse = call_from_hbm(
        split_matrices,
        [kept(*implicit.shape, dtype=BF16)] * 3,
        [pltpu.VMEM(implicit.shape, F32), pltpu.VMEM(implicit.shape, F32), pltpu.SemaphoreType.DMA((2,))],
        implicit, coarse_implicit,
    )
    high_m, low_m, coarse = in_vmem(high_m), in_vmem(low_m), in_vmem(coarse)
    second_pack = kept(lay.second_rows, columns, dtype=BF16)
    a, head, tail = call(
        inner_sweep,
        lay,
        [kept(own, columns), second_pack, second_pack],
        place, forcing, velocity, diffusion, initial_state, high_m, low_m,
    )
    far_low = in_vmem(lax.ppermute(tail, "space", ring(slabs, 1)))
    far_high = in_vmem(lax.ppermute(head, "space", ring(slabs, -1)))
    windows = call(
        early_edge_sweep,
        lay,
        kept(4 * lay.fine, columns),
        place, low, high, forcing, velocity, diffusion, initial_state, high_m, low_m,
    )
    edges = call(
        late_edge_sweep,
        lay,
        kept(2 * lay.fine, columns),
        in_vmem(windows), low, high, late_low, late_high, forcing, velocity, diffusion, high_m, low_m,
    )
    rho, rho_low, a_near, weights = call(
        second_sweep,
        lay,
        [
            kept(own + 2 * lay.keep, columns, dtype=BF16),
            kept(own, columns, dtype=BF16),
            kept(near, columns),
            kept(3, own + 2 * lay.wide, columns),
        ],
        low, high, far_low, far_high, in_vmem(a), in_vmem(edges), velocity, diffusion, high_m, low_m,
        field=own + 2 * lay.wide,
    )
    weights = in_vmem(weights)
    rho_all = lax.all_gather(rho, "tm", axis=0)
    shared = blocks % 2 == 0 and 4 <= blocks <= 8
    count = (blocks - 2) // 2 if shared else 1
    change, passed, b_own = call(
        coarse_and_third,
        lay,
        [
            kept(count, own + 2 * lay.fine, columns),
            kept(2 * near + own, columns, dtype=BF16),
            kept(own, columns),
        ],
        place, rho_all, in_vmem(rho_low), in_vmem(a_near), weights, high_m, low_m, coarse,
        field=count * (own + 2 * lay.keep),
    )
    passed = lax.ppermute(passed, "tm", ring(blocks, 1))
    psi = call(
        fourth_sweep,
        lay,
        kept(count, near, columns, dtype=BF16),
        in_vmem(change), weights, high_m,
        field=count * (own + 2 * lay.fine),
    )
    if shared:
        psi_other = lax.ppermute(psi, "tm", [(i, i ^ 1) for i in range(blocks)])
        sources, kernel = (in_vmem(psi), in_vmem(psi_other)), last_sweep
    else:
        sources, kernel = (lax.all_gather(psi[0], "tm", axis=0),), last_sweep_gathered
    return call(
        kernel,
        lay,
        jax.ShapeDtypeStruct((steps, own, columns), F32),
        place, *sources, in_vmem(passed), in_vmem(b_own), low, high, late_low, late_high, forcing, weights, initial_state,
        high_m, low_m, coarse,
    )


def solution(mesh):
    in_specs = (
        P("space", None),
        P("space", None),
        P("space", None),
        P("tm", "space", None),
        P(),
        P(),
    )
    out_specs = P("tm", "space", None)
    return jax.shard_map(per_device, mesh=mesh, in_specs=in_specs, out_specs=out_specs, check_vma=False)
```

```python
import functools

import jax
import jax.numpy as jnp
from jax import lax
from jax.experimental import pallas as pl
from jax.experimental.pallas import tpu as pltpu
from jax.sharding import PartitionSpec as P


F32 = jnp.float32
BF16 = jnp.bfloat16
LIMIT = 16 << 20
MARGIN = 8


def ring(count, distance):
    return [(i, (i + distance) % count) for i in range(count)]


def split(value):
    high = value.astype(BF16)
    return high, (value - high.astype(F32)).astype(BF16)


def product(left, right):
    return jnp.dot(left, right, preferred_element_type=F32)


def product3(value, high_matrix, low_matrix):
    rows = value.shape[0]
    high, low = split(value)
    both = product(jnp.concatenate([high, low], axis=0), high_matrix)
    return both[:rows] + (both[rows:] + product(high, low_matrix))


def stencil(value, weights):
    west, centre, east = weights
    return centre * value + east * jnp.roll(value, -1, 0) + west * jnp.roll(value, 1, 0)


def stored_stencil(kept, value, weights):
    west, centre, east = weights
    rows = value.shape[0]
    kept[MARGIN : MARGIN + rows] = value
    return centre * value + east * kept[MARGIN + 1 : MARGIN + 1 + rows] + west * kept[MARGIN - 1 : MARGIN - 1 + rows]


def clear_margins(kept):
    rows = kept.shape[0]
    kept[:MARGIN] = jnp.zeros((MARGIN, kept.shape[1]), F32)
    kept[rows - MARGIN :] = jnp.zeros((MARGIN, kept.shape[1]), F32)


def turned(value, shift):
    return value if shift % value.shape[0] == 0 else jnp.roll(value, shift, 0)


class Layout:
    def __init__(self, steps, own):
        self.steps = steps
        self.own = own
        self.fine = 2 * steps
        self.keep = 3 * steps
        self.wide = 4 * steps
        self.groups = steps // 2
        self.outer = steps * steps
        self.velocity = self.outer + self.groups * steps
        self.diffusion = self.velocity + self.fine
        self.start = self.diffusion + self.fine
        self.start_low = self.start + self.fine
        self.first_rows = self.start_low + steps
        self.sent = self.wide - steps
        self.far_velocity = self.sent
        self.far_diffusion = self.far_velocity + self.wide - self.fine
        self.second_rows = self.far_diffusion + self.wide - self.fine

    def centred(self, width, inside):
        return slice(width - inside, width + self.own + inside)


def pack(lay, velocity, diffusion, forcing, start, head, tail, start_kept, outer_kept, semaphores):
    steps, own, fine = lay.steps, lay.own, lay.fine
    sides = ((head, 0, 0, steps), (tail, own - fine, own - steps, own - fine))
    copies = [(start, start_kept)]
    for side, (out, first, inner, outer) in enumerate(sides):
        near = pl.ds(first, fine)
        copies.append((forcing.at[:, pl.ds(outer, steps)], outer_kept.at[side]))
        for step in range(steps):
            copies.append((forcing.at[step, pl.ds(inner, steps)], out.at[pl.ds(step * steps, steps)]))
        copies.append((velocity.at[near], out.at[pl.ds(lay.velocity, fine)]))
        copies.append((diffusion.at[near], out.at[pl.ds(lay.diffusion, fine)]))
    copies = [pltpu.make_async_copy(*pair, semaphores.at[i]) for i, pair in enumerate(copies)]
    for copy in copies:
        copy.start()
    for copy in copies:
        copy.wait()
    for side, (out, first, _, _) in enumerate(sides):
        high, low = split(start_kept[first : first + fine])
        out[lay.start : lay.start_low] = high
        out[lay.start_low : lay.first_rows] = low[:steps] if side == 0 else low[fine - steps :]
        for group in range(lay.groups):
            one = outer_kept[side, group].astype(F32)
            other = outer_kept[side, steps - 1 - group].astype(F32)
            row = lax.broadcasted_iota(jnp.int32, one.shape, 0)
            if side == 0:
                both = jnp.where(row < steps - 1 - group, one, turned(other, -group))
            else:
                both = jnp.where(row > group, one, turned(other, group))
            at = lay.outer + group * steps
            out[at : at + steps] = both.astype(BF16)


def split_matrices(implicit, coarse_implicit, high_m, low_m, coarse, fine_kept, coarse_kept, semaphores):
    fine_copy = pltpu.make_async_copy(implicit, fine_kept, semaphores.at[0])
    coarse_copy = pltpu.make_async_copy(coarse_implicit, coarse_kept, semaphores.at[1])
    fine_copy.start()
    coarse_copy.start()
    fine_copy.wait()
    high_m[...], low_m[...] = split(fine_kept[...])
    coarse_copy.wait()
    coarse[...] = coarse_kept[...].astype(BF16)


def joined(low, own, high):
    return jnp.concatenate([low.astype(F32), own.astype(F32), high.astype(F32)], axis=0)


def near_forcing(lay, low, own, high, step):
    rows = slice(step * lay.steps, (step + 1) * lay.steps)
    return joined(low[rows], own, high[rows])


def start_rows(lay, packed, first):
    at = lay.start + first
    return packed[at : at + lay.steps].astype(F32) + packed[lay.start_low : lay.first_rows].astype(F32)


def make_weights(moving, spread):
    return spread + 0.5 * moving, 1.0 - 2.0 * spread, spread - 0.5 * moving


def inner_sweep(lay, place, forcing, velocity, diffusion, start, high_m, low_m, a, head, tail):
    steps, own = lay.steps, lay.own
    weights = make_weights(velocity[...].astype(F32), diffusion[...].astype(F32))
    current = jnp.where(place[0] == 0, start[...], 0.0)
    for step in range(steps):
        current = product3(stencil(current, weights) + forcing[step].astype(F32), high_m[...], low_m[...])
    a[...] = current
    for out, first, far in (
        (head, steps, slice(lay.fine, lay.wide)),
        (tail, own - steps - lay.sent, slice(own - lay.wide, own - lay.fine)),
    ):
        out[: lay.sent] = current[first : first + lay.sent].astype(BF16)
        out[lay.far_velocity : lay.far_diffusion] = velocity[far]
        out[lay.far_diffusion :] = diffusion[far]


def edge_sweep(lay, place, low, high, forcing, velocity, diffusion, start, high_m, low_m, edges):
    steps, own, fine = lay.steps, lay.own, lay.fine

    def windows(before, ours, after):
        return jnp.concatenate(
            [part.astype(F32) for part in (before, ours[:fine], ours[own - fine :], after)], axis=0
        )

    def packed(ours, at):
        return windows(low[at : at + fine], ours, high[at : at + fine])

    weights = make_weights(packed(velocity[...], lay.velocity), packed(diffusion[...], lay.diffusion))
    far_before = low[lay.start : lay.start + steps].astype(F32)
    far_after = high[lay.start + fine - steps : lay.start + fine].astype(F32)
    current = windows(
        jnp.concatenate([far_before, start_rows(lay, low, fine - steps)], axis=0),
        start[...],
        jnp.concatenate([start_rows(lay, high, 0), far_after], axis=0),
    )
    current = jnp.where(place[0] == 0, current, 0.0)
    for step in range(steps):
        rows = slice(step * steps, (step + 1) * steps)
        group = min(step, steps - 1 - step)
        at = lay.outer + group * steps
        before, after = low[at : at + steps].astype(F32), high[at : at + steps].astype(F32)
        if step > group:
            before, after = turned(before, -group), turned(after, group)
        source = windows(
            jnp.concatenate([before, low[rows].astype(F32)], axis=0),
            forcing[step],
            jnp.concatenate([high[rows].astype(F32), after], axis=0),
        )
        current = product3(stencil(current, weights) + source, high_m[...], low_m[...])
    edges[:fine] = current[steps : steps + fine]
    edges[fine:] = current[3 * steps + fine : 3 * steps + 2 * fine]


def second_sweep(
    lay, low, high, far_low, far_high, a, edges, velocity, diffusion, high_m, low_m, rho, rho_low, a_near, weights, kept
):
    steps, fine, wide, own = lay.steps, lay.fine, lay.wide, lay.own

    def extended(ours, at, far):
        rows, far_rows = slice(at, at + fine), slice(far, far + wide - fine)
        return joined(
            jnp.concatenate([far_low[far_rows].astype(F32), low[rows].astype(F32)], axis=0),
            ours,
            jnp.concatenate([high[rows].astype(F32), far_high[far_rows].astype(F32)], axis=0),
        )

    weights[0], weights[1], weights[2] = make_weights(
        extended(velocity[...], lay.velocity, lay.far_velocity),
        extended(diffusion[...], lay.diffusion, lay.far_diffusion),
    )
    near = jnp.concatenate([edges[:fine], a[steps : own - steps], edges[fine:]], axis=0)
    a_near[...] = near
    current = joined(far_low[: lay.sent], near, far_high[: lay.sent])
    clear_margins(kept)
    for _ in range(steps):
        current = product3(stored_stencil(kept, current, weights[...]), high_m[...], low_m[...])
    high_part, low_part = split(current)
    rho[...] = high_part[lay.centred(wide, lay.keep)]
    rho_low[...] = low_part[lay.centred(wide, 0)]


def coarse_and_third(lay, place, rho, rho_low, a_near, weights, high_m, low_m, coarse, change, passed, b_own, field):
    keep, steps, own = lay.keep, lay.steps, lay.own
    rows = own + 2 * keep
    count = change.shape[0]
    at = place[0]
    narrow = weights[:, lay.centred(lay.wide, keep)]
    near = lay.centred(keep, steps)
    shared = count > 1

    def turn(source, carried):
        return product(carried.astype(BF16), coarse[...]) + rho[source].astype(F32)

    if shared:
        odd = at % 2 == 1
        error = rho[0].astype(F32)
        errors = []
        for item in range(count):
            following = turn(2 * item + 1, error)
            errors.append(jnp.where(odd, following, error))
            if item < count - 1:
                error = turn(2 * item + 2, following)
    else:
        first = jnp.where(at >= 2, rho[0].astype(F32), 0.0)
        errors = [lax.fori_loop(1, at - 1, turn, first)]
    kept = jnp.concatenate([error.astype(BF16) for error in errors], axis=0)
    current = jnp.concatenate(errors, axis=0)
    narrow = jnp.concatenate([narrow] * count, axis=1)
    clear_margins(field)
    for _ in range(steps):
        current = product3(stored_stencil(field, current, narrow), high_m[...], low_m[...])
    coarse_part = product(kept, coarse[...])
    mine = jnp.zeros((own + 2 * steps, current.shape[1]), F32)
    inner = lay.centred(keep, lay.fine)
    for i in range(count):
        swept = current[i * rows : (i + 1) * rows]
        here = (at - 2) // 2 == i if shared else True
        mine = mine + jnp.where(jnp.logical_and(here, at >= 2), swept[near], 0.0)
        change[i] = swept[inner] - coarse_part[i * rows : (i + 1) * rows][inner]
    before = rho[jnp.maximum(at - 1, 0)].astype(F32)[near]
    b = a_near[...] + jnp.where(at == 0, 0.0, before) + mine
    b_own[...] = b[lay.centred(steps, 0)]
    rows = own + 2 * steps
    passed[:rows], passed[rows : 2 * rows] = split(b)
    passed[2 * rows :] = rho_low[...]


def fourth_sweep(lay, change, weights, high_m, psi, field):
    steps = lay.steps
    count, rows, _ = change.shape
    narrow = weights[:, lay.centred(lay.wide, lay.fine)]
    narrow = jnp.concatenate([narrow] * count, axis=1)
    current = jnp.concatenate([change[i] for i in range(count)], axis=0)
    clear_margins(field)
    for _ in range(steps):
        current = product(stored_stencil(field, current, narrow).astype(BF16), high_m[...])
    for i in range(count):
        psi[i] = current[i * rows : (i + 1) * rows][lay.centred(lay.fine, steps)].astype(BF16)


def last_sweep(lay, place, psi, psi_other, passed, b_own, low, high, forcing, weights, start, high_m, low_m, coarse, out, out_kept, semaphores):
    steps, own = lay.steps, lay.own
    at = place[0]
    rows = own + 2 * steps
    narrow = weights[:, lay.centred(lay.wide, steps)]
    shared = psi_other is not None

    def source(block):
        if not shared:
            return psi[block].astype(F32)
        item = block // 2 - 1
        return jnp.where((block - at) % 2 == 0, psi[item].astype(F32), psi_other[item].astype(F32))

    def turn(block, carried):
        return product(carried.astype(BF16), coarse[...]) + source(block)

    error = lax.fori_loop(2, at - 1, turn, jnp.zeros((rows, start.shape[1]), F32))
    b_before = passed[:rows].astype(F32) + passed[rows : 2 * rows].astype(F32)
    initial = joined(start_rows(lay, low, lay.fine - steps), start[...], start_rows(lay, high, 0))
    current = jnp.where(at == 0, initial, b_before + error)
    mid = lay.centred(steps, 0)
    last = product(error[mid].astype(BF16), coarse[...])
    last = last + jnp.where(at >= 3, source(jnp.maximum(at - 1, 2))[mid], 0.0)
    last = last + passed[2 * rows :].astype(F32)
    copies = [pltpu.make_async_copy(out_kept.at[step], out.at[step], semaphores.at[step]) for step in range(steps)]
    out_kept[steps - 1] = b_own[...] + jnp.where(at == 0, 0.0, last)
    copies[steps - 1].start()
    for step in range(steps - 1):
        summed = stencil(current, narrow) + near_forcing(lay, low, forcing[step], high, step)
        current = product3(summed, high_m[...], low_m[...])
        out_kept[step] = current[mid]
        copies[step].start()
    for copy in copies:
        copy.wait()


def last_sweep_gathered(lay, place, psi, *rest):
    last_sweep(lay, place, psi, None, *rest)


def in_vmem(value):
    return pltpu.with_memory_space_constraint(value, pltpu.VMEM)


def call(kernel, lay, outs, *operands, field=0):
    spaces = [pltpu.SMEM if o.dtype == jnp.int32 else pltpu.VMEM for o in operands]
    return pl.pallas_call(
        kernel if lay is None else functools.partial(kernel, lay),
        out_shape=outs,
        in_specs=[pl.BlockSpec(memory_space=space) for space in spaces],
        out_specs=jax.tree.map(lambda _: pl.BlockSpec(memory_space=pltpu.VMEM), outs),
        scratch_shapes=[pltpu.VMEM((field + 2 * MARGIN, operands[-1].shape[1]), F32)] if field else [],
        compiler_params=pltpu.CompilerParams(vmem_limit_bytes=LIMIT),
    )(*operands)


def call_from_hbm(kernel, outs, scratch, *operands):
    return pl.pallas_call(
        kernel,
        out_shape=outs,
        in_specs=[pl.BlockSpec(memory_space=pltpu.HBM)] * len(operands),
        out_specs=[pl.BlockSpec(memory_space=pltpu.VMEM)] * len(outs),
        scratch_shapes=scratch,
        compiler_params=pltpu.CompilerParams(vmem_limit_bytes=LIMIT),
    )(*(pltpu.with_memory_space_constraint(value, pltpu.HBM) for value in operands))


def per_device(initial_state, velocity, diffusion, forcing, implicit, coarse_implicit):
    own, columns = initial_state.shape
    steps = forcing.shape[0]
    blocks = lax.axis_size("tm")
    slabs = lax.axis_size("space")
    place = lax.axis_index("tm").astype(jnp.int32).reshape(1)
    lay = Layout(steps, own)
    near = own + 2 * steps

    def kept(*shape, dtype=F32):
        return pltpu.VMEM(shape, dtype)

    first_pack = kept(lay.first_rows, columns, dtype=BF16)
    head, tail = call_from_hbm(
        functools.partial(pack, lay),
        [first_pack] * 2,
        [
            pltpu.VMEM((own, columns), F32),
            pltpu.VMEM((2, steps, steps, columns), BF16),
            pltpu.SemaphoreType.DMA((1 + 2 * (steps + 3),)),
        ],
        velocity, diffusion, forcing, initial_state,
    )
    low = in_vmem(lax.ppermute(tail, "space", ring(slabs, 1)))
    high = in_vmem(lax.ppermute(head, "space", ring(slabs, -1)))
    high_m, low_m, coarse = call_from_hbm(
        split_matrices,
        [kept(*implicit.shape, dtype=BF16)] * 3,
        [pltpu.VMEM(implicit.shape, F32), pltpu.VMEM(implicit.shape, F32), pltpu.SemaphoreType.DMA((2,))],
        implicit, coarse_implicit,
    )
    high_m, low_m, coarse = in_vmem(high_m), in_vmem(low_m), in_vmem(coarse)
    second_pack = kept(lay.second_rows, columns, dtype=BF16)
    a, head, tail = call(
        inner_sweep,
        lay,
        [kept(own, columns), second_pack, second_pack],
        place, forcing, velocity, diffusion, initial_state, high_m, low_m,
    )
    far_low = in_vmem(lax.ppermute(tail, "space", ring(slabs, 1)))
    far_high = in_vmem(lax.ppermute(head, "space", ring(slabs, -1)))
    edges = call(
        edge_sweep,
        lay,
        kept(2 * lay.fine, columns),
        place, low, high, forcing, velocity, diffusion, initial_state, high_m, low_m,
    )
    rho, rho_low, a_near, weights = call(
        second_sweep,
        lay,
        [
            kept(own + 2 * lay.keep, columns, dtype=BF16),
            kept(own, columns, dtype=BF16),
            kept(near, columns),
            kept(3, own + 2 * lay.wide, columns),
        ],
        low, high, far_low, far_high, in_vmem(a), in_vmem(edges), velocity, diffusion, high_m, low_m,
        field=own + 2 * lay.wide,
    )
    weights = in_vmem(weights)
    rho_all = lax.all_gather(rho, "tm", axis=0)
    shared = blocks % 2 == 0 and 4 <= blocks <= 8
    count = (blocks - 2) // 2 if shared else 1
    change, passed, b_own = call(
        coarse_and_third,
        lay,
        [
            kept(count, own + 2 * lay.fine, columns),
            kept(2 * near + own, columns, dtype=BF16),
            kept(own, columns),
        ],
        place, rho_all, in_vmem(rho_low), in_vmem(a_near), weights, high_m, low_m, coarse,
        field=count * (own + 2 * lay.keep),
    )
    passed = lax.ppermute(passed, "tm", ring(blocks, 1))
    psi = call(
        fourth_sweep,
        lay,
        kept(count, near, columns, dtype=BF16),
        in_vmem(change), weights, high_m,
        field=count * (own + 2 * lay.fine),
    )
    if shared:
        psi_other = lax.ppermute(psi, "tm", [(i, i ^ 1) for i in range(blocks)])
        sources, kernel = (in_vmem(psi), in_vmem(psi_other)), last_sweep
    else:
        sources, kernel = (lax.all_gather(psi[0], "tm", axis=0),), last_sweep_gathered
    operands = (
        place, *sources, in_vmem(passed), in_vmem(b_own), low, high, forcing, weights, initial_state,
        high_m, low_m, coarse,
    )
    return pl.pallas_call(
        functools.partial(kernel, lay),
        out_shape=jax.ShapeDtypeStruct((steps, own, columns), F32),
        in_specs=[pl.BlockSpec(memory_space=pltpu.SMEM)]
        + [pl.BlockSpec(memory_space=pltpu.VMEM)] * (len(operands) - 1),
        out_specs=pl.BlockSpec(memory_space=pltpu.HBM),
        scratch_shapes=[pltpu.VMEM((steps, own, columns), F32), pltpu.SemaphoreType.DMA((steps,))],
        compiler_params=pltpu.CompilerParams(vmem_limit_bytes=LIMIT),
        name="last_sweep",
    )(*operands)


def solution(mesh):
    in_specs = (
        P("space", None),
        P("space", None),
        P("space", None),
        P("tm", "space", None),
        P(),
        P(),
    )
    out_specs = P("tm", "space", None)
    return jax.shard_map(per_device, mesh=mesh, in_specs=in_specs, out_specs=out_specs, check_vma=False)
```

```python
import functools

import jax
import jax.numpy as jnp
from jax import lax
from jax.experimental import pallas as pl
from jax.experimental.pallas import tpu as pltpu
from jax.sharding import PartitionSpec as P


F32 = jnp.float32
BF16 = jnp.bfloat16
LIMIT = 16 << 20
MARGIN = 8


def ring(count, distance):
    return [(i, (i + distance) % count) for i in range(count)]


def split(value):
    high = value.astype(BF16)
    return high, (value - high.astype(F32)).astype(BF16)


def product(left, right):
    return jnp.dot(left, right, preferred_element_type=F32)


def product3(value, high_matrix, low_matrix):
    rows = value.shape[0]
    high, low = split(value)
    both = product(jnp.concatenate([high, low], axis=0), high_matrix)
    return both[:rows] + (both[rows:] + product(high, low_matrix))


def stencil(value, weights):
    west, centre, east = weights
    return centre * value + east * jnp.roll(value, -1, 0) + west * jnp.roll(value, 1, 0)


def stored_stencil(kept, value, weights):
    west, centre, east = weights
    rows = value.shape[0]
    kept[MARGIN : MARGIN + rows] = value
    return centre * value + east * kept[MARGIN + 1 : MARGIN + 1 + rows] + west * kept[MARGIN - 1 : MARGIN - 1 + rows]


def clear_margins(kept):
    rows = kept.shape[0]
    kept[:MARGIN] = jnp.zeros((MARGIN, kept.shape[1]), F32)
    kept[rows - MARGIN :] = jnp.zeros((MARGIN, kept.shape[1]), F32)


def turned(value, shift):
    return value if shift % value.shape[0] == 0 else jnp.roll(value, shift, 0)


class Layout:
    def __init__(self, steps, own):
        self.steps = steps
        self.own = own
        self.fine = 2 * steps
        self.keep = 3 * steps
        self.wide = 4 * steps
        self.groups = steps // 2
        self.outer = steps * steps
        self.velocity = self.outer + self.groups * steps
        self.diffusion = self.velocity + self.fine
        self.start = self.diffusion + self.fine
        self.start_low = self.start + self.fine
        self.first_rows = self.start_low + steps
        self.sent = self.wide - steps
        self.far_velocity = self.sent
        self.far_diffusion = self.far_velocity + self.wide - self.fine
        self.second_rows = self.far_diffusion + self.wide - self.fine

    def centred(self, width, inside):
        return slice(width - inside, width + self.own + inside)


def pack(lay, velocity, diffusion, forcing, start, head, tail, start_kept, outer_kept, semaphores):
    steps, own, fine = lay.steps, lay.own, lay.fine
    sides = ((head, 0, 0, steps), (tail, own - fine, own - steps, own - fine))
    copies = [(start, start_kept)]
    for side, (out, first, inner, outer) in enumerate(sides):
        near = pl.ds(first, fine)
        copies.append((forcing.at[:, pl.ds(outer, steps)], outer_kept.at[side]))
        target = out.at[pl.ds(0, steps * steps)].reshape(steps, steps, out.shape[1])
        copies.append((forcing.at[:, pl.ds(inner, steps)], target))
        copies.append((velocity.at[near], out.at[pl.ds(lay.velocity, fine)]))
        copies.append((diffusion.at[near], out.at[pl.ds(lay.diffusion, fine)]))
    copies = [pltpu.make_async_copy(*pair, semaphores.at[i]) for i, pair in enumerate(copies)]
    for copy in copies:
        copy.start()
    for copy in copies:
        copy.wait()
    for side, (out, first, _, _) in enumerate(sides):
        high, low = split(start_kept[first : first + fine])
        out[lay.start : lay.start_low] = high
        out[lay.start_low : lay.first_rows] = low[:steps] if side == 0 else low[fine - steps :]
        for group in range(lay.groups):
            one = outer_kept[side, group].astype(F32)
            other = outer_kept[side, steps - 1 - group].astype(F32)
            row = lax.broadcasted_iota(jnp.int32, one.shape, 0)
            if side == 0:
                both = jnp.where(row < steps - 1 - group, one, turned(other, -group))
            else:
                both = jnp.where(row > group, one, turned(other, group))
            at = lay.outer + group * steps
            out[at : at + steps] = both.astype(BF16)


def split_matrices(implicit, coarse_implicit, high_m, low_m, coarse, fine_kept, coarse_kept, semaphores):
    fine_copy = pltpu.make_async_copy(implicit, fine_kept, semaphores.at[0])
    coarse_copy = pltpu.make_async_copy(coarse_implicit, coarse_kept, semaphores.at[1])
    fine_copy.start()
    coarse_copy.start()
    fine_copy.wait()
    high_m[...], low_m[...] = split(fine_kept[...])
    coarse_copy.wait()
    coarse[...] = coarse_kept[...].astype(BF16)


def joined(low, own, high):
    return jnp.concatenate([low.astype(F32), own.astype(F32), high.astype(F32)], axis=0)


def near_forcing(lay, low, own, high, step):
    rows = slice(step * lay.steps, (step + 1) * lay.steps)
    return joined(low[rows], own, high[rows])


def start_rows(lay, packed, first):
    at = lay.start + first
    return packed[at : at + lay.steps].astype(F32) + packed[lay.start_low : lay.first_rows].astype(F32)


def make_weights(moving, spread):
    return spread + 0.5 * moving, 1.0 - 2.0 * spread, spread - 0.5 * moving


def inner_sweep(lay, place, forcing, velocity, diffusion, start, high_m, low_m, a, head, tail):
    steps, own = lay.steps, lay.own
    weights = make_weights(velocity[...].astype(F32), diffusion[...].astype(F32))
    current = jnp.where(place[0] == 0, start[...], 0.0)
    for step in range(steps):
        current = product3(stencil(current, weights) + forcing[step].astype(F32), high_m[...], low_m[...])
    a[...] = current
    for out, first, far in (
        (head, steps, slice(lay.fine, lay.wide)),
        (tail, own - steps - lay.sent, slice(own - lay.wide, own - lay.fine)),
    ):
        out[: lay.sent] = current[first : first + lay.sent].astype(BF16)
        out[lay.far_velocity : lay.far_diffusion] = velocity[far]
        out[lay.far_diffusion :] = diffusion[far]


def edge_sweep(lay, place, low, high, forcing, velocity, diffusion, start, high_m, low_m, edges):
    steps, own, fine = lay.steps, lay.own, lay.fine

    def windows(before, ours, after):
        return jnp.concatenate(
            [part.astype(F32) for part in (before, ours[:fine], ours[own - fine :], after)], axis=0
        )

    def packed(ours, at):
        return windows(low[at : at + fine], ours, high[at : at + fine])

    weights = make_weights(packed(velocity[...], lay.velocity), packed(diffusion[...], lay.diffusion))
    far_before = low[lay.start : lay.start + steps].astype(F32)
    far_after = high[lay.start + fine - steps : lay.start + fine].astype(F32)
    current = windows(
        jnp.concatenate([far_before, start_rows(lay, low, fine - steps)], axis=0),
        start[...],
        jnp.concatenate([start_rows(lay, high, 0), far_after], axis=0),
    )
    current = jnp.where(place[0] == 0, current, 0.0)
    for step in range(steps):
        rows = slice(step * steps, (step + 1) * steps)
        group = min(step, steps - 1 - step)
        at = lay.outer + group * steps
        before, after = low[at : at + steps].astype(F32), high[at : at + steps].astype(F32)
        if step > group:
            before, after = turned(before, -group), turned(after, group)
        source = windows(
            jnp.concatenate([before, low[rows].astype(F32)], axis=0),
            forcing[step],
            jnp.concatenate([high[rows].astype(F32), after], axis=0),
        )
        current = product3(stencil(current, weights) + source, high_m[...], low_m[...])
    edges[:fine] = current[steps : steps + fine]
    edges[fine:] = current[3 * steps + fine : 3 * steps + 2 * fine]


def second_sweep(
    lay, low, high, far_low, far_high, a, edges, velocity, diffusion, high_m, low_m, rho, rho_low, a_near, weights, kept
):
    steps, fine, wide, own = lay.steps, lay.fine, lay.wide, lay.own

    def extended(ours, at, far):
        rows, far_rows = slice(at, at + fine), slice(far, far + wide - fine)
        return joined(
            jnp.concatenate([far_low[far_rows].astype(F32), low[rows].astype(F32)], axis=0),
            ours,
            jnp.concatenate([high[rows].astype(F32), far_high[far_rows].astype(F32)], axis=0),
        )

    weights[0], weights[1], weights[2] = make_weights(
        extended(velocity[...], lay.velocity, lay.far_velocity),
        extended(diffusion[...], lay.diffusion, lay.far_diffusion),
    )
    near = jnp.concatenate([edges[:fine], a[steps : own - steps], edges[fine:]], axis=0)
    a_near[...] = near
    current = joined(far_low[: lay.sent], near, far_high[: lay.sent])
    clear_margins(kept)
    for _ in range(steps):
        current = product3(stored_stencil(kept, current, weights[...]), high_m[...], low_m[...])
    high_part, low_part = split(current)
    rho[...] = high_part[lay.centred(wide, lay.keep)]
    rho_low[...] = low_part[lay.centred(wide, 0)]


def coarse_and_third(lay, place, rho, rho_low, a_near, weights, high_m, low_m, coarse, change, passed, b_own, field):
    keep, steps, own = lay.keep, lay.steps, lay.own
    rows = own + 2 * keep
    count = change.shape[0]
    at = place[0]
    narrow = weights[:, lay.centred(lay.wide, keep)]
    near = lay.centred(keep, steps)
    shared = count > 1

    def turn(source, carried):
        return product(carried.astype(BF16), coarse[...]) + rho[source].astype(F32)

    if shared:
        odd = at % 2 == 1
        error = rho[0].astype(F32)
        errors = []
        for item in range(count):
            following = turn(2 * item + 1, error)
            errors.append(jnp.where(odd, following, error))
            if item < count - 1:
                error = turn(2 * item + 2, following)
    else:
        first = jnp.where(at >= 2, rho[0].astype(F32), 0.0)
        errors = [lax.fori_loop(1, at - 1, turn, first)]
    kept = jnp.concatenate([error.astype(BF16) for error in errors], axis=0)
    current = jnp.concatenate(errors, axis=0)
    narrow = jnp.concatenate([narrow] * count, axis=1)
    clear_margins(field)
    for _ in range(steps):
        current = product3(stored_stencil(field, current, narrow), high_m[...], low_m[...])
    coarse_part = product(kept, coarse[...])
    mine = jnp.zeros((own + 2 * steps, current.shape[1]), F32)
    inner = lay.centred(keep, lay.fine)
    for i in range(count):
        swept = current[i * rows : (i + 1) * rows]
        here = (at - 2) // 2 == i if shared else True
        mine = mine + jnp.where(jnp.logical_and(here, at >= 2), swept[near], 0.0)
        change[i] = swept[inner] - coarse_part[i * rows : (i + 1) * rows][inner]
    before = rho[jnp.maximum(at - 1, 0)].astype(F32)[near]
    b = a_near[...] + jnp.where(at == 0, 0.0, before) + mine
    b_own[...] = b[lay.centred(steps, 0)]
    rows = own + 2 * steps
    passed[:rows], passed[rows : 2 * rows] = split(b)
    passed[2 * rows :] = rho_low[...]


def fourth_sweep(lay, change, weights, high_m, psi, field):
    steps = lay.steps
    count, rows, _ = change.shape
    narrow = weights[:, lay.centred(lay.wide, lay.fine)]
    narrow = jnp.concatenate([narrow] * count, axis=1)
    current = jnp.concatenate([change[i] for i in range(count)], axis=0)
    clear_margins(field)
    for _ in range(steps):
        current = product(stored_stencil(field, current, narrow).astype(BF16), high_m[...])
    for i in range(count):
        psi[i] = current[i * rows : (i + 1) * rows][lay.centred(lay.fine, steps)].astype(BF16)


def last_sweep(lay, place, psi, psi_other, passed, b_own, low, high, forcing, weights, start, high_m, low_m, coarse, out, out_kept, semaphores):
    steps, own = lay.steps, lay.own
    at = place[0]
    rows = own + 2 * steps
    narrow = weights[:, lay.centred(lay.wide, steps)]
    shared = psi_other is not None

    def source(block):
        if not shared:
            return psi[block].astype(F32)
        item = block // 2 - 1
        return jnp.where((block - at) % 2 == 0, psi[item].astype(F32), psi_other[item].astype(F32))

    def turn(block, carried):
        return product(carried.astype(BF16), coarse[...]) + source(block)

    error = lax.fori_loop(2, at - 1, turn, jnp.zeros((rows, start.shape[1]), F32))
    b_before = passed[:rows].astype(F32) + passed[rows : 2 * rows].astype(F32)
    initial = joined(start_rows(lay, low, lay.fine - steps), start[...], start_rows(lay, high, 0))
    current = jnp.where(at == 0, initial, b_before + error)
    mid = lay.centred(steps, 0)
    last = product(error[mid].astype(BF16), coarse[...])
    last = last + jnp.where(at >= 3, source(jnp.maximum(at - 1, 2))[mid], 0.0)
    last = last + passed[2 * rows :].astype(F32)
    copies = [pltpu.make_async_copy(out_kept.at[step], out.at[step], semaphores.at[step]) for step in range(steps)]
    out_kept[steps - 1] = b_own[...] + jnp.where(at == 0, 0.0, last)
    copies[steps - 1].start()
    for step in range(steps - 1):
        summed = stencil(current, narrow) + near_forcing(lay, low, forcing[step], high, step)
        current = product3(summed, high_m[...], low_m[...])
        out_kept[step] = current[mid]
        copies[step].start()
    for copy in copies:
        copy.wait()


def last_sweep_gathered(lay, place, psi, *rest):
    last_sweep(lay, place, psi, None, *rest)


def in_vmem(value):
    return pltpu.with_memory_space_constraint(value, pltpu.VMEM)


def call(kernel, lay, outs, *operands, field=0):
    spaces = [pltpu.SMEM if o.dtype == jnp.int32 else pltpu.VMEM for o in operands]
    return pl.pallas_call(
        kernel if lay is None else functools.partial(kernel, lay),
        out_shape=outs,
        in_specs=[pl.BlockSpec(memory_space=space) for space in spaces],
        out_specs=jax.tree.map(lambda _: pl.BlockSpec(memory_space=pltpu.VMEM), outs),
        scratch_shapes=[pltpu.VMEM((field + 2 * MARGIN, operands[-1].shape[1]), F32)] if field else [],
        compiler_params=pltpu.CompilerParams(vmem_limit_bytes=LIMIT),
    )(*operands)


def call_from_hbm(kernel, outs, scratch, *operands):
    return pl.pallas_call(
        kernel,
        out_shape=outs,
        in_specs=[pl.BlockSpec(memory_space=pltpu.HBM)] * len(operands),
        out_specs=[pl.BlockSpec(memory_space=pltpu.VMEM)] * len(outs),
        scratch_shapes=scratch,
        compiler_params=pltpu.CompilerParams(vmem_limit_bytes=LIMIT),
    )(*(pltpu.with_memory_space_constraint(value, pltpu.HBM) for value in operands))


def per_device(initial_state, velocity, diffusion, forcing, implicit, coarse_implicit):
    own, columns = initial_state.shape
    steps = forcing.shape[0]
    blocks = lax.axis_size("tm")
    slabs = lax.axis_size("space")
    place = lax.axis_index("tm").astype(jnp.int32).reshape(1)
    lay = Layout(steps, own)
    near = own + 2 * steps

    def kept(*shape, dtype=F32):
        return pltpu.VMEM(shape, dtype)

    first_pack = kept(lay.first_rows, columns, dtype=BF16)
    head, tail = call_from_hbm(
        functools.partial(pack, lay),
        [first_pack] * 2,
        [
            pltpu.VMEM((own, columns), F32),
            pltpu.VMEM((2, steps, steps, columns), BF16),
            pltpu.SemaphoreType.DMA((1 + 2 * 4,)),
        ],
        velocity, diffusion, forcing, initial_state,
    )
    low = in_vmem(lax.ppermute(tail, "space", ring(slabs, 1)))
    high = in_vmem(lax.ppermute(head, "space", ring(slabs, -1)))
    high_m, low_m, coarse = call_from_hbm(
        split_matrices,
        [kept(*implicit.shape, dtype=BF16)] * 3,
        [pltpu.VMEM(implicit.shape, F32), pltpu.VMEM(implicit.shape, F32), pltpu.SemaphoreType.DMA((2,))],
        implicit, coarse_implicit,
    )
    high_m, low_m, coarse = in_vmem(high_m), in_vmem(low_m), in_vmem(coarse)
    second_pack = kept(lay.second_rows, columns, dtype=BF16)
    a, head, tail = call(
        inner_sweep,
        lay,
        [kept(own, columns), second_pack, second_pack],
        place, forcing, velocity, diffusion, initial_state, high_m, low_m,
    )
    far_low = in_vmem(lax.ppermute(tail, "space", ring(slabs, 1)))
    far_high = in_vmem(lax.ppermute(head, "space", ring(slabs, -1)))
    edges = call(
        edge_sweep,
        lay,
        kept(2 * lay.fine, columns),
        place, low, high, forcing, velocity, diffusion, initial_state, high_m, low_m,
    )
    rho, rho_low, a_near, weights = call(
        second_sweep,
        lay,
        [
            kept(own + 2 * lay.keep, columns, dtype=BF16),
            kept(own, columns, dtype=BF16),
            kept(near, columns),
            kept(3, own + 2 * lay.wide, columns),
        ],
        low, high, far_low, far_high, in_vmem(a), in_vmem(edges), velocity, diffusion, high_m, low_m,
        field=own + 2 * lay.wide,
    )
    weights = in_vmem(weights)
    rho_all = lax.all_gather(rho, "tm", axis=0)
    shared = blocks % 2 == 0 and 4 <= blocks <= 8
    count = (blocks - 2) // 2 if shared else 1
    change, passed, b_own = call(
        coarse_and_third,
        lay,
        [
            kept(count, own + 2 * lay.fine, columns),
            kept(2 * near + own, columns, dtype=BF16),
            kept(own, columns),
        ],
        place, rho_all, in_vmem(rho_low), in_vmem(a_near), weights, high_m, low_m, coarse,
        field=count * (own + 2 * lay.keep),
    )
    passed = lax.ppermute(passed, "tm", ring(blocks, 1)[:-1])
    psi = call(
        fourth_sweep,
        lay,
        kept(count, near, columns, dtype=BF16),
        in_vmem(change), weights, high_m,
        field=count * (own + 2 * lay.fine),
    )
    if shared:
        psi_other = lax.ppermute(psi, "tm", [(i, i ^ 1) for i in range(blocks)])
        sources, kernel = (in_vmem(psi), in_vmem(psi_other)), last_sweep
    else:
        sources, kernel = (lax.all_gather(psi[0], "tm", axis=0),), last_sweep_gathered
    operands = (
        place, *sources, in_vmem(passed), in_vmem(b_own), low, high, forcing, weights, initial_state,
        high_m, low_m, coarse,
    )
    return pl.pallas_call(
        functools.partial(kernel, lay),
        out_shape=jax.ShapeDtypeStruct((steps, own, columns), F32),
        in_specs=[pl.BlockSpec(memory_space=pltpu.SMEM)]
        + [pl.BlockSpec(memory_space=pltpu.VMEM)] * (len(operands) - 1),
        out_specs=pl.BlockSpec(memory_space=pltpu.HBM),
        scratch_shapes=[pltpu.VMEM((steps, own, columns), F32), pltpu.SemaphoreType.DMA((steps,))],
        compiler_params=pltpu.CompilerParams(vmem_limit_bytes=LIMIT),
        name="last_sweep",
    )(*operands)


def solution(mesh):
    in_specs = (
        P("space", None),
        P("space", None),
        P("space", None),
        P("tm", "space", None),
        P(),
        P(),
    )
    out_specs = P("tm", "space", None)
    return jax.shard_map(per_device, mesh=mesh, in_specs=in_specs, out_specs=out_specs, check_vma=False)
```

```python
import functools

import jax
import jax.numpy as jnp
from jax import lax
from jax.experimental import pallas as pl
from jax.experimental.pallas import tpu as pltpu
from jax.sharding import PartitionSpec as P


F32 = jnp.float32
BF16 = jnp.bfloat16
LIMIT = 16 << 20
MARGIN = 8


def ring(count, distance):
    return [(i, (i + distance) % count) for i in range(count)]


def split(value):
    high = value.astype(BF16)
    return high, (value - high.astype(F32)).astype(BF16)


def product(left, right):
    return jnp.dot(left, right, preferred_element_type=F32)


def product3(value, high_matrix, low_matrix):
    rows = value.shape[0]
    high, low = split(value)
    both = product(jnp.concatenate([high, low], axis=0), high_matrix)
    return both[:rows] + (both[rows:] + product(high, low_matrix))


def stencil(value, weights):
    west, centre, east = weights
    return centre * value + east * jnp.roll(value, -1, 0) + west * jnp.roll(value, 1, 0)


def stored_stencil(kept, value, weights):
    west, centre, east = weights
    rows = value.shape[0]
    kept[MARGIN : MARGIN + rows] = value
    return centre * value + east * kept[MARGIN + 1 : MARGIN + 1 + rows] + west * kept[MARGIN - 1 : MARGIN - 1 + rows]


def clear_margins(kept):
    rows = kept.shape[0]
    kept[:MARGIN] = jnp.zeros((MARGIN, kept.shape[1]), F32)
    kept[rows - MARGIN :] = jnp.zeros((MARGIN, kept.shape[1]), F32)


def turned(value, shift):
    return value if shift % value.shape[0] == 0 else jnp.roll(value, shift, 0)


class Layout:
    def __init__(self, steps, own):
        self.steps = steps
        self.own = own
        self.fine = 2 * steps
        self.keep = 3 * steps
        self.wide = 4 * steps
        self.groups = steps // 2
        self.outer = steps * steps
        self.velocity = self.outer + self.groups * steps
        self.diffusion = self.velocity + self.fine
        self.start = self.diffusion + self.fine
        self.start_low = self.start + self.fine
        self.first_rows = self.start_low + steps
        self.sent = self.wide - steps
        self.far_velocity = self.sent
        self.far_diffusion = self.far_velocity + self.wide - self.fine
        self.second_rows = self.far_diffusion + self.wide - self.fine

    def centred(self, width, inside):
        return slice(width - inside, width + self.own + inside)


def pack(lay, velocity, diffusion, forcing, start, head, tail, start_kept, outer_kept, semaphores):
    steps, own, fine = lay.steps, lay.own, lay.fine
    sides = ((head, 0, 0, steps), (tail, own - fine, own - steps, own - fine))
    copies = [(start, start_kept)]
    for side, (out, first, inner, outer) in enumerate(sides):
        near = pl.ds(first, fine)
        copies.append((forcing.at[:, pl.ds(outer, steps)], outer_kept.at[side]))
        for step in range(steps):
            copies.append((forcing.at[step, pl.ds(inner, steps)], out.at[pl.ds(step * steps, steps)]))
        copies.append((velocity.at[near], out.at[pl.ds(lay.velocity, fine)]))
        copies.append((diffusion.at[near], out.at[pl.ds(lay.diffusion, fine)]))
    copies = [pltpu.make_async_copy(*pair, semaphores.at[i]) for i, pair in enumerate(copies)]
    for copy in copies:
        copy.start()
    for copy in copies:
        copy.wait()
    for side, (out, first, _, _) in enumerate(sides):
        high, low = split(start_kept[first : first + fine])
        out[lay.start : lay.start_low] = high
        out[lay.start_low : lay.first_rows] = low[:steps] if side == 0 else low[fine - steps :]
        for group in range(lay.groups):
            one = outer_kept[side, group].astype(F32)
            other = outer_kept[side, steps - 1 - group].astype(F32)
            row = lax.broadcasted_iota(jnp.int32, one.shape, 0)
            if side == 0:
                both = jnp.where(row < steps - 1 - group, one, turned(other, -group))
            else:
                both = jnp.where(row > group, one, turned(other, group))
            at = lay.outer + group * steps
            out[at : at + steps] = both.astype(BF16)


def split_matrices(implicit, coarse_implicit, high_m, low_m, coarse, fine_kept, coarse_kept, semaphores):
    fine_copy = pltpu.make_async_copy(implicit, fine_kept, semaphores.at[0])
    coarse_copy = pltpu.make_async_copy(coarse_implicit, coarse_kept, semaphores.at[1])
    fine_copy.start()
    coarse_copy.start()
    fine_copy.wait()
    high_m[...], low_m[...] = split(fine_kept[...])
    coarse_copy.wait()
    coarse[...] = coarse_kept[...].astype(BF16)


def joined(low, own, high):
    return jnp.concatenate([low.astype(F32), own.astype(F32), high.astype(F32)], axis=0)


def near_forcing(lay, low, own, high, step):
    rows = slice(step * lay.steps, (step + 1) * lay.steps)
    return joined(low[rows], own, high[rows])


def start_rows(lay, packed, first):
    at = lay.start + first
    return packed[at : at + lay.steps].astype(F32) + packed[lay.start_low : lay.first_rows].astype(F32)


def make_weights(moving, spread):
    return spread + 0.5 * moving, 1.0 - 2.0 * spread, spread - 0.5 * moving


def inner_sweep(lay, place, forcing, velocity, diffusion, start, high_m, low_m, a, head, tail):
    steps, own = lay.steps, lay.own
    weights = make_weights(velocity[...].astype(F32), diffusion[...].astype(F32))
    current = jnp.where(place[0] == 0, start[...], 0.0)
    for step in range(steps):
        current = product3(stencil(current, weights) + forcing[step].astype(F32), high_m[...], low_m[...])
    a[...] = current
    for out, first, far in (
        (head, steps, slice(lay.fine, lay.wide)),
        (tail, own - steps - lay.sent, slice(own - lay.wide, own - lay.fine)),
    ):
        out[: lay.sent] = current[first : first + lay.sent].astype(BF16)
        out[lay.far_velocity : lay.far_diffusion] = velocity[far]
        out[lay.far_diffusion :] = diffusion[far]


def edge_sweep(lay, place, low, high, forcing, velocity, diffusion, start, high_m, low_m, edges):
    steps, own, fine = lay.steps, lay.own, lay.fine

    def windows(before, ours, after):
        return jnp.concatenate(
            [part.astype(F32) for part in (before, ours[:fine], ours[own - fine :], after)], axis=0
        )

    def packed(ours, at):
        return windows(low[at : at + fine], ours, high[at : at + fine])

    weights = make_weights(packed(velocity[...], lay.velocity), packed(diffusion[...], lay.diffusion))
    far_before = low[lay.start : lay.start + steps].astype(F32)
    far_after = high[lay.start + fine - steps : lay.start + fine].astype(F32)
    current = windows(
        jnp.concatenate([far_before, start_rows(lay, low, fine - steps)], axis=0),
        start[...],
        jnp.concatenate([start_rows(lay, high, 0), far_after], axis=0),
    )
    current = jnp.where(place[0] == 0, current, 0.0)
    for step in range(steps):
        rows = slice(step * steps, (step + 1) * steps)
        group = min(step, steps - 1 - step)
        at = lay.outer + group * steps
        before, after = low[at : at + steps].astype(F32), high[at : at + steps].astype(F32)
        if step > group:
            before, after = turned(before, -group), turned(after, group)
        source = windows(
            jnp.concatenate([before, low[rows].astype(F32)], axis=0),
            forcing[step],
            jnp.concatenate([high[rows].astype(F32), after], axis=0),
        )
        current = product3(stencil(current, weights) + source, high_m[...], low_m[...])
    edges[:fine] = current[steps : steps + fine]
    edges[fine:] = current[3 * steps + fine : 3 * steps + 2 * fine]


def second_sweep(
    lay, low, high, far_low, far_high, a, edges, velocity, diffusion, high_m, low_m, rho, rho_low, a_near, weights, kept
):
    steps, fine, wide, own = lay.steps, lay.fine, lay.wide, lay.own

    def extended(ours, at, far):
        rows, far_rows = slice(at, at + fine), slice(far, far + wide - fine)
        return joined(
            jnp.concatenate([far_low[far_rows].astype(F32), low[rows].astype(F32)], axis=0),
            ours,
            jnp.concatenate([high[rows].astype(F32), far_high[far_rows].astype(F32)], axis=0),
        )

    weights[0], weights[1], weights[2] = make_weights(
        extended(velocity[...], lay.velocity, lay.far_velocity),
        extended(diffusion[...], lay.diffusion, lay.far_diffusion),
    )
    near = jnp.concatenate([edges[:fine], a[steps : own - steps], edges[fine:]], axis=0)
    a_near[...] = near
    current = joined(far_low[: lay.sent], near, far_high[: lay.sent])
    clear_margins(kept)
    for _ in range(steps):
        current = product3(stored_stencil(kept, current, weights[...]), high_m[...], low_m[...])
    high_part, low_part = split(current)
    rho[...] = high_part[lay.centred(wide, lay.keep)]
    rho_low[...] = low_part[lay.centred(wide, 0)]


def coarse_and_third(lay, place, rho, rho_low, a_near, weights, high_m, low_m, coarse, change, passed, b_own, field):
    keep, steps, own = lay.keep, lay.steps, lay.own
    rows = own + 2 * keep
    count = change.shape[0]
    at = place[0]
    narrow = weights[:, lay.centred(lay.wide, keep)]
    near = lay.centred(keep, steps)
    shared = count > 1

    def turn(source, carried):
        return product(carried.astype(BF16), coarse[...]) + rho[source].astype(F32)

    if shared:
        odd = at % 2 == 1
        error = rho[0].astype(F32)
        errors = []
        for item in range(count):
            following = turn(2 * item + 1, error)
            errors.append(jnp.where(odd, following, error))
            if item < count - 1:
                error = turn(2 * item + 2, following)
    else:
        first = jnp.where(at >= 2, rho[0].astype(F32), 0.0)
        errors = [lax.fori_loop(1, at - 1, turn, first)]
    kept = jnp.concatenate([error.astype(BF16) for error in errors], axis=0)
    current = jnp.concatenate(errors, axis=0)
    narrow = jnp.concatenate([narrow] * count, axis=1)
    clear_margins(field)
    for _ in range(steps):
        current = product3(stored_stencil(field, current, narrow), high_m[...], low_m[...])
    coarse_part = product(kept, coarse[...])
    mine = jnp.zeros((own + 2 * steps, current.shape[1]), F32)
    inner = lay.centred(keep, lay.fine)
    for i in range(count):
        swept = current[i * rows : (i + 1) * rows]
        here = (at - 2) // 2 == i if shared else True
        mine = mine + jnp.where(jnp.logical_and(here, at >= 2), swept[near], 0.0)
        change[i] = swept[inner] - coarse_part[i * rows : (i + 1) * rows][inner]
    before = rho[jnp.maximum(at - 1, 0)].astype(F32)[near]
    b = a_near[...] + jnp.where(at == 0, 0.0, before) + mine
    b_own[...] = b[lay.centred(steps, 0)]
    rows = own + 2 * steps
    passed[:rows], passed[rows : 2 * rows] = split(b)
    passed[2 * rows :] = rho_low[...]


def fourth_sweep(lay, change, weights, high_m, psi, field):
    steps = lay.steps
    count, rows, _ = change.shape
    narrow = weights[:, lay.centred(lay.wide, lay.fine)]
    narrow = jnp.concatenate([narrow] * count, axis=1)
    current = jnp.concatenate([change[i] for i in range(count)], axis=0)
    clear_margins(field)
    for _ in range(steps):
        current = product(stored_stencil(field, current, narrow).astype(BF16), high_m[...])
    for i in range(count):
        psi[i] = current[i * rows : (i + 1) * rows][lay.centred(lay.fine, steps)].astype(BF16)


def last_sweep(lay, place, psi, psi_other, passed, b_own, low, high, forcing, weights, start, high_m, low_m, coarse, out, out_kept, semaphores):
    steps, own = lay.steps, lay.own
    at = place[0]
    rows = own + 2 * steps
    narrow = weights[:, lay.centred(lay.wide, steps)]
    shared = psi_other is not None

    def source(block):
        if not shared:
            return psi[block].astype(F32)
        item = block // 2 - 1
        return jnp.where((block - at) % 2 == 0, psi[item].astype(F32), psi_other[item].astype(F32))

    def turn(block, carried):
        return product(carried.astype(BF16), coarse[...]) + source(block)

    error = lax.fori_loop(2, at - 1, turn, jnp.zeros((rows, start.shape[1]), F32))
    b_before = passed[:rows].astype(F32) + passed[rows : 2 * rows].astype(F32)
    initial = joined(start_rows(lay, low, lay.fine - steps), start[...], start_rows(lay, high, 0))
    current = jnp.where(at == 0, initial, b_before + error)
    mid = lay.centred(steps, 0)
    last = product(error[mid].astype(BF16), coarse[...])
    last = last + jnp.where(at >= 3, source(jnp.maximum(at - 1, 2))[mid], 0.0)
    last = last + passed[2 * rows :].astype(F32)
    copies = [pltpu.make_async_copy(out_kept.at[step], out.at[step], semaphores.at[step]) for step in range(steps)]
    out_kept[steps - 1] = b_own[...] + jnp.where(at == 0, 0.0, last)
    copies[steps - 1].start()
    for step in range(steps - 1):
        summed = stencil(current, narrow) + near_forcing(lay, low, forcing[step], high, step)
        current = product3(summed, high_m[...], low_m[...])
        out_kept[step] = current[mid]
        copies[step].start()
    for copy in copies:
        copy.wait()


def last_sweep_gathered(lay, place, psi, *rest):
    last_sweep(lay, place, psi, None, *rest)


def in_vmem(value):
    return pltpu.with_memory_space_constraint(value, pltpu.VMEM)


def call(kernel, lay, outs, *operands, field=0):
    spaces = [pltpu.SMEM if o.dtype == jnp.int32 else pltpu.VMEM for o in operands]
    return pl.pallas_call(
        kernel if lay is None else functools.partial(kernel, lay),
        out_shape=outs,
        in_specs=[pl.BlockSpec(memory_space=space) for space in spaces],
        out_specs=jax.tree.map(lambda _: pl.BlockSpec(memory_space=pltpu.VMEM), outs),
        scratch_shapes=[pltpu.VMEM((field + 2 * MARGIN, operands[-1].shape[1]), F32)] if field else [],
        compiler_params=pltpu.CompilerParams(vmem_limit_bytes=LIMIT),
    )(*operands)


def call_from_hbm(kernel, outs, scratch, *operands):
    return pl.pallas_call(
        kernel,
        out_shape=outs,
        in_specs=[pl.BlockSpec(memory_space=pltpu.HBM)] * len(operands),
        out_specs=[pl.BlockSpec(memory_space=pltpu.VMEM)] * len(outs),
        scratch_shapes=scratch,
        compiler_params=pltpu.CompilerParams(vmem_limit_bytes=LIMIT),
    )(*(pltpu.with_memory_space_constraint(value, pltpu.HBM) for value in operands))


def per_device(initial_state, velocity, diffusion, forcing, implicit, coarse_implicit):
    own, columns = initial_state.shape
    steps = forcing.shape[0]
    blocks = lax.axis_size("tm")
    slabs = lax.axis_size("space")
    place = lax.axis_index("tm").astype(jnp.int32).reshape(1)
    lay = Layout(steps, own)
    near = own + 2 * steps

    def kept(*shape, dtype=F32):
        return pltpu.VMEM(shape, dtype)

    first_pack = kept(lay.first_rows, columns, dtype=BF16)
    head, tail = call_from_hbm(
        functools.partial(pack, lay),
        [first_pack] * 2,
        [
            pltpu.VMEM((own, columns), F32),
            pltpu.VMEM((2, steps, steps, columns), BF16),
            pltpu.SemaphoreType.DMA((1 + 2 * (steps + 3),)),
        ],
        velocity, diffusion, forcing, initial_state,
    )
    low = in_vmem(lax.ppermute(tail, "space", ring(slabs, 1)))
    high = in_vmem(lax.ppermute(head, "space", ring(slabs, -1)))
    high_m, low_m, coarse = call_from_hbm(
        split_matrices,
        [kept(*implicit.shape, dtype=BF16)] * 3,
        [pltpu.VMEM(implicit.shape, F32), pltpu.VMEM(implicit.shape, F32), pltpu.SemaphoreType.DMA((2,))],
        implicit, coarse_implicit,
    )
    high_m, low_m, coarse = in_vmem(high_m), in_vmem(low_m), in_vmem(coarse)
    second_pack = kept(lay.second_rows, columns, dtype=BF16)
    a, head, tail = call(
        inner_sweep,
        lay,
        [kept(own, columns), second_pack, second_pack],
        place, forcing, velocity, diffusion, initial_state, high_m, low_m,
    )
    far_low = lax.ppermute(tail, "space", ring(slabs, 1))
    far_high = lax.ppermute(head, "space", ring(slabs, -1))
    far_low, far_high = in_vmem(far_low), in_vmem(far_high)
    edges = call(
        edge_sweep,
        lay,
        kept(2 * lay.fine, columns),
        place, low, high, forcing, velocity, diffusion, initial_state, high_m, low_m,
    )
    rho, rho_low, a_near, weights = call(
        second_sweep,
        lay,
        [
            kept(own + 2 * lay.keep, columns, dtype=BF16),
            kept(own, columns, dtype=BF16),
            kept(near, columns),
            kept(3, own + 2 * lay.wide, columns),
        ],
        low, high, far_low, far_high, in_vmem(a), in_vmem(edges), velocity, diffusion, high_m, low_m,
        field=own + 2 * lay.wide,
    )
    weights = in_vmem(weights)
    rho_all = lax.all_gather(rho, "tm", axis=0)
    shared = blocks % 2 == 0 and 4 <= blocks <= 8
    count = (blocks - 2) // 2 if shared else 1
    change, passed, b_own = call(
        coarse_and_third,
        lay,
        [
            kept(count, own + 2 * lay.fine, columns),
            kept(2 * near + own, columns, dtype=BF16),
            kept(own, columns),
        ],
        place, rho_all, in_vmem(rho_low), in_vmem(a_near), weights, high_m, low_m, coarse,
        field=count * (own + 2 * lay.keep),
    )
    passed = lax.ppermute(passed, "tm", ring(blocks, 1))
    psi = call(
        fourth_sweep,
        lay,
        kept(count, near, columns, dtype=BF16),
        in_vmem(change), weights, high_m,
        field=count * (own + 2 * lay.fine),
    )
    if shared:
        psi_other = lax.ppermute(psi, "tm", [(i, i ^ 1) for i in range(blocks)])
        sources, kernel = (in_vmem(psi), in_vmem(psi_other)), last_sweep
    else:
        sources, kernel = (lax.all_gather(psi[0], "tm", axis=0),), last_sweep_gathered
    operands = (
        place, *sources, in_vmem(passed), in_vmem(b_own), low, high, forcing, weights, initial_state,
        high_m, low_m, coarse,
    )
    return pl.pallas_call(
        functools.partial(kernel, lay),
        out_shape=jax.ShapeDtypeStruct((steps, own, columns), F32),
        in_specs=[pl.BlockSpec(memory_space=pltpu.SMEM)]
        + [pl.BlockSpec(memory_space=pltpu.VMEM)] * (len(operands) - 1),
        out_specs=pl.BlockSpec(memory_space=pltpu.HBM),
        scratch_shapes=[pltpu.VMEM((steps, own, columns), F32), pltpu.SemaphoreType.DMA((steps,))],
        compiler_params=pltpu.CompilerParams(vmem_limit_bytes=LIMIT),
        name="last_sweep",
    )(*operands)


def solution(mesh):
    in_specs = (
        P("space", None),
        P("space", None),
        P("space", None),
        P("tm", "space", None),
        P(),
        P(),
    )
    out_specs = P("tm", "space", None)
    return jax.shard_map(per_device, mesh=mesh, in_specs=in_specs, out_specs=out_specs, check_vma=False)
```

```python
import functools

import jax
import jax.numpy as jnp
from jax import lax
from jax.experimental import pallas as pl
from jax.experimental.pallas import tpu as pltpu
from jax.sharding import PartitionSpec as P


F32 = jnp.float32
BF16 = jnp.bfloat16
LIMIT = 16 << 20
MARGIN = 8


def ring(count, distance):
    return [(i, (i + distance) % count) for i in range(count)]


def split(value):
    high = value.astype(BF16)
    return high, (value - high.astype(F32)).astype(BF16)


def product(left, right):
    return jnp.dot(left, right, preferred_element_type=F32)


def product3(value, high_matrix, low_matrix):
    rows = value.shape[0]
    high, low = split(value)
    both = product(jnp.concatenate([high, low], axis=0), high_matrix)
    return both[:rows] + (both[rows:] + product(high, low_matrix))


def stencil(value, weights):
    west, centre, east = weights
    return centre * value + east * jnp.roll(value, -1, 0) + west * jnp.roll(value, 1, 0)


def stored_stencil(kept, value, weights):
    west, centre, east = weights
    rows = value.shape[0]
    kept[MARGIN : MARGIN + rows] = value
    return centre * value + east * kept[MARGIN + 1 : MARGIN + 1 + rows] + west * kept[MARGIN - 1 : MARGIN - 1 + rows]


def clear_margins(kept):
    rows = kept.shape[0]
    kept[:MARGIN] = jnp.zeros((MARGIN, kept.shape[1]), F32)
    kept[rows - MARGIN :] = jnp.zeros((MARGIN, kept.shape[1]), F32)


def turned(value, shift):
    return value if shift % value.shape[0] == 0 else jnp.roll(value, shift, 0)


class Layout:
    def __init__(self, steps, own):
        self.steps = steps
        self.own = own
        self.fine = 2 * steps
        self.keep = 3 * steps
        self.wide = 4 * steps
        self.groups = steps // 2
        self.outer = steps * steps
        self.velocity = self.outer + self.groups * steps
        self.diffusion = self.velocity + self.fine
        self.start = self.diffusion + self.fine
        self.start_low = self.start + self.fine
        self.first_rows = self.start_low + steps
        self.sent = self.wide - steps
        self.far_velocity = self.sent
        self.far_diffusion = self.far_velocity + self.wide - self.fine
        self.second_rows = self.far_diffusion + self.wide - self.fine

    def centred(self, width, inside):
        return slice(width - inside, width + self.own + inside)


def pack(lay, velocity, diffusion, forcing, start, head, tail, start_kept, outer_kept, semaphores):
    steps, own, fine = lay.steps, lay.own, lay.fine
    sides = ((head, 0, 0, steps), (tail, own - fine, own - steps, own - fine))
    copies = [(start, start_kept)]
    for side, (out, first, inner, outer) in enumerate(sides):
        near = pl.ds(first, fine)
        copies.append((forcing.at[:, pl.ds(outer, steps)], outer_kept.at[side]))
        for step in range(steps):
            copies.append((forcing.at[step, pl.ds(inner, steps)], out.at[pl.ds(step * steps, steps)]))
        copies.append((velocity.at[near], out.at[pl.ds(lay.velocity, fine)]))
        copies.append((diffusion.at[near], out.at[pl.ds(lay.diffusion, fine)]))
    copies = [pltpu.make_async_copy(*pair, semaphores.at[i]) for i, pair in enumerate(copies)]
    for copy in copies:
        copy.start()
    for copy in copies:
        copy.wait()
    for side, (out, first, _, _) in enumerate(sides):
        high, low = split(start_kept[first : first + fine])
        out[lay.start : lay.start_low] = high
        out[lay.start_low : lay.first_rows] = low[:steps] if side == 0 else low[fine - steps :]
        for group in range(lay.groups):
            one = outer_kept[side, group].astype(F32)
            other = outer_kept[side, steps - 1 - group].astype(F32)
            row = lax.broadcasted_iota(jnp.int32, one.shape, 0)
            if side == 0:
                both = jnp.where(row < steps - 1 - group, one, turned(other, -group))
            else:
                both = jnp.where(row > group, one, turned(other, group))
            at = lay.outer + group * steps
            out[at : at + steps] = both.astype(BF16)


def split_matrices(implicit, coarse_implicit, high_m, low_m, coarse, fine_kept, coarse_kept, semaphores):
    fine_copy = pltpu.make_async_copy(implicit, fine_kept, semaphores.at[0])
    coarse_copy = pltpu.make_async_copy(coarse_implicit, coarse_kept, semaphores.at[1])
    fine_copy.start()
    coarse_copy.start()
    fine_copy.wait()
    high_m[...], low_m[...] = split(fine_kept[...])
    coarse_copy.wait()
    coarse[...] = coarse_kept[...].astype(BF16)


def joined(low, own, high):
    return jnp.concatenate([low.astype(F32), own.astype(F32), high.astype(F32)], axis=0)


def near_forcing(lay, low, own, high, step):
    rows = slice(step * lay.steps, (step + 1) * lay.steps)
    return joined(low[rows], own, high[rows])


def start_rows(lay, packed, first):
    at = lay.start + first
    return packed[at : at + lay.steps].astype(F32) + packed[lay.start_low : lay.first_rows].astype(F32)


def make_weights(moving, spread):
    return spread + 0.5 * moving, 1.0 - 2.0 * spread, spread - 0.5 * moving


def inner_sweep(lay, place, forcing, velocity, diffusion, start, high_m, low_m, a, head, tail):
    steps, own = lay.steps, lay.own
    weights = make_weights(velocity[...].astype(F32), diffusion[...].astype(F32))
    current = jnp.where(place[0] == 0, start[...], 0.0)
    for step in range(steps):
        current = product3(stencil(current, weights) + forcing[step].astype(F32), high_m[...], low_m[...])
    a[...] = current
    for out, first, far in (
        (head, steps, slice(lay.fine, lay.wide)),
        (tail, own - steps - lay.sent, slice(own - lay.wide, own - lay.fine)),
    ):
        out[: lay.sent] = current[first : first + lay.sent].astype(BF16)
        out[lay.far_velocity : lay.far_diffusion] = velocity[far]
        out[lay.far_diffusion :] = diffusion[far]


def edge_sweep(lay, place, low, high, forcing, velocity, diffusion, start, high_m, low_m, edges):
    steps, own, fine = lay.steps, lay.own, lay.fine

    def windows(before, ours, after):
        return jnp.concatenate(
            [part.astype(F32) for part in (before, ours[:fine], ours[own - fine :], after)], axis=0
        )

    def packed(ours, at):
        return windows(low[at : at + fine], ours, high[at : at + fine])

    weights = make_weights(packed(velocity[...], lay.velocity), packed(diffusion[...], lay.diffusion))
    far_before = low[lay.start : lay.start + steps].astype(F32)
    far_after = high[lay.start + fine - steps : lay.start + fine].astype(F32)
    current = windows(
        jnp.concatenate([far_before, start_rows(lay, low, fine - steps)], axis=0),
        start[...],
        jnp.concatenate([start_rows(lay, high, 0), far_after], axis=0),
    )
    current = jnp.where(place[0] == 0, current, 0.0)
    for step in range(steps):
        rows = slice(step * steps, (step + 1) * steps)
        group = min(step, steps - 1 - step)
        at = lay.outer + group * steps
        before, after = low[at : at + steps].astype(F32), high[at : at + steps].astype(F32)
        if step > group:
            before, after = turned(before, -group), turned(after, group)
        source = windows(
            jnp.concatenate([before, low[rows].astype(F32)], axis=0),
            forcing[step],
            jnp.concatenate([high[rows].astype(F32), after], axis=0),
        )
        current = product3(stencil(current, weights) + source, high_m[...], low_m[...])
    edges[:fine] = current[steps : steps + fine]
    edges[fine:] = current[3 * steps + fine : 3 * steps + 2 * fine]


def second_sweep(
    lay, low, high, far_low, far_high, a, edges, velocity, diffusion, high_m, low_m, rho, rho_low, a_near, weights, kept
):
    steps, fine, wide, own = lay.steps, lay.fine, lay.wide, lay.own

    def extended(ours, at, far):
        rows, far_rows = slice(at, at + fine), slice(far, far + wide - fine)
        return joined(
            jnp.concatenate([far_low[far_rows].astype(F32), low[rows].astype(F32)], axis=0),
            ours,
            jnp.concatenate([high[rows].astype(F32), far_high[far_rows].astype(F32)], axis=0),
        )

    weights[0], weights[1], weights[2] = make_weights(
        extended(velocity[...], lay.velocity, lay.far_velocity),
        extended(diffusion[...], lay.diffusion, lay.far_diffusion),
    )
    near = jnp.concatenate([edges[:fine], a[steps : own - steps], edges[fine:]], axis=0)
    a_near[...] = near
    current = joined(far_low[: lay.sent], near, far_high[: lay.sent])
    clear_margins(kept)
    for _ in range(steps):
        current = product3(stored_stencil(kept, current, weights[...]), high_m[...], low_m[...])
    high_part, low_part = split(current)
    rho[...] = high_part[lay.centred(wide, lay.keep)]
    rho_low[...] = low_part[lay.centred(wide, 0)]


def coarse_and_third(lay, place, rho, rho_low, a_near, weights, high_m, low_m, coarse, change, passed, b_own, field):
    keep, steps, own = lay.keep, lay.steps, lay.own
    rows = own + 2 * keep
    count = change.shape[0]
    at = place[0]
    narrow = weights[:, lay.centred(lay.wide, keep)]
    near = lay.centred(keep, steps)
    shared = count > 1

    def turn(source, carried):
        return product(carried.astype(BF16), coarse[...]) + rho[source].astype(F32)

    if shared:
        odd = at % 2 == 1
        error = rho[0].astype(F32)
        errors = []
        for item in range(count):
            following = turn(2 * item + 1, error)
            errors.append(jnp.where(odd, following, error))
            if item < count - 1:
                error = turn(2 * item + 2, following)
    else:
        first = jnp.where(at >= 2, rho[0].astype(F32), 0.0)
        errors = [lax.fori_loop(1, at - 1, turn, first)]
    kept = jnp.concatenate([error.astype(BF16) for error in errors], axis=0)
    current = jnp.concatenate(errors, axis=0)
    narrow = jnp.concatenate([narrow] * count, axis=1)
    clear_margins(field)
    for _ in range(steps):
        current = product3(stored_stencil(field, current, narrow), high_m[...], low_m[...])
    coarse_part = product(kept, coarse[...])
    mine = jnp.zeros((own + 2 * steps, current.shape[1]), F32)
    inner = lay.centred(keep, lay.fine)
    for i in range(count):
        swept = current[i * rows : (i + 1) * rows]
        here = (at - 2) // 2 == i if shared else True
        mine = mine + jnp.where(jnp.logical_and(here, at >= 2), swept[near], 0.0)
        change[i] = swept[inner] - coarse_part[i * rows : (i + 1) * rows][inner]
    before = rho[jnp.maximum(at - 1, 0)].astype(F32)[near]
    b = a_near[...] + jnp.where(at == 0, 0.0, before) + mine
    b_own[...] = b[lay.centred(steps, 0)]
    rows = own + 2 * steps
    passed[:rows], passed[rows : 2 * rows] = split(b)
    passed[2 * rows :] = rho_low[...]


def fourth_sweep(lay, change, weights, high_m, psi, field):
    steps = lay.steps
    count, rows, _ = change.shape
    narrow = weights[:, lay.centred(lay.wide, lay.fine)]
    narrow = jnp.concatenate([narrow] * count, axis=1)
    current = jnp.concatenate([change[i] for i in range(count)], axis=0)
    clear_margins(field)
    for _ in range(steps):
        current = product(stored_stencil(field, current, narrow).astype(BF16), high_m[...])
    for i in range(count):
        psi[i] = current[i * rows : (i + 1) * rows][lay.centred(lay.fine, steps)].astype(BF16)


def last_sweep(lay, place, psi, psi_other, passed, b_own, low, high, forcing, weights, start, high_m, low_m, coarse, out, out_kept, semaphores):
    steps, own = lay.steps, lay.own
    at = place[0]
    rows = own + 2 * steps
    narrow = weights[:, lay.centred(lay.wide, steps)]
    shared = psi_other is not None

    def source(block):
        if not shared:
            return psi[block].astype(F32)
        item = block // 2 - 1
        return jnp.where((block - at) % 2 == 0, psi[item].astype(F32), psi_other[item].astype(F32))

    def turn(block, carried):
        return product(carried.astype(BF16), coarse[...]) + source(block)

    error = lax.fori_loop(2, at - 1, turn, jnp.zeros((rows, start.shape[1]), F32))
    b_before = passed[:rows].astype(F32) + passed[rows : 2 * rows].astype(F32)
    initial = joined(start_rows(lay, low, lay.fine - steps), start[...], start_rows(lay, high, 0))
    current = jnp.where(at == 0, initial, b_before + error)
    mid = lay.centred(steps, 0)
    last = product(error[mid].astype(BF16), coarse[...])
    last = last + jnp.where(at >= 3, source(jnp.maximum(at - 1, 2))[mid], 0.0)
    last = last + passed[2 * rows :].astype(F32)
    copies = [pltpu.make_async_copy(out_kept.at[step], out.at[step], semaphores.at[step]) for step in range(steps)]
    out_kept[steps - 1] = b_own[...] + jnp.where(at == 0, 0.0, last)
    copies[steps - 1].start()
    for step in range(steps - 1):
        summed = stencil(current, narrow) + near_forcing(lay, low, forcing[step], high, step)
        current = product3(summed, high_m[...], low_m[...])
        out_kept[step] = current[mid]
        copies[step].start()
    for copy in copies:
        copy.wait()


def last_sweep_gathered(lay, place, psi, *rest):
    last_sweep(lay, place, psi, None, *rest)


def in_vmem(value):
    return pltpu.with_memory_space_constraint(value, pltpu.VMEM)


def call(kernel, lay, outs, *operands, field=0):
    spaces = [pltpu.SMEM if o.dtype == jnp.int32 else pltpu.VMEM for o in operands]
    return pl.pallas_call(
        kernel if lay is None else functools.partial(kernel, lay),
        out_shape=outs,
        in_specs=[pl.BlockSpec(memory_space=space) for space in spaces],
        out_specs=jax.tree.map(lambda _: pl.BlockSpec(memory_space=pltpu.VMEM), outs),
        scratch_shapes=[pltpu.VMEM((field + 2 * MARGIN, operands[-1].shape[1]), F32)] if field else [],
        compiler_params=pltpu.CompilerParams(vmem_limit_bytes=LIMIT),
    )(*operands)


def call_from_hbm(kernel, outs, scratch, *operands):
    return pl.pallas_call(
        kernel,
        out_shape=outs,
        in_specs=[pl.BlockSpec(memory_space=pltpu.HBM)] * len(operands),
        out_specs=[pl.BlockSpec(memory_space=pltpu.VMEM)] * len(outs),
        scratch_shapes=scratch,
        compiler_params=pltpu.CompilerParams(vmem_limit_bytes=LIMIT),
    )(*(pltpu.with_memory_space_constraint(value, pltpu.HBM) for value in operands))


def per_device(initial_state, velocity, diffusion, forcing, implicit, coarse_implicit):
    own, columns = initial_state.shape
    steps = forcing.shape[0]
    blocks = lax.axis_size("tm")
    slabs = lax.axis_size("space")
    place = lax.axis_index("tm").astype(jnp.int32).reshape(1)
    lay = Layout(steps, own)
    near = own + 2 * steps

    def kept(*shape, dtype=F32):
        return pltpu.VMEM(shape, dtype)

    first_pack = kept(lay.first_rows, columns, dtype=BF16)
    head, tail = call_from_hbm(
        functools.partial(pack, lay),
        [first_pack] * 2,
        [
            pltpu.VMEM((own, columns), F32),
            pltpu.VMEM((2, steps, steps, columns), BF16),
            pltpu.SemaphoreType.DMA((1 + 2 * (steps + 3),)),
        ],
        velocity, diffusion, forcing, initial_state,
    )
    low = lax.ppermute(tail, "space", ring(slabs, 1))
    high = lax.ppermute(head, "space", ring(slabs, -1))
    low, high = in_vmem(low), in_vmem(high)
    high_m, low_m, coarse = call_from_hbm(
        split_matrices,
        [kept(*implicit.shape, dtype=BF16)] * 3,
        [pltpu.VMEM(implicit.shape, F32), pltpu.VMEM(implicit.shape, F32), pltpu.SemaphoreType.DMA((2,))],
        implicit, coarse_implicit,
    )
    high_m, low_m, coarse = in_vmem(high_m), in_vmem(low_m), in_vmem(coarse)
    second_pack = kept(lay.second_rows, columns, dtype=BF16)
    a, head, tail = call(
        inner_sweep,
        lay,
        [kept(own, columns), second_pack, second_pack],
        place, forcing, velocity, diffusion, initial_state, high_m, low_m,
    )
    far_low = in_vmem(lax.ppermute(tail, "space", ring(slabs, 1)))
    far_high = in_vmem(lax.ppermute(head, "space", ring(slabs, -1)))
    edges = call(
        edge_sweep,
        lay,
        kept(2 * lay.fine, columns),
        place, low, high, forcing, velocity, diffusion, initial_state, high_m, low_m,
    )
    rho, rho_low, a_near, weights = call(
        second_sweep,
        lay,
        [
            kept(own + 2 * lay.keep, columns, dtype=BF16),
            kept(own, columns, dtype=BF16),
            kept(near, columns),
            kept(3, own + 2 * lay.wide, columns),
        ],
        low, high, far_low, far_high, in_vmem(a), in_vmem(edges), velocity, diffusion, high_m, low_m,
        field=own + 2 * lay.wide,
    )
    weights = in_vmem(weights)
    rho_all = lax.all_gather(rho, "tm", axis=0)
    shared = blocks % 2 == 0 and 4 <= blocks <= 8
    count = (blocks - 2) // 2 if shared else 1
    change, passed, b_own = call(
        coarse_and_third,
        lay,
        [
            kept(count, own + 2 * lay.fine, columns),
            kept(2 * near + own, columns, dtype=BF16),
            kept(own, columns),
        ],
        place, rho_all, in_vmem(rho_low), in_vmem(a_near), weights, high_m, low_m, coarse,
        field=count * (own + 2 * lay.keep),
    )
    passed = lax.ppermute(passed, "tm", ring(blocks, 1))
    psi = call(
        fourth_sweep,
        lay,
        kept(count, near, columns, dtype=BF16),
        in_vmem(change), weights, high_m,
        field=count * (own + 2 * lay.fine),
    )
    if shared:
        psi_other = lax.ppermute(psi, "tm", [(i, i ^ 1) for i in range(blocks)])
        sources, kernel = (in_vmem(psi), in_vmem(psi_other)), last_sweep
    else:
        sources, kernel = (lax.all_gather(psi[0], "tm", axis=0),), last_sweep_gathered
    operands = (
        place, *sources, in_vmem(passed), in_vmem(b_own), low, high, forcing, weights, initial_state,
        high_m, low_m, coarse,
    )
    return pl.pallas_call(
        functools.partial(kernel, lay),
        out_shape=jax.ShapeDtypeStruct((steps, own, columns), F32),
        in_specs=[pl.BlockSpec(memory_space=pltpu.SMEM)]
        + [pl.BlockSpec(memory_space=pltpu.VMEM)] * (len(operands) - 1),
        out_specs=pl.BlockSpec(memory_space=pltpu.HBM),
        scratch_shapes=[pltpu.VMEM((steps, own, columns), F32), pltpu.SemaphoreType.DMA((steps,))],
        compiler_params=pltpu.CompilerParams(vmem_limit_bytes=LIMIT),
        name="last_sweep",
    )(*operands)


def solution(mesh):
    in_specs = (
        P("space", None),
        P("space", None),
        P("space", None),
        P("tm", "space", None),
        P(),
        P(),
    )
    out_specs = P("tm", "space", None)
    return jax.shard_map(per_device, mesh=mesh, in_specs=in_specs, out_specs=out_specs, check_vma=False)
```

```python
import functools

import jax
import jax.numpy as jnp
from jax import lax
from jax.experimental import pallas as pl
from jax.experimental.pallas import tpu as pltpu
from jax.sharding import PartitionSpec as P


F32 = jnp.float32
BF16 = jnp.bfloat16
LIMIT = 16 << 20
MARGIN = 8


def ring(count, distance):
    return [(i, (i + distance) % count) for i in range(count)]


def split(value):
    high = value.astype(BF16)
    return high, (value - high.astype(F32)).astype(BF16)


def product(left, right):
    return jnp.dot(left, right, preferred_element_type=F32)


def product3(value, high_matrix, low_matrix):
    rows = value.shape[0]
    high, low = split(value)
    both = product(jnp.concatenate([high, low], axis=0), high_matrix)
    return both[:rows] + (both[rows:] + product(high, low_matrix))


def stencil(value, weights):
    west, centre, east = weights
    return centre * value + east * jnp.roll(value, -1, 0) + west * jnp.roll(value, 1, 0)


def stored_stencil(kept, value, weights):
    west, centre, east = weights
    rows = value.shape[0]
    kept[MARGIN : MARGIN + rows] = value
    return centre * value + east * kept[MARGIN + 1 : MARGIN + 1 + rows] + west * kept[MARGIN - 1 : MARGIN - 1 + rows]


def clear_margins(kept):
    rows = kept.shape[0]
    kept[:MARGIN] = jnp.zeros((MARGIN, kept.shape[1]), F32)
    kept[rows - MARGIN :] = jnp.zeros((MARGIN, kept.shape[1]), F32)


def turned(value, shift):
    return value if shift % value.shape[0] == 0 else jnp.roll(value, shift, 0)


class Layout:
    def __init__(self, steps, own):
        self.steps = steps
        self.own = own
        self.fine = 2 * steps
        self.keep = 3 * steps
        self.wide = 4 * steps
        self.groups = steps // 2
        self.outer = steps * steps
        self.velocity = self.outer + self.groups * steps
        self.diffusion = self.velocity + self.fine
        self.start = self.diffusion + self.fine
        self.start_low = self.start + self.fine
        self.first_rows = self.start_low + steps
        self.sent = self.wide - steps
        self.far_velocity = self.sent
        self.far_diffusion = self.far_velocity + self.wide - self.fine
        self.second_rows = self.far_diffusion + self.wide - self.fine

    def centred(self, width, inside):
        return slice(width - inside, width + self.own + inside)


def pack(lay, velocity, diffusion, forcing, start, head, tail, start_kept, outer_kept, semaphores):
    steps, own, fine = lay.steps, lay.own, lay.fine
    sides = ((head, 0, 0, steps), (tail, own - fine, own - steps, own - fine))
    copies = [(start, start_kept)]
    for side, (out, first, inner, outer) in enumerate(sides):
        near = pl.ds(first, fine)
        copies.append((forcing.at[:, pl.ds(outer, steps)], outer_kept.at[side]))
        for step in range(steps):
            copies.append((forcing.at[step, pl.ds(inner, steps)], out.at[pl.ds(step * steps, steps)]))
        copies.append((velocity.at[near], out.at[pl.ds(lay.velocity, fine)]))
        copies.append((diffusion.at[near], out.at[pl.ds(lay.diffusion, fine)]))
    copies = [pltpu.make_async_copy(*pair, semaphores.at[i]) for i, pair in enumerate(copies)]
    for copy in copies:
        copy.start()
    for copy in copies:
        copy.wait()
    for side, (out, first, _, _) in enumerate(sides):
        high, low = split(start_kept[first : first + fine])
        out[lay.start : lay.start_low] = high
        out[lay.start_low : lay.first_rows] = low[:steps] if side == 0 else low[fine - steps :]
        for group in range(lay.groups):
            one = outer_kept[side, group].astype(F32)
            other = outer_kept[side, steps - 1 - group].astype(F32)
            row = lax.broadcasted_iota(jnp.int32, one.shape, 0)
            if side == 0:
                both = jnp.where(row < steps - 1 - group, one, turned(other, -group))
            else:
                both = jnp.where(row > group, one, turned(other, group))
            at = lay.outer + group * steps
            out[at : at + steps] = both.astype(BF16)


def split_matrix(implicit, high_m, low_m, kept, semaphore):
    copy = pltpu.make_async_copy(implicit, kept, semaphore.at[0])
    copy.start()
    copy.wait()
    high_m[...], low_m[...] = split(kept[...])


def round_matrix(coarse_implicit, coarse, kept, semaphore):
    copy = pltpu.make_async_copy(coarse_implicit, kept, semaphore.at[0])
    copy.start()
    copy.wait()
    coarse[...] = kept[...].astype(BF16)


def joined(low, own, high):
    return jnp.concatenate([low.astype(F32), own.astype(F32), high.astype(F32)], axis=0)


def near_forcing(lay, low, own, high, step):
    rows = slice(step * lay.steps, (step + 1) * lay.steps)
    return joined(low[rows], own, high[rows])


def start_rows(lay, packed, first):
    at = lay.start + first
    return packed[at : at + lay.steps].astype(F32) + packed[lay.start_low : lay.first_rows].astype(F32)


def make_weights(moving, spread):
    return spread + 0.5 * moving, 1.0 - 2.0 * spread, spread - 0.5 * moving


def inner_sweep(lay, place, forcing, velocity, diffusion, start, high_m, low_m, a, head, tail):
    steps, own = lay.steps, lay.own
    weights = make_weights(velocity[...].astype(F32), diffusion[...].astype(F32))
    current = jnp.where(place[0] == 0, start[...], 0.0)
    for step in range(steps):
        current = product3(stencil(current, weights) + forcing[step].astype(F32), high_m[...], low_m[...])
    a[...] = current
    for out, first, far in (
        (head, steps, slice(lay.fine, lay.wide)),
        (tail, own - steps - lay.sent, slice(own - lay.wide, own - lay.fine)),
    ):
        out[: lay.sent] = current[first : first + lay.sent].astype(BF16)
        out[lay.far_velocity : lay.far_diffusion] = velocity[far]
        out[lay.far_diffusion :] = diffusion[far]


def edge_sweep(lay, place, low, high, forcing, velocity, diffusion, start, high_m, low_m, edges):
    steps, own, fine = lay.steps, lay.own, lay.fine

    def windows(before, ours, after):
        return jnp.concatenate(
            [part.astype(F32) for part in (before, ours[:fine], ours[own - fine :], after)], axis=0
        )

    def packed(ours, at):
        return windows(low[at : at + fine], ours, high[at : at + fine])

    weights = make_weights(packed(velocity[...], lay.velocity), packed(diffusion[...], lay.diffusion))
    far_before = low[lay.start : lay.start + steps].astype(F32)
    far_after = high[lay.start + fine - steps : lay.start + fine].astype(F32)
    current = windows(
        jnp.concatenate([far_before, start_rows(lay, low, fine - steps)], axis=0),
        start[...],
        jnp.concatenate([start_rows(lay, high, 0), far_after], axis=0),
    )
    current = jnp.where(place[0] == 0, current, 0.0)
    for step in range(steps):
        rows = slice(step * steps, (step + 1) * steps)
        group = min(step, steps - 1 - step)
        at = lay.outer + group * steps
        before, after = low[at : at + steps].astype(F32), high[at : at + steps].astype(F32)
        if step > group:
            before, after = turned(before, -group), turned(after, group)
        source = windows(
            jnp.concatenate([before, low[rows].astype(F32)], axis=0),
            forcing[step],
            jnp.concatenate([high[rows].astype(F32), after], axis=0),
        )
        current = product3(stencil(current, weights) + source, high_m[...], low_m[...])
    edges[:fine] = current[steps : steps + fine]
    edges[fine:] = current[3 * steps + fine : 3 * steps + 2 * fine]


def second_sweep(
    lay, low, high, far_low, far_high, a, edges, velocity, diffusion, high_m, low_m, rho, rho_low, a_near, weights, kept
):
    steps, fine, wide, own = lay.steps, lay.fine, lay.wide, lay.own

    def extended(ours, at, far):
        rows, far_rows = slice(at, at + fine), slice(far, far + wide - fine)
        return joined(
            jnp.concatenate([far_low[far_rows].astype(F32), low[rows].astype(F32)], axis=0),
            ours,
            jnp.concatenate([high[rows].astype(F32), far_high[far_rows].astype(F32)], axis=0),
        )

    weights[0], weights[1], weights[2] = make_weights(
        extended(velocity[...], lay.velocity, lay.far_velocity),
        extended(diffusion[...], lay.diffusion, lay.far_diffusion),
    )
    near = jnp.concatenate([edges[:fine], a[steps : own - steps], edges[fine:]], axis=0)
    a_near[...] = near
    current = joined(far_low[: lay.sent], near, far_high[: lay.sent])
    clear_margins(kept)
    for _ in range(steps):
        current = product3(stored_stencil(kept, current, weights[...]), high_m[...], low_m[...])
    high_part, low_part = split(current)
    rho[...] = high_part[lay.centred(wide, lay.keep)]
    rho_low[...] = low_part[lay.centred(wide, 0)]


def coarse_and_third(lay, place, rho, rho_low, a_near, weights, high_m, low_m, coarse, change, passed, b_own, field):
    keep, steps, own = lay.keep, lay.steps, lay.own
    rows = own + 2 * keep
    count = change.shape[0]
    at = place[0]
    narrow = weights[:, lay.centred(lay.wide, keep)]
    near = lay.centred(keep, steps)
    shared = count > 1

    def turn(source, carried):
        return product(carried.astype(BF16), coarse[...]) + rho[source].astype(F32)

    if shared:
        odd = at % 2 == 1
        error = rho[0].astype(F32)
        errors = []
        for item in range(count):
            following = turn(2 * item + 1, error)
            errors.append(jnp.where(odd, following, error))
            if item < count - 1:
                error = turn(2 * item + 2, following)
    else:
        first = jnp.where(at >= 2, rho[0].astype(F32), 0.0)
        errors = [lax.fori_loop(1, at - 1, turn, first)]
    kept = jnp.concatenate([error.astype(BF16) for error in errors], axis=0)
    current = jnp.concatenate(errors, axis=0)
    narrow = jnp.concatenate([narrow] * count, axis=1)
    clear_margins(field)
    for _ in range(steps):
        current = product3(stored_stencil(field, current, narrow), high_m[...], low_m[...])
    coarse_part = product(kept, coarse[...])
    mine = jnp.zeros((own + 2 * steps, current.shape[1]), F32)
    inner = lay.centred(keep, lay.fine)
    for i in range(count):
        swept = current[i * rows : (i + 1) * rows]
        here = (at - 2) // 2 == i if shared else True
        mine = mine + jnp.where(jnp.logical_and(here, at >= 2), swept[near], 0.0)
        change[i] = swept[inner] - coarse_part[i * rows : (i + 1) * rows][inner]
    before = rho[jnp.maximum(at - 1, 0)].astype(F32)[near]
    b = a_near[...] + jnp.where(at == 0, 0.0, before) + mine
    b_own[...] = b[lay.centred(steps, 0)]
    rows = own + 2 * steps
    passed[:rows], passed[rows : 2 * rows] = split(b)
    passed[2 * rows :] = rho_low[...]


def fourth_sweep(lay, change, weights, high_m, psi, field):
    steps = lay.steps
    count, rows, _ = change.shape
    narrow = weights[:, lay.centred(lay.wide, lay.fine)]
    narrow = jnp.concatenate([narrow] * count, axis=1)
    current = jnp.concatenate([change[i] for i in range(count)], axis=0)
    clear_margins(field)
    for _ in range(steps):
        current = product(stored_stencil(field, current, narrow).astype(BF16), high_m[...])
    for i in range(count):
        psi[i] = current[i * rows : (i + 1) * rows][lay.centred(lay.fine, steps)].astype(BF16)


def last_sweep(lay, place, psi, psi_other, passed, b_own, low, high, forcing, weights, start, high_m, low_m, coarse, out, out_kept, semaphores):
    steps, own = lay.steps, lay.own
    at = place[0]
    rows = own + 2 * steps
    narrow = weights[:, lay.centred(lay.wide, steps)]
    shared = psi_other is not None

    def source(block):
        if not shared:
            return psi[block].astype(F32)
        item = block // 2 - 1
        return jnp.where((block - at) % 2 == 0, psi[item].astype(F32), psi_other[item].astype(F32))

    def turn(block, carried):
        return product(carried.astype(BF16), coarse[...]) + source(block)

    error = lax.fori_loop(2, at - 1, turn, jnp.zeros((rows, start.shape[1]), F32))
    b_before = passed[:rows].astype(F32) + passed[rows : 2 * rows].astype(F32)
    initial = joined(start_rows(lay, low, lay.fine - steps), start[...], start_rows(lay, high, 0))
    current = jnp.where(at == 0, initial, b_before + error)
    mid = lay.centred(steps, 0)
    last = product(error[mid].astype(BF16), coarse[...])
    last = last + jnp.where(at >= 3, source(jnp.maximum(at - 1, 2))[mid], 0.0)
    last = last + passed[2 * rows :].astype(F32)
    copies = [pltpu.make_async_copy(out_kept.at[step], out.at[step], semaphores.at[step]) for step in range(steps)]
    out_kept[steps - 1] = b_own[...] + jnp.where(at == 0, 0.0, last)
    copies[steps - 1].start()
    for step in range(steps - 1):
        summed = stencil(current, narrow) + near_forcing(lay, low, forcing[step], high, step)
        current = product3(summed, high_m[...], low_m[...])
        out_kept[step] = current[mid]
        copies[step].start()
    for copy in copies:
        copy.wait()


def last_sweep_gathered(lay, place, psi, *rest):
    last_sweep(lay, place, psi, None, *rest)


def in_vmem(value):
    return pltpu.with_memory_space_constraint(value, pltpu.VMEM)


def call(kernel, lay, outs, *operands, field=0):
    spaces = [pltpu.SMEM if o.dtype == jnp.int32 else pltpu.VMEM for o in operands]
    return pl.pallas_call(
        kernel if lay is None else functools.partial(kernel, lay),
        out_shape=outs,
        in_specs=[pl.BlockSpec(memory_space=space) for space in spaces],
        out_specs=jax.tree.map(lambda _: pl.BlockSpec(memory_space=pltpu.VMEM), outs),
        scratch_shapes=[pltpu.VMEM((field + 2 * MARGIN, operands[-1].shape[1]), F32)] if field else [],
        compiler_params=pltpu.CompilerParams(vmem_limit_bytes=LIMIT),
    )(*operands)


def call_from_hbm(kernel, outs, scratch, *operands):
    return pl.pallas_call(
        kernel,
        out_shape=outs,
        in_specs=[pl.BlockSpec(memory_space=pltpu.HBM)] * len(operands),
        out_specs=[pl.BlockSpec(memory_space=pltpu.VMEM)] * len(outs),
        scratch_shapes=scratch,
        compiler_params=pltpu.CompilerParams(vmem_limit_bytes=LIMIT),
    )(*(pltpu.with_memory_space_constraint(value, pltpu.HBM) for value in operands))


def per_device(initial_state, velocity, diffusion, forcing, implicit, coarse_implicit):
    own, columns = initial_state.shape
    steps = forcing.shape[0]
    blocks = lax.axis_size("tm")
    slabs = lax.axis_size("space")
    place = lax.axis_index("tm").astype(jnp.int32).reshape(1)
    lay = Layout(steps, own)
    near = own + 2 * steps

    def kept(*shape, dtype=F32):
        return pltpu.VMEM(shape, dtype)

    first_pack = kept(lay.first_rows, columns, dtype=BF16)
    head, tail = call_from_hbm(
        functools.partial(pack, lay),
        [first_pack] * 2,
        [
            pltpu.VMEM((own, columns), F32),
            pltpu.VMEM((2, steps, steps, columns), BF16),
            pltpu.SemaphoreType.DMA((1 + 2 * (steps + 3),)),
        ],
        velocity, diffusion, forcing, initial_state,
    )
    low = in_vmem(lax.ppermute(tail, "space", ring(slabs, 1)))
    high = in_vmem(lax.ppermute(head, "space", ring(slabs, -1)))
    matrix, scratch = kept(*implicit.shape, dtype=BF16), [pltpu.VMEM(implicit.shape, F32), pltpu.SemaphoreType.DMA((1,))]
    high_m, low_m = call_from_hbm(split_matrix, [matrix] * 2, scratch, implicit)
    (coarse,) = call_from_hbm(round_matrix, [matrix], scratch, coarse_implicit)
    high_m, low_m, coarse = in_vmem(high_m), in_vmem(low_m), in_vmem(coarse)
    second_pack = kept(lay.second_rows, columns, dtype=BF16)
    a, head, tail = call(
        inner_sweep,
        lay,
        [kept(own, columns), second_pack, second_pack],
        place, forcing, velocity, diffusion, initial_state, high_m, low_m,
    )
    far_low = in_vmem(lax.ppermute(tail, "space", ring(slabs, 1)))
    far_high = lax.ppermute(head, "space", ring(slabs, -1))
    far_high = in_vmem(far_high)
    edges = call(
        edge_sweep,
        lay,
        kept(2 * lay.fine, columns),
        place, low, high, forcing, velocity, diffusion, initial_state, high_m, low_m,
    )
    rho, rho_low, a_near, weights = call(
        second_sweep,
        lay,
        [
            kept(own + 2 * lay.keep, columns, dtype=BF16),
            kept(own, columns, dtype=BF16),
            kept(near, columns),
            kept(3, own + 2 * lay.wide, columns),
        ],
        low, high, far_low, far_high, in_vmem(a), in_vmem(edges), velocity, diffusion, high_m, low_m,
        field=own + 2 * lay.wide,
    )
    weights = in_vmem(weights)
    rho_all = lax.all_gather(rho, "tm", axis=0)
    shared = blocks % 2 == 0 and 4 <= blocks <= 8
    count = (blocks - 2) // 2 if shared else 1
    change, passed, b_own = call(
        coarse_and_third,
        lay,
        [
            kept(count, own + 2 * lay.fine, columns),
            kept(2 * near + own, columns, dtype=BF16),
            kept(own, columns),
        ],
        place, rho_all, in_vmem(rho_low), in_vmem(a_near), weights, high_m, low_m, coarse,
        field=count * (own + 2 * lay.keep),
    )
    passed = lax.ppermute(passed, "tm", ring(blocks, 1))
    psi = call(
        fourth_sweep,
        lay,
        kept(count, near, columns, dtype=BF16),
        in_vmem(change), weights, high_m,
        field=count * (own + 2 * lay.fine),
    )
    if shared:
        psi_other = lax.ppermute(psi, "tm", [(i, i ^ 1) for i in range(blocks)])
        sources, kernel = (in_vmem(psi), in_vmem(psi_other)), last_sweep
    else:
        sources, kernel = (lax.all_gather(psi[0], "tm", axis=0),), last_sweep_gathered
    operands = (
        place, *sources, in_vmem(passed), in_vmem(b_own), low, high, forcing, weights, initial_state,
        high_m, low_m, coarse,
    )
    return pl.pallas_call(
        functools.partial(kernel, lay),
        out_shape=jax.ShapeDtypeStruct((steps, own, columns), F32),
        in_specs=[pl.BlockSpec(memory_space=pltpu.SMEM)]
        + [pl.BlockSpec(memory_space=pltpu.VMEM)] * (len(operands) - 1),
        out_specs=pl.BlockSpec(memory_space=pltpu.HBM),
        scratch_shapes=[pltpu.VMEM((steps, own, columns), F32), pltpu.SemaphoreType.DMA((steps,))],
        compiler_params=pltpu.CompilerParams(vmem_limit_bytes=LIMIT),
        name="last_sweep",
    )(*operands)


def solution(mesh):
    in_specs = (
        P("space", None),
        P("space", None),
        P("space", None),
        P("tm", "space", None),
        P(),
        P(),
    )
    out_specs = P("tm", "space", None)
    return jax.shard_map(per_device, mesh=mesh, in_specs=in_specs, out_specs=out_specs, check_vma=False)
```
